32 devices in a mesh: row: 8 (over y, x, core), col: 4 (over z).
Axes of the slice: x: 2, y: 2, z: 4, core: 2. Of those that a mesh axis runs over, the one named last changes fastest.
Arguments:
- site_tensors: float32 [8, 4, 144, 144], P('row', 'col'), may hold values from -4 to 4
- start_basis: float32 [3, 12, 144], replicated, may hold values from -4 to 4
Outputs:
- coarse: float32 [8, 4, 144, 144], P('row', 'col')
- log_scale: float32 [8, 4], P('row', 'col')
The draws below stay inside these ranges and needn't reach their ends.
All inputs are finite; a program needn't handle non-finite values.
Results may differ from the reference program's by a relative error of at most 0.03.
Values may be sent and summed in bfloat16 or wider, within the bound.
No kernel may reach another device: no remote copies, remote signals or barrier semaphores. Data moves between devices by JAX's collectives and lax.ppermute only.
A program may use at most 64 MiB of HBM per device.

```python
import jax
import jax.numpy as jnp
from jax import lax

CHI = 12
LEVELS = 3
SWEEPS = 2
NR = 8
NC = 4


def draw_site_tensors(key, part):
    square = CHI * CHI
    low_end = 0.5
    leg_scales = []
    for leg_num in range(4):
        leg_key = jax.random.fold_in(key, 11 + leg_num)
        leg_draw = jax.random.uniform(leg_key, (NR, NC, CHI), jnp.float32, jnp.log(low_end), 0.0)
        leg_scales.append(jnp.exp(leg_draw))
    row_scale = (leg_scales[0][..., :, None] * leg_scales[1][..., None, :]).reshape(NR, NC, square)
    col_scale = (leg_scales[2][..., :, None] * leg_scales[3][..., None, :]).reshape(NR, NC, square)
    noise_key = jax.random.fold_in(key, 3)
    base_draw = jnp.clip(jax.random.normal(noise_key, (NR, NC, square, square), jnp.float32), -4.0, 4.0)
    return (base_draw * row_scale[..., :, None] * col_scale[..., None, :]).astype(jnp.float32)


def scatter_about(key, dims, spread, bound, held_as=jnp.bfloat16):
    values = jax.random.normal(key, dims, jnp.float32) * spread
    return jnp.minimum(jnp.maximum(values, -bound), bound).astype(held_as)


def setup_inputs(seed: int = 0) -> dict:
    keys = jax.random.split(jax.random.key(seed), 3)
    site_tensors = draw_site_tensors(jax.random.fold_in(keys[2], 71), 0)
    start_basis = scatter_about(keys[1], (LEVELS, CHI, CHI * CHI), 1.0, 4.0, jnp.float32)
    return {"site_tensors": site_tensors, "start_basis": start_basis}


def contract_gram(side_a, side_b):
    square = CHI * CHI
    prod_a = jnp.dot(side_a.astype(jnp.float32), side_a.T.astype(jnp.float32), preferred_element_type=jnp.float32).astype(jnp.bfloat16)
    prod_b = jnp.dot(side_b.astype(jnp.float32), side_b.T.astype(jnp.float32), preferred_element_type=jnp.float32).astype(jnp.bfloat16)
    prod_a = prod_a.reshape(CHI, CHI, CHI, CHI).transpose(1, 3, 0, 2).reshape(square, square)
    prod_b = prod_b.reshape(CHI, CHI, CHI, CHI).transpose(0, 2, 1, 3).reshape(square, square)
    outer_prod = jnp.dot(prod_a.astype(jnp.float32), prod_b.astype(jnp.float32), preferred_element_type=jnp.float32)
    return outer_prod.reshape(CHI, CHI, CHI, CHI).transpose(0, 2, 1, 3).reshape(square, square).astype(jnp.bfloat16)

def pair_grams(upper_low, lower_low):
    square = CHI * CHI
    upper_legs = upper_low.reshape(CHI, CHI, CHI, CHI)
    lower_legs = lower_low.reshape(CHI, CHI, CHI, CHI)
    left_a = upper_legs.transpose(1, 2, 0, 3).reshape(square, square)
    left_b = lower_legs.transpose(0, 2, 1, 3).reshape(square, square)
    right_a = upper_legs.transpose(1, 3, 0, 2).reshape(square, square)
    right_b = lower_legs.transpose(0, 3, 1, 2).reshape(square, square)
    return (contract_gram(left_a, left_b), contract_gram(right_a, right_b))

def isometry(bond_gram, start_rows):
    shift = jnp.trace(bond_gram) / (CHI * CHI)
    basis_now = start_rows.T
    for sweep_num in range(SWEEPS):
        image_now = jnp.dot(bond_gram, basis_now, precision=lax.Precision.HIGHEST) + shift * basis_now
        inner_prod = jnp.dot(image_now.T, image_now, precision=lax.Precision.HIGHEST)
        factor = jnp.linalg.cholesky(inner_prod)
        basis_now = jax.scipy.linalg.solve_triangular(factor, image_now.T, lower=True).T
    return basis_now

def pair_merge(upper_low, lower_low, left_iso, right_iso):
    upper_legs = upper_low.astype(jnp.float32).reshape(CHI, CHI, CHI, CHI)
    lower_legs = lower_low.astype(jnp.float32).reshape(CHI, CHI, CHI, CHI)
    left_legs = left_iso.astype(jnp.float32).reshape(CHI, CHI, CHI)
    right_legs = right_iso.astype(jnp.float32).reshape(CHI, CHI, CHI)
    first_section = jnp.einsum('umlr,lka->umrka', upper_legs, left_legs, precision=lax.Precision.HIGHEST).astype(jnp.bfloat16)
    second = jnp.einsum('umrka,mdks->urads', first_section.astype(jnp.float32), lower_legs, precision=lax.Precision.HIGHEST).astype(jnp.bfloat16)
    merged = jnp.einsum('urads,rsb->udab', second.astype(jnp.float32), right_legs, precision=lax.Precision.HIGHEST)
    return merged.reshape(CHI * CHI, CHI * CHI)

def reference(site_tensors, start_basis):
    square = CHI * CHI
    current = site_tensors
    log_total = jnp.zeros((NR, NC), jnp.float32)
    for level_num in range(LEVELS):
        upper_low = current[0::2].astype(jnp.bfloat16)
        lower_low = current[1::2].astype(jnp.bfloat16)
        pair_rows = upper_low.shape[0]
        flat_upper = upper_low.reshape(pair_rows * NC, square, square)
        flat_lower = lower_low.reshape(pair_rows * NC, square, square)
        grams_left, grams_right = lax.map(lambda both: pair_grams(both[0], both[1]), (flat_upper, flat_lower))
        grams_left = grams_left.reshape(pair_rows, NC, square, square)
        grams_right = grams_right.reshape(pair_rows, NC, square, square)
        bond_gram = jnp.roll(grams_right, 1, axis=1).astype(jnp.float32) + grams_left.astype(jnp.float32)
        start_rows = start_basis[level_num]
        bases = lax.map(lambda one_gram: isometry(one_gram, start_rows), bond_gram.reshape(pair_rows * NC, square, square))
        iso_low = bases.astype(jnp.bfloat16).reshape(pair_rows, NC, square, CHI)
        left_iso = iso_low.reshape(pair_rows * NC, square, CHI)
        right_iso = jnp.roll(iso_low, -1, axis=1).reshape(pair_rows * NC, square, CHI)
        merged = lax.map(lambda items: pair_merge(items[0], items[1], items[2], items[3]), (flat_upper, flat_lower, left_iso, right_iso))
        norm_value = jnp.sqrt(lax.optimization_barrier(jnp.mean(merged * merged, axis=(1, 2))) + 1e-06)
        current = (merged / norm_value[:, None, None]).reshape(pair_rows, NC, square, square)
        log_total = log_total + jnp.repeat(jnp.log(norm_value).reshape(pair_rows, NC), 2 ** (level_num + 1), axis=0)
    coarse = jnp.repeat(current, 2 ** LEVELS, axis=0)
    return (coarse, log_total)
```

```python
import functools

import jax
import jax.numpy as jnp
from jax import lax
from jax.experimental import pallas as pl
from jax.experimental.pallas import tpu as pltpu
from jax.sharding import PartitionSpec as P

CHI = 12
LEVELS = 3
SWEEPS = 2
PAD = 16
SHIFT = 4
ROWS = CHI * PAD
LANES = PAD * PAD
F32 = jnp.float32
BF16 = jnp.bfloat16

NN = (((1,), (0,)), ((), ()))
NT = (((1,), (1,)), ((), ()))
TN = (((0,), (0,)), ((), ()))


def mm(a, b, dims=NN):
    return lax.dot_general(a, b, dims, preferred_element_type=F32)


def iota(shape, dim):
    return lax.broadcasted_iota(jnp.int32, shape, dim)


def group(index):
    return lax.shift_right_logical(index, SHIFT)


def minor(index):
    return lax.bitwise_and(index, PAD - 1)


def one_hot(mask):
    return jnp.where(mask, 1.0, 0.0).astype(BF16)


def swap_matrix(rows=LANES):
    i, j = iota((rows, LANES), 0), iota((rows, LANES), 1)
    return one_hot((group(i) == minor(j)) & (minor(i) == group(j)))


def spread_matrix(mirror):
    i, j = iota((CHI * CHI, LANES), 0), iota((CHI * CHI, LANES), 1)
    s, t = group(j), minor(j)
    source = jnp.where(mirror, t * CHI + s, s * CHI + t)
    return one_hot((i == source) & (s < CHI) & (t < CHI))


def row_spread():
    i, j = iota((ROWS, CHI * CHI), 0), iota((ROWS, CHI * CHI), 1)
    return one_hot((j == minor(i) * CHI + group(i)) & (minor(i) < CHI))


def block_swap(x):
    lane_group = group(iota((PAD, 128), 1))
    zero = jnp.zeros((PAD, 128), x.dtype)
    tiles = {}
    for p in range(PAD):
        for t in range(2):
            src, src_tile = (p & 7) | (t << 3), p >> 3
            if src < CHI:
                tiles[p, t] = x[src * PAD : (src + 1) * PAD, src_tile * 128 : (src_tile + 1) * 128]
            else:
                tiles[p, t] = None
    for bit in range(3):
        step = 1 << bit
        low = lax.bitwise_and(lane_group, step) == 0
        new = {}
        for p in range(PAD):
            if p & step:
                continue
            for t in range(2):
                a, b = tiles[p, t], tiles[p | step, t]
                if a is None and b is None:
                    new[p, t] = new[p | step, t] = None
                    continue
                a_moved = zero if a is None else pltpu.roll(a, 128 - step * PAD, 1)
                b_moved = zero if b is None else pltpu.roll(b, step * PAD, 1)
                a = zero if a is None else a
                b = zero if b is None else b
                new[p, t] = jnp.where(low, a, b_moved)
                new[p | step, t] = jnp.where(low, a_moved, b)
        tiles = new
    rows = []
    for p in range(CHI):
        pair = [zero if tiles[p, t] is None else tiles[p, t] for t in range(2)]
        rows.append(jnp.concatenate(pair, axis=1))
    return jnp.concatenate(rows, axis=0)


def widen(x):
    return jnp.concatenate([x, jnp.zeros((x.shape[0], LANES - x.shape[1]), x.dtype)], axis=1)


def parts3(x):
    a = x.astype(BF16)
    rest = x - a.astype(F32)
    b = rest.astype(BF16)
    c = (rest - b.astype(F32)).astype(BF16)
    return jnp.concatenate([a, b, c], axis=0)


def fold3(y):
    n = y.shape[0] // 3
    return (y[2 * n :] + y[n : 2 * n]) + y[:n]


def gram_body(upper, lower, swap):
    turned = block_swap(mm(upper, swap).astype(BF16))
    row_swap = swap[:ROWS, :ROWS]
    lower_m = mm(swap[:, :ROWS], lower).astype(BF16)
    prod_b = mm(lower_m[:ROWS], lower, NT).astype(BF16)
    prod_b = block_swap(widen(prod_b))
    prod_b = mm(row_swap, prod_b).astype(BF16)
    turned_m = mm(turned, swap).astype(BF16)
    prod_a = mm(turned_m, turned, TN).astype(BF16)
    prod_a = block_swap(prod_a[:ROWS])
    outer = mm(prod_a, prod_b, NT).astype(BF16)
    return block_swap(widen(outer)), turned


def start_body(start, swap):
    start = jnp.concatenate([start, jnp.zeros((PAD - CHI, CHI * CHI), F32)], axis=0)
    pieces = parts3(start)
    spread = spread_matrix(False)
    plain = mm(pieces, spread)
    turned = mm(plain.astype(BF16), swap)
    return fold3(plain), fold3(turned)


def orthonormal(y):
    gram = lax.dot_general(
        y, y, NT, preferred_element_type=F32, precision=lax.Precision.HIGHEST
    )
    width = y.shape[1]
    row = iota((PAD, 128), 0)
    cols = [jnp.broadcast_to(gram[:, k : k + 1], (PAD, 128)) for k in range(CHI)]
    scale = jnp.zeros((PAD, 128), F32)
    for k in range(CHI):
        pivot = jnp.broadcast_to(cols[k][k : k + 1, :], (PAD, 128))
        scale = jnp.where(row == k, lax.rsqrt(pivot), scale)
        factor = jnp.where(row > k, cols[k] / pivot, 0.0)
        for j in range(k + 1, CHI):
            cols[j] = cols[j] - factor * jnp.broadcast_to(cols[j][k : k + 1, :], (PAD, 128))
        wide = jnp.concatenate([factor] * (width // 128), axis=1)
        y = y - wide * jnp.broadcast_to(y[k : k + 1, :], (PAD, width))
    return y * jnp.concatenate([scale] * (width // 128), axis=1)


def iso_body(own, other, start, start_turned, swap):
    total = own.astype(F32) + other.astype(F32)
    i, j = iota((ROWS, LANES), 0), iota((ROWS, LANES), 1)
    diagonal = (group(i) == minor(j)) & (minor(i) == group(j))
    shift = jnp.sum(jnp.where(diagonal, total, 0.0)) / (CHI * CHI)
    pieces = parts3(start)
    image = fold3(mm(pieces, own, NT) + mm(pieces, other, NT))
    image = widen(image) + shift * start_turned
    basis = orthonormal(image)
    pieces = parts3(basis)
    image = fold3(mm(pieces[:, :ROWS], own) + mm(pieces[:, :ROWS], other))
    image = image + shift * fold3(mm(pieces, swap))
    return orthonormal(image).astype(BF16)


def first_second(turned, lower, left, second_ref):
    lane = iota((PAD, LANES), 1)
    masked = [jnp.where(group(lane) == k, left.astype(F32), 0.0) for k in range(CHI)]
    masked = jnp.concatenate(masked, axis=0).astype(BF16)
    i, j = iota((LANES, LANES), 0), iota((LANES, LANES), 1)
    values = mm(masked, one_hot(minor(i) == group(j)))
    eye = minor(lane) == iota((PAD, LANES), 0)
    for a in range(CHI):
        blocks = []
        for k in range(CHI):
            line = jnp.broadcast_to(values[k * PAD + a : k * PAD + a + 1, :], (PAD, LANES))
            blocks.append(jnp.where(eye, line, 0.0).astype(BF16))
        kron = jnp.concatenate(blocks, axis=0)
        first = mm(turned[:, :ROWS], kron).astype(BF16)
        second = mm(first[:, :ROWS], lower).astype(BF16)
        for k in range(CHI):
            second_ref[a * PAD : (a + 1) * PAD, k * LANES : (k + 1) * LANES] = second[
                k * PAD : (k + 1) * PAD, :
            ]


def third(second_ref, right, kron_ref):
    tile = one_hot(minor(iota((PAD, LANES), 1)) == iota((PAD, LANES), 0))
    values = mm(right, tile, TN)
    lane_group = group(iota((PAD, LANES), 1))
    for k in range(CHI):
        block = values[k * PAD : (k + 1) * PAD, :]
        for d in range(PAD):
            kept = jnp.where(lane_group == d, block, 0.0) if d < CHI else jnp.zeros_like(block)
            start = k * LANES + d * PAD
            kron_ref[start : start + PAD, :] = kept.astype(BF16)
    return mm(second_ref[...], kron_ref[...])


def pick(is_upper, own, other):
    return jnp.where(is_upper, own, other), jnp.where(is_upper, other, own)


def first_gram_kernel(role, own, other, start, lower_o, turned_o, gram_o, starts_o):
    mirror, is_upper = role[0] != 0, role[1] != 0
    swap = swap_matrix()
    rows, spread = row_spread(), spread_matrix(mirror)

    def placed(site):
        spaced = mm(rows, site[...].astype(BF16)).astype(BF16)
        return block_swap(mm(spaced, spread).astype(BF16))

    upper, lower = pick(is_upper, placed(own), placed(other))
    gram, turned = gram_body(upper, lower, swap)
    lower_o[...], turned_o[...], gram_o[...] = lower, turned, gram
    for level in range(LEVELS):
        plain, turn = start_body(start[level], swap)
        starts_o[level, :PAD], starts_o[level, PAD:] = plain, turn


def gram_kernel(role, own, other, lower_o, turned_o, gram_o):
    upper, lower = pick(role[0] != 0, own[...], other[...])
    gram, turned = gram_body(upper, lower, swap_matrix())
    lower_o[...], turned_o[...], gram_o[...] = lower, turned, gram


def iso_kernel(own, other, starts, iso_o):
    iso_o[...] = iso_body(own[...], other[...], starts[:PAD], starts[PAD:], swap_matrix())


def second_kernel(turned, lower, left, second_o):
    first_second(turned[...], lower[...], left[...], second_o)


def scaled(merged):
    mean = jnp.sum(merged * merged) / (CHI**4)
    return jnp.sqrt(jnp.full((1, LANES), mean) + 1e-06)


def third_kernel(second, right, log_in, next_o, log_o, kron):
    merged = third(second, right[...], kron)
    norm = scaled(merged)
    next_o[...] = (merged / norm).astype(BF16)
    log_o[...] = log_in[...] + jnp.log(norm)


def last_kernel(role, second, right, log_in, coarse_o, log_o, kron):
    merged = third(second, right[...], kron)
    norm = scaled(merged)
    log_o[...] = log_in[...] + jnp.log(norm)
    wide = block_swap(merged / norm)
    spread, rows = spread_matrix(role[0] != 0), row_spread()
    total = jnp.zeros((CHI * CHI, CHI * CHI), F32)
    high = wide.astype(BF16)
    low = (wide - high.astype(F32)).astype(BF16)
    for part in (high, low):
        narrow = mm(part, spread, NT).astype(BF16)
        total = total + mm(rows, narrow, TN)
    coarse_o[...] = total


def call(kernel, outs, smem, n_in, scratch=()):
    specs = [pl.BlockSpec(memory_space=pltpu.VMEM)] * n_in
    if smem:
        specs[0] = pl.BlockSpec(memory_space=pltpu.SMEM)
    return pl.pallas_call(
        kernel,
        out_shape=[jax.ShapeDtypeStruct(s, d) for s, d in outs],
        in_specs=specs,
        out_specs=[pl.BlockSpec(memory_space=pltpu.VMEM)] * len(outs),
        scratch_shapes=list(scratch),
    )


def from_partner(array, stride):
    count = lax.axis_size("row")
    return lax.ppermute(array, "row", [(i, i ^ 1 << stride) for i in range(count)])


def from_bond(array):
    rows, cols = lax.axis_size("row"), lax.axis_size("col")
    pairs = []
    for i in range(rows):
        for c in range(cols):
            target = (c - 1) % cols if i % 2 == 0 else (c + 1) % cols
            pairs.append((i * cols + c, (i ^ 1) * cols + target))
    return lax.ppermute(array, ("row", "col"), pairs)


def per_device(site_tensors, start_basis):
    square = CHI * CHI
    row = lax.axis_index("row")
    mirror = row % 2
    mat = ((ROWS, LANES), BF16)
    kron = [pltpu.VMEM((CHI * LANES, LANES), BF16)]
    log_total = jnp.zeros((1, LANES), F32)
    own = site_tensors[0, 0]
    for level in range(LEVELS):
        other = from_partner(own, level)
        is_upper = 1 - row // 2**level % 2
        if level == 0:
            role = jnp.stack([mirror, is_upper]).astype(jnp.int32)
            lower, turned, gram, starts = call(
                first_gram_kernel,
                [mat, mat, mat, ((LEVELS, 2 * PAD, LANES), F32)],
                True,
                4,
            )(role, own, other, start_basis)
        else:
            role = is_upper.reshape(1).astype(jnp.int32)
            lower, turned, gram = call(gram_kernel, [mat, mat, mat], True, 3)(role, own, other)
        gram_other = from_bond(gram)
        (left,) = call(iso_kernel, [((PAD, LANES), BF16)], False, 3)(gram, gram_other, starts[level])
        right = from_partner(left, 0)
        (second,) = call(second_kernel, [((ROWS, CHI * LANES), BF16)], False, 3)(turned, lower, left)
        if level < LEVELS - 1:
            own, log_total = call(third_kernel, [mat, ((1, LANES), F32)], False, 3, kron)(
                second, right, log_total
            )
        else:
            role = mirror.reshape(1).astype(jnp.int32)
            coarse, log_total = call(
                last_kernel, [((square, square), F32), ((1, LANES), F32)], True, 4, kron
            )(role, second, right, log_total)
    return (coarse[None, None], log_total[:, :1])


def solution(mesh):
    return jax.shard_map(
        per_device,
        mesh=mesh,
        in_specs=(P("row", "col", None, None), P()),
        out_specs=(P("row", "col", None, None), P("row", "col")),
        check_vma=False,
    )
```

```python
import functools

import jax
import jax.numpy as jnp
from jax import lax
from jax.experimental import pallas as pl
from jax.experimental.pallas import tpu as pltpu
from jax.sharding import PartitionSpec as P

CHI = 12
LEVELS = 3
SWEEPS = 2
PAD = 16
SHIFT = 4
ROWS = CHI * PAD
LANES = PAD * PAD
VMEM_BYTES = 8 << 20
F32 = jnp.float32
BF16 = jnp.bfloat16

NN = (((1,), (0,)), ((), ()))
NT = (((1,), (1,)), ((), ()))
TN = (((0,), (0,)), ((), ()))


def mm(a, b, dims=NN):
    return lax.dot_general(a, b, dims, preferred_element_type=F32)


def iota(shape, dim):
    return lax.broadcasted_iota(jnp.int32, shape, dim)


def group(index):
    return lax.shift_right_logical(index, SHIFT)


def minor(index):
    return lax.bitwise_and(index, PAD - 1)


def one_hot(mask):
    return jnp.where(mask, 1.0, 0.0).astype(BF16)


def swap_matrix(rows=LANES):
    i, j = iota((rows, LANES), 0), iota((rows, LANES), 1)
    return one_hot((group(i) == minor(j)) & (minor(i) == group(j)))


def spread_matrix(mirror):
    i, j = iota((CHI * CHI, LANES), 0), iota((CHI * CHI, LANES), 1)
    s, t = group(j), minor(j)
    source = jnp.where(mirror, t * CHI + s, s * CHI + t)
    return one_hot((i == source) & (s < CHI) & (t < CHI))


def row_spread():
    i, j = iota((ROWS, CHI * CHI), 0), iota((ROWS, CHI * CHI), 1)
    return one_hot((j == minor(i) * CHI + group(i)) & (minor(i) < CHI))


def block_swap(x):
    lane_group = group(iota((PAD, 128), 1))
    zero = jnp.zeros((PAD, 128), x.dtype)
    tiles = {}
    for p in range(PAD):
        for t in range(2):
            src, src_tile = (p & 7) | (t << 3), p >> 3
            if src < CHI:
                tiles[p, t] = x[src * PAD : (src + 1) * PAD, src_tile * 128 : (src_tile + 1) * 128]
            else:
                tiles[p, t] = None
    for bit in range(3):
        step = 1 << bit
        low = lax.bitwise_and(lane_group, step) == 0
        new = {}
        for p in range(PAD):
            if p & step:
                continue
            for t in range(2):
                a, b = tiles[p, t], tiles[p | step, t]
                if a is None and b is None:
                    new[p, t] = new[p | step, t] = None
                    continue
                a_moved = zero if a is None else pltpu.roll(a, 128 - step * PAD, 1)
                b_moved = zero if b is None else pltpu.roll(b, step * PAD, 1)
                a = zero if a is None else a
                b = zero if b is None else b
                new[p, t] = jnp.where(low, a, b_moved)
                new[p | step, t] = jnp.where(low, a_moved, b)
        tiles = new
    rows = []
    for p in range(CHI):
        pair = [zero if tiles[p, t] is None else tiles[p, t] for t in range(2)]
        rows.append(jnp.concatenate(pair, axis=1))
    return jnp.concatenate(rows, axis=0)


def widen(x):
    return jnp.concatenate([x, jnp.zeros((x.shape[0], LANES - x.shape[1]), x.dtype)], axis=1)


def parts3(x):
    a = x.astype(BF16)
    rest = x - a.astype(F32)
    b = rest.astype(BF16)
    c = (rest - b.astype(F32)).astype(BF16)
    return jnp.concatenate([a, b, c], axis=0)


def fold3(y):
    n = y.shape[0] // 3
    return (y[2 * n :] + y[n : 2 * n]) + y[:n]


def gram_body(upper, lower, swap):
    turned = block_swap(mm(upper, swap).astype(BF16))
    row_swap = swap[:ROWS, :ROWS]
    lower_m = mm(swap[:, :ROWS], lower).astype(BF16)
    prod_b = mm(lower_m[:ROWS], lower, NT).astype(BF16)
    prod_b = block_swap(widen(prod_b))
    prod_b = mm(row_swap, prod_b).astype(BF16)
    turned_m = mm(turned, swap).astype(BF16)
    prod_a = mm(turned_m, turned, TN).astype(BF16)
    prod_a = block_swap(prod_a[:ROWS])
    outer = mm(prod_a, prod_b, NT).astype(BF16)
    return block_swap(widen(outer)), turned


def start_body(start, swap):
    start = jnp.concatenate([start, jnp.zeros((PAD - CHI, CHI * CHI), F32)], axis=0)
    pieces = parts3(start)
    spread = spread_matrix(False)
    plain = mm(pieces, spread)
    turned = mm(plain.astype(BF16), swap)
    return fold3(plain), fold3(turned)


def orthonormal(y):
    gram = lax.dot_general(
        y, y, NT, preferred_element_type=F32, precision=lax.Precision.HIGHEST
    )
    width = y.shape[1]
    row = iota((PAD, 128), 0)
    cols = [jnp.broadcast_to(gram[:, k : k + 1], (PAD, 128)) for k in range(CHI)]
    scale = jnp.zeros((PAD, 128), F32)
    for k in range(CHI):
        pivot = jnp.broadcast_to(cols[k][k : k + 1, :], (PAD, 128))
        scale = jnp.where(row == k, lax.rsqrt(pivot), scale)
        factor = jnp.where(row > k, cols[k] / pivot, 0.0)
        for j in range(k + 1, CHI):
            cols[j] = cols[j] - factor * jnp.broadcast_to(cols[j][k : k + 1, :], (PAD, 128))
        wide = jnp.concatenate([factor] * (width // 128), axis=1)
        y = y - wide * jnp.broadcast_to(y[k : k + 1, :], (PAD, width))
    return y * jnp.concatenate([scale] * (width // 128), axis=1)


def iso_body(own, other, start, start_turned, swap):
    total = own.astype(F32) + other.astype(F32)
    i, j = iota((ROWS, LANES), 0), iota((ROWS, LANES), 1)
    diagonal = (group(i) == minor(j)) & (minor(i) == group(j))
    shift = jnp.sum(jnp.where(diagonal, total, 0.0)) / (CHI * CHI)
    pieces = parts3(start)
    image = fold3(mm(pieces, own, NT) + mm(pieces, other, NT))
    image = widen(image) + shift * start_turned
    basis = orthonormal(image)
    pieces = parts3(basis)
    image = fold3(mm(pieces[:, :ROWS], own) + mm(pieces[:, :ROWS], other))
    image = image + shift * fold3(mm(pieces, swap))
    return orthonormal(image).astype(BF16)


def first_second(turned, lower, left, second_ref):
    lane = iota((PAD, LANES), 1)
    masked = [jnp.where(group(lane) == k, left.astype(F32), 0.0) for k in range(CHI)]
    masked = jnp.concatenate(masked, axis=0).astype(BF16)
    i, j = iota((LANES, LANES), 0), iota((LANES, LANES), 1)
    values = mm(masked, one_hot(minor(i) == group(j)))
    eye = minor(lane) == iota((PAD, LANES), 0)
    for a in range(CHI):
        blocks = []
        for k in range(CHI):
            line = jnp.broadcast_to(values[k * PAD + a : k * PAD + a + 1, :], (PAD, LANES))
            blocks.append(jnp.where(eye, line, 0.0).astype(BF16))
        kron = jnp.concatenate(blocks, axis=0)
        first = mm(turned[:, :ROWS], kron).astype(BF16)
        second = mm(first[:, :ROWS], lower).astype(BF16)
        for k in range(CHI):
            second_ref[a * PAD : (a + 1) * PAD, k * LANES : (k + 1) * LANES] = second[
                k * PAD : (k + 1) * PAD, :
            ]


def third(second_ref, right, kron_ref):
    tile = one_hot(minor(iota((PAD, LANES), 1)) == iota((PAD, LANES), 0))
    values = mm(right, tile, TN)
    lane_group = group(iota((PAD, LANES), 1))
    for k in range(CHI):
        block = values[k * PAD : (k + 1) * PAD, :]
        for d in range(PAD):
            kept = jnp.where(lane_group == d, block, 0.0) if d < CHI else jnp.zeros_like(block)
            start = k * LANES + d * PAD
            kron_ref[start : start + PAD, :] = kept.astype(BF16)
    return mm(second_ref[...], kron_ref[...])


def pick(is_upper, own, other):
    return jnp.where(is_upper, own, other), jnp.where(is_upper, other, own)


def first_gram_kernel(role, own, other, start, lower_o, turned_o, gram_o, starts_o):
    mirror, is_upper = role[0] != 0, role[1] != 0
    swap = swap_matrix()
    rows, spread = row_spread(), spread_matrix(mirror)

    def placed(site):
        spaced = mm(rows, site[...].astype(BF16)).astype(BF16)
        return block_swap(mm(spaced, spread).astype(BF16))

    upper, lower = pick(is_upper, placed(own), placed(other))
    gram, turned = gram_body(upper, lower, swap)
    lower_o[...], turned_o[...], gram_o[...] = lower, turned, gram
    for level in range(LEVELS):
        plain, turn = start_body(start[level], swap)
        starts_o[level, :PAD], starts_o[level, PAD:] = plain, turn


def gram_kernel(role, own, other, lower_o, turned_o, gram_o):
    upper, lower = pick(role[0] != 0, own[...], other[...])
    gram, turned = gram_body(upper, lower, swap_matrix())
    lower_o[...], turned_o[...], gram_o[...] = lower, turned, gram


def iso_kernel(own, other, starts, iso_o):
    iso_o[...] = iso_body(own[...], other[...], starts[:PAD], starts[PAD:], swap_matrix())


def second_kernel(turned, lower, left, second_o):
    first_second(turned[...], lower[...], left[...], second_o)


def scaled(merged):
    mean = jnp.sum(merged * merged) / (CHI**4)
    return jnp.sqrt(jnp.full((1, LANES), mean) + 1e-06)


def third_kernel(second, right, log_in, next_o, log_o, kron):
    merged = third(second, right[...], kron)
    norm = scaled(merged)
    next_o[...] = (merged / norm).astype(BF16)
    log_o[...] = log_in[...] + jnp.log(norm)


def last_kernel(role, second, right, log_in, coarse_o, log_o, kron):
    merged = third(second, right[...], kron)
    norm = scaled(merged)
    log_o[...] = log_in[...] + jnp.log(norm)
    wide = block_swap(merged / norm)
    spread, rows = spread_matrix(role[0] != 0), row_spread()
    total = jnp.zeros((CHI * CHI, CHI * CHI), F32)
    high = wide.astype(BF16)
    low = (wide - high.astype(F32)).astype(BF16)
    for part in (high, low):
        narrow = mm(part, spread, NT).astype(BF16)
        total = total + mm(rows, narrow, TN)
    coarse_o[...] = total


def call(kernel, outs, smem, n_in, scratch=()):
    specs = [pl.BlockSpec(memory_space=pltpu.VMEM)] * n_in
    if smem:
        specs[0] = pl.BlockSpec(memory_space=pltpu.SMEM)
    return pl.pallas_call(
        kernel,
        out_shape=[jax.ShapeDtypeStruct(s, d) for s, d in outs],
        in_specs=specs,
        out_specs=[pl.BlockSpec(memory_space=pltpu.VMEM)] * len(outs),
        scratch_shapes=list(scratch),
        compiler_params=pltpu.CompilerParams(vmem_limit_bytes=VMEM_BYTES),
    )


def from_partner(array, stride):
    count = lax.axis_size("row")
    return lax.ppermute(array, "row", [(i, i ^ 1 << stride) for i in range(count)])


def from_bond(array):
    rows, cols = lax.axis_size("row"), lax.axis_size("col")
    pairs = []
    for i in range(rows):
        for c in range(cols):
            target = (c - 1) % cols if i % 2 == 0 else (c + 1) % cols
            pairs.append((i * cols + c, (i ^ 1) * cols + target))
    return lax.ppermute(array, ("row", "col"), pairs)


def per_device(site_tensors, start_basis):
    square = CHI * CHI
    row = lax.axis_index("row")
    mirror = row % 2
    mat = ((ROWS, LANES), BF16)
    kron = [pltpu.VMEM((CHI * LANES, LANES), BF16)]
    log_total = jnp.zeros((1, LANES), F32)
    own = site_tensors[0, 0]
    for level in range(LEVELS):
        other = from_partner(own, level)
        is_upper = 1 - row // 2**level % 2
        if level == 0:
            role = jnp.stack([mirror, is_upper]).astype(jnp.int32)
            lower, turned, gram, starts = call(
                first_gram_kernel,
                [mat, mat, mat, ((LEVELS, 2 * PAD, LANES), F32)],
                True,
                4,
            )(role, own, other, start_basis)
        else:
            role = is_upper.reshape(1).astype(jnp.int32)
            lower, turned, gram = call(gram_kernel, [mat, mat, mat], True, 3)(role, own, other)
        gram_other = from_bond(gram)
        (left,) = call(iso_kernel, [((PAD, LANES), BF16)], False, 3)(gram, gram_other, starts[level])
        right = from_partner(left, 0)
        (second,) = call(second_kernel, [((ROWS, CHI * LANES), BF16)], False, 3)(turned, lower, left)
        if level < LEVELS - 1:
            own, log_total = call(third_kernel, [mat, ((1, LANES), F32)], False, 3, kron)(
                second, right, log_total
            )
        else:
            role = mirror.reshape(1).astype(jnp.int32)
            coarse, log_total = call(
                last_kernel, [((square, square), F32), ((1, LANES), F32)], True, 4, kron
            )(role, second, right, log_total)
    return (coarse[None, None], log_total[:, :1])


def solution(mesh):
    return jax.shard_map(
        per_device,
        mesh=mesh,
        in_specs=(P("row", "col", None, None), P()),
        out_specs=(P("row", "col", None, None), P("row", "col")),
        check_vma=False,
    )
```

```python
import functools

import jax
import jax.numpy as jnp
from jax import lax
from jax.experimental import pallas as pl
from jax.experimental.pallas import tpu as pltpu
from jax.sharding import PartitionSpec as P

CHI = 12
LEVELS = 3
SWEEPS = 2
PAD = 16
SHIFT = 4
ROWS = CHI * PAD
LANES = PAD * PAD
VMEM_BYTES = 8 << 20
F32 = jnp.float32
BF16 = jnp.bfloat16

NN = (((1,), (0,)), ((), ()))
NT = (((1,), (1,)), ((), ()))
TN = (((0,), (0,)), ((), ()))


def mm(a, b, dims=NN):
    return lax.dot_general(a, b, dims, preferred_element_type=F32)


def iota(shape, dim):
    return lax.broadcasted_iota(jnp.int32, shape, dim)


def group(index):
    return lax.shift_right_logical(index, SHIFT)


def minor(index):
    return lax.bitwise_and(index, PAD - 1)


def one_hot(mask):
    return jnp.where(mask, 1.0, 0.0).astype(BF16)


def swap_matrix(rows=LANES):
    i, j = iota((rows, LANES), 0), iota((rows, LANES), 1)
    return one_hot((group(i) == minor(j)) & (minor(i) == group(j)))


def spread_matrix(mirror):
    i, j = iota((CHI * CHI, LANES), 0), iota((CHI * CHI, LANES), 1)
    s, t = group(j), minor(j)
    source = jnp.where(mirror, t * CHI + s, s * CHI + t)
    return one_hot((i == source) & (s < CHI) & (t < CHI))


def row_spread():
    i, j = iota((ROWS, CHI * CHI), 0), iota((ROWS, CHI * CHI), 1)
    return one_hot((j == minor(i) * CHI + group(i)) & (minor(i) < CHI))


def block_swap(x):
    lane_group = group(iota((PAD, 128), 1))
    zero = jnp.zeros((PAD, 128), x.dtype)
    tiles = {}
    for p in range(PAD):
        for t in range(2):
            src, src_tile = (p & 7) | (t << 3), p >> 3
            if src < CHI:
                tiles[p, t] = x[src * PAD : (src + 1) * PAD, src_tile * 128 : (src_tile + 1) * 128]
            else:
                tiles[p, t] = None
    for bit in range(3):
        step = 1 << bit
        low = lax.bitwise_and(lane_group, step) == 0
        new = {}
        for p in range(PAD):
            if p & step:
                continue
            for t in range(2):
                a, b = tiles[p, t], tiles[p | step, t]
                if a is None and b is None:
                    new[p, t] = new[p | step, t] = None
                    continue
                a_moved = zero if a is None else pltpu.roll(a, 128 - step * PAD, 1)
                b_moved = zero if b is None else pltpu.roll(b, step * PAD, 1)
                a = zero if a is None else a
                b = zero if b is None else b
                new[p, t] = jnp.where(low, a, b_moved)
                new[p | step, t] = jnp.where(low, a_moved, b)
        tiles = new
    rows = []
    for p in range(CHI):
        pair = [zero if tiles[p, t] is None else tiles[p, t] for t in range(2)]
        rows.append(jnp.concatenate(pair, axis=1))
    return jnp.concatenate(rows, axis=0)


def widen(x):
    return jnp.concatenate([x, jnp.zeros((x.shape[0], LANES - x.shape[1]), x.dtype)], axis=1)


def parts3(x):
    a = x.astype(BF16)
    rest = x - a.astype(F32)
    b = rest.astype(BF16)
    c = (rest - b.astype(F32)).astype(BF16)
    return jnp.concatenate([a, b, c], axis=0)


def fold3(y):
    n = y.shape[0] // 3
    return (y[2 * n :] + y[n : 2 * n]) + y[:n]


def pack(x):
    half = ROWS // 2
    side, used = x[:, 128:], ROWS - 128
    lane = iota((half, 128), 1)
    folded = jnp.where(lane < used, side[:half], pltpu.roll(side[half:], used, 1))
    return jnp.concatenate([x[:, :128], folded], axis=0)


def unpack(x):
    half, used = ROWS // 2, ROWS - 128
    folded = x[ROWS:]
    lane = iota((half, 128), 1)
    zero = jnp.zeros((half, 128), x.dtype)
    first = jnp.where(lane < used, folded, zero)
    last = jnp.where(lane < used, pltpu.roll(folded, 128 - used, 1), zero)
    return jnp.concatenate([x[:ROWS], jnp.concatenate([first, last], axis=0)], axis=1)


def upper_part(upper, swap):
    turned = block_swap(mm(upper, swap).astype(BF16))
    turned_m = mm(turned, swap).astype(BF16)
    product = mm(turned_m, turned, TN).astype(BF16)
    return turned, block_swap(product[:ROWS])


def lower_part(lower, swap):
    lower_m = mm(swap[:, :ROWS], lower).astype(BF16)
    product = mm(lower_m[:ROWS], lower, NT).astype(BF16)
    product = block_swap(widen(product))
    return mm(swap[:ROWS, :ROWS], product).astype(BF16)


def outer_part(upper_product, lower_product):
    outer = mm(upper_product, lower_product, NT).astype(BF16)
    return block_swap(widen(outer))


def start_body(start, swap):
    start = jnp.concatenate([start, jnp.zeros((PAD - CHI, CHI * CHI), F32)], axis=0)
    pieces = parts3(start)
    spread = spread_matrix(False)
    plain = mm(pieces, spread)
    turned = mm(plain.astype(BF16), swap)
    return fold3(plain), fold3(turned)


def orthonormal(y):
    gram = lax.dot_general(
        y, y, NT, preferred_element_type=F32, precision=lax.Precision.HIGHEST
    )
    width = y.shape[1]
    row = iota((PAD, 128), 0)
    cols = [jnp.broadcast_to(gram[:, k : k + 1], (PAD, 128)) for k in range(CHI)]
    scale = jnp.zeros((PAD, 128), F32)
    for k in range(CHI):
        pivot = jnp.broadcast_to(cols[k][k : k + 1, :], (PAD, 128))
        scale = jnp.where(row == k, lax.rsqrt(pivot), scale)
        factor = jnp.where(row > k, cols[k] / pivot, 0.0)
        for j in range(k + 1, CHI):
            cols[j] = cols[j] - factor * jnp.broadcast_to(cols[j][k : k + 1, :], (PAD, 128))
        wide = jnp.concatenate([factor] * (width // 128), axis=1)
        y = y - wide * jnp.broadcast_to(y[k : k + 1, :], (PAD, width))
    return y * jnp.concatenate([scale] * (width // 128), axis=1)


def iso_body(own, other, start, start_turned, swap):
    total = own.astype(F32) + other.astype(F32)
    i, j = iota((ROWS, LANES), 0), iota((ROWS, LANES), 1)
    diagonal = (group(i) == minor(j)) & (minor(i) == group(j))
    shift = jnp.sum(jnp.where(diagonal, total, 0.0)) / (CHI * CHI)
    pieces = parts3(start)
    image = fold3(mm(pieces, own, NT) + mm(pieces, other, NT))
    image = widen(image) + shift * start_turned
    basis = orthonormal(image)
    pieces = parts3(basis)
    image = fold3(mm(pieces[:, :ROWS], own) + mm(pieces[:, :ROWS], other))
    image = image + shift * fold3(mm(pieces, swap))
    return orthonormal(image).astype(BF16)


def first_second(turned, lower, left, second_ref):
    lane = iota((PAD, LANES), 1)
    masked = [jnp.where(group(lane) == k, left.astype(F32), 0.0) for k in range(CHI)]
    masked = jnp.concatenate(masked, axis=0).astype(BF16)
    i, j = iota((LANES, LANES), 0), iota((LANES, LANES), 1)
    values = mm(masked, one_hot(minor(i) == group(j)))
    eye = minor(lane) == iota((PAD, LANES), 0)
    for a in range(CHI):
        blocks = []
        for k in range(CHI):
            line = jnp.broadcast_to(values[k * PAD + a : k * PAD + a + 1, :], (PAD, LANES))
            blocks.append(jnp.where(eye, line, 0.0).astype(BF16))
        kron = jnp.concatenate(blocks, axis=0)
        first = mm(turned[:, :ROWS], kron).astype(BF16)
        second = mm(first[:, :ROWS], lower).astype(BF16)
        for k in range(CHI):
            second_ref[a * PAD : (a + 1) * PAD, k * LANES : (k + 1) * LANES] = second[
                k * PAD : (k + 1) * PAD, :
            ]


def third(second_ref, right, kron_ref):
    tile = one_hot(minor(iota((PAD, LANES), 1)) == iota((PAD, LANES), 0))
    values = mm(right, tile, TN)
    lane_group = group(iota((PAD, LANES), 1))
    for k in range(CHI):
        block = values[k * PAD : (k + 1) * PAD, :]
        for d in range(PAD):
            kept = jnp.where(lane_group == d, block, 0.0) if d < CHI else jnp.zeros_like(block)
            start = k * LANES + d * PAD
            kron_ref[start : start + PAD, :] = kept.astype(BF16)
    return mm(second_ref[...], kron_ref[...])


def placed(site, mirror):
    spaced = mm(row_spread(), site.astype(BF16)).astype(BF16)
    return block_swap(mm(spaced, spread_matrix(mirror)).astype(BF16))


def first_own_kernel(role, own, start, own_o, starts_o, site, basis, sems):
    copies = [
        pltpu.make_async_copy(own, site, sems.at[0]),
        pltpu.make_async_copy(start, basis, sems.at[1]),
    ]
    for copy in copies:
        copy.start()
    copies[0].wait()
    own_o[...] = placed(site[...], role[0] != 0)
    copies[1].wait()
    swap = swap_matrix()
    for level in range(LEVELS):
        plain, turn = start_body(basis[level], swap)
        starts_o[level, :PAD], starts_o[level, PAD:] = plain, turn


def first_gram_kernel(role, own, other, lower_o, turned_o, gram_o):
    swap = swap_matrix()
    mine, theirs = own[...], placed(other[...], role[0] != 0)
    is_upper = role[1] != 0
    upper, lower = jnp.where(is_upper, mine, theirs), jnp.where(is_upper, theirs, mine)
    turned, upper_product = upper_part(upper, swap)
    gram_o[...] = pack(outer_part(upper_product, lower_part(lower, swap)))
    lower_o[...], turned_o[...] = lower, turned


def own_kernel(role, own, wide_o, turned_o, product_o):
    swap = swap_matrix()
    wide = unpack(own[...])
    wide_o[...] = wide

    @pl.when(role[0] != 0)
    def _():
        turned_o[...], product_o[...] = upper_part(wide, swap)

    @pl.when(role[0] == 0)
    def _():
        turned_o[...] = jnp.zeros_like(turned_o)
        product_o[...] = lower_part(wide, swap)


def gram_kernel(role, wide, own_turned, product, other, lower_o, turned_o, gram_o, up, low):
    swap = swap_matrix()
    theirs = unpack(other[...])

    @pl.when(role[0] != 0)
    def _():
        lower_o[...], turned_o[...] = theirs, own_turned[...]
        up[...], low[...] = product[...], lower_part(theirs, swap)

    @pl.when(role[0] == 0)
    def _():
        lower_o[...] = wide[...]
        turned_o[...], up[...] = upper_part(theirs, swap)
        low[...] = product[...]

    gram_o[...] = pack(outer_part(up[...], low[...]))


def iso_kernel(own, other, starts, iso_o):
    iso_o[...] = iso_body(unpack(own[...]), unpack(other[...]), starts[:PAD], starts[PAD:], swap_matrix())


def second_kernel(turned, lower, left, second_o):
    first_second(turned[...], lower[...], left[...], second_o)


def scaled(merged):
    mean = jnp.sum(merged * merged) / (CHI**4)
    return jnp.sqrt(jnp.full((1, LANES), mean) + 1e-06)


def third_kernel(second, right, log_in, next_o, log_o, kron):
    merged = third(second, right[...], kron)
    norm = scaled(merged)
    next_o[...] = pack((merged / norm).astype(BF16))
    log_o[...] = log_in[...] + jnp.log(norm)


def last_kernel(role, second, right, log_in, coarse_o, log_o, kron):
    merged = third(second, right[...], kron)
    norm = scaled(merged)
    log_o[...] = (log_in[...] + jnp.log(norm))[:, :1]
    wide = block_swap(merged / norm)
    spread, rows = spread_matrix(role[0] != 0), row_spread()
    total = jnp.zeros((CHI * CHI, CHI * CHI), F32)
    high = wide.astype(BF16)
    low = (wide - high.astype(F32)).astype(BF16)
    for part in (high, low):
        narrow = mm(part, spread, NT).astype(BF16)
        total = total + mm(rows, narrow, TN)
    coarse_o[...] = total


def call(kernel, outs, places, scratch=()):
    return pl.pallas_call(
        kernel,
        out_shape=[jax.ShapeDtypeStruct(s, d) for s, d in outs],
        in_specs=[pl.BlockSpec(memory_space=place) for place in places],
        out_specs=[pl.BlockSpec(memory_space=pltpu.VMEM)] * len(outs),
        scratch_shapes=list(scratch),
        compiler_params=pltpu.CompilerParams(vmem_limit_bytes=VMEM_BYTES),
        cost_estimate=pl.CostEstimate(flops=10**8, bytes_accessed=10**6, transcendentals=0),
    )


def from_partner(array, flip):
    count = lax.axis_size("row")
    return lax.ppermute(array, "row", [(i, i ^ flip) for i in range(count)])


def mirrored(row):
    parity = row * 0
    for bit in range(LEVELS):
        parity = parity ^ (row >> bit & 1)
    return parity


def from_bond(array):
    rows, cols = lax.axis_size("row"), lax.axis_size("col")
    pairs = []
    for i in range(rows):
        for c in range(cols):
            target = (c + 1) % cols if mirrored(i) else (c - 1) % cols
            pairs.append((i * cols + c, (i ^ 1) * cols + target))
    return lax.ppermute(array, ("row", "col"), pairs)


def per_device(site_tensors, start_basis):
    square = CHI * CHI
    row = lax.axis_index("row")
    mirror = mirrored(row)
    vmem, smem, hbm = pltpu.VMEM, pltpu.SMEM, pltpu.HBM
    mat, packed = ((ROWS, LANES), BF16), ((ROWS * 3 // 2, 128), BF16)
    kron = [vmem((CHI * LANES, LANES), BF16)]
    log_total = jnp.zeros((1, LANES), F32)
    own = site_tensors[0, 0]
    for level in range(LEVELS):
        is_upper = 1 - (row >> level & 1)
        if level == 0:
            other = from_partner(own, 1)
            role = jnp.stack([mirror, is_upper]).astype(jnp.int32)
            wide, starts = call(
                first_own_kernel,
                [mat, ((LEVELS, 2 * PAD, LANES), F32)],
                [smem, hbm, hbm],
                [
                    vmem((square, square), F32),
                    vmem((LEVELS, CHI, square), F32),
                    pltpu.SemaphoreType.DMA((2,)),
                ],
            )(role, own, start_basis)
            lower, turned, gram = call(first_gram_kernel, [mat, mat, packed], [smem, vmem, vmem])(
                role, wide, other
            )
        else:
            other = from_partner(own, 1 << level | 1)
            role = is_upper.reshape(1).astype(jnp.int32)
            wide, own_turned, product = call(own_kernel, [mat, mat, mat], [smem, vmem])(role, own)
            lower, turned, gram = call(
                gram_kernel,
                [mat, mat, packed],
                [smem, vmem, vmem, vmem, vmem],
                [vmem(*mat), vmem(*mat)],
            )(role, wide, own_turned, product, other)
        gram_other = from_bond(gram)
        (left,) = call(iso_kernel, [((PAD, LANES), BF16)], [vmem] * 3)(
            gram, gram_other, starts[level]
        )
        right = from_partner(left, 1)
        (second,) = call(second_kernel, [((ROWS, CHI * LANES), BF16)], [vmem] * 3)(
            turned, lower, left
        )
        if level < LEVELS - 1:
            own, log_total = call(third_kernel, [packed, ((1, LANES), F32)], [vmem] * 3, kron)(
                second, right, log_total
            )
        else:
            role = mirror.reshape(1).astype(jnp.int32)
            coarse, log_total = call(
                last_kernel, [((square, square), F32), ((1, 1), F32)], [smem] + [vmem] * 3, kron
            )(role, second, right, log_total)
    return (coarse[None, None], log_total)


def solution(mesh):
    return jax.shard_map(
        per_device,
        mesh=mesh,
        in_specs=(P("row", "col", None, None), P()),
        out_specs=(P("row", "col", None, None), P("row", "col")),
        check_vma=False,
    )
```

```python
import functools

import jax
import jax.numpy as jnp
from jax import lax
from jax.experimental import pallas as pl
from jax.experimental.pallas import tpu as pltpu
from jax.sharding import PartitionSpec as P

CHI = 12
LEVELS = 3
SWEEPS = 2
PAD = 16
SHIFT = 4
ROWS = CHI * PAD
LANES = PAD * PAD
VMEM_BYTES = 8 << 20
PIVOT = 1.0 / 64
F32 = jnp.float32
BF16 = jnp.bfloat16

NN = (((1,), (0,)), ((), ()))
NT = (((1,), (1,)), ((), ()))
TN = (((0,), (0,)), ((), ()))


def mm(a, b, dims=NN):
    return lax.dot_general(a, b, dims, preferred_element_type=F32)


def iota(shape, dim):
    return lax.broadcasted_iota(jnp.int32, shape, dim)


def group(index):
    return lax.shift_right_logical(index, SHIFT)


def minor(index):
    return lax.bitwise_and(index, PAD - 1)


def one_hot(mask):
    return jnp.where(mask, 1.0, 0.0).astype(BF16)


def swap_matrix(rows=LANES):
    i, j = iota((rows, LANES), 0), iota((rows, LANES), 1)
    return one_hot((group(i) == minor(j)) & (minor(i) == group(j)))


def spread_matrix(mirror):
    i, j = iota((CHI * CHI, LANES), 0), iota((CHI * CHI, LANES), 1)
    s, t = group(j), minor(j)
    source = jnp.where(mirror, t * CHI + s, s * CHI + t)
    return one_hot((i == source) & (s < CHI) & (t < CHI))


def row_spread(turn):
    i, j = iota((ROWS, CHI * CHI), 0), iota((ROWS, CHI * CHI), 1)
    s, t = group(i), minor(i)
    source = t * CHI + s if turn else s * CHI + t
    return one_hot((j == source) & (t < CHI))


def block_swap(x):
    lane_group = group(iota((PAD, 128), 1))
    zero = jnp.zeros((PAD, 128), x.dtype)
    tiles = {}
    for p in range(PAD):
        for t in range(2):
            src, src_tile = (p & 7) | (t << 3), p >> 3
            if src < CHI:
                tiles[p, t] = x[src * PAD : (src + 1) * PAD, src_tile * 128 : (src_tile + 1) * 128]
            else:
                tiles[p, t] = None
    for bit in range(3):
        step = 1 << bit
        low = lax.bitwise_and(lane_group, step) == 0
        new = {}
        for p in range(PAD):
            if p & step:
                continue
            for t in range(2):
                a, b = tiles[p, t], tiles[p | step, t]
                if a is None and b is None:
                    new[p, t] = new[p | step, t] = None
                    continue
                a_moved = zero if a is None else pltpu.roll(a, 128 - step * PAD, 1)
                b_moved = zero if b is None else pltpu.roll(b, step * PAD, 1)
                a = zero if a is None else a
                b = zero if b is None else b
                new[p, t] = jnp.where(low, a, b_moved)
                new[p | step, t] = jnp.where(low, a_moved, b)
        tiles = new
    rows = []
    for p in range(CHI):
        pair = [zero if tiles[p, t] is None else tiles[p, t] for t in range(2)]
        rows.append(jnp.concatenate(pair, axis=1))
    return jnp.concatenate(rows, axis=0)


def widen(x):
    return jnp.concatenate([x, jnp.zeros((x.shape[0], LANES - x.shape[1]), x.dtype)], axis=1)


def parts3(x):
    a = x.astype(BF16)
    rest = x - a.astype(F32)
    b = rest.astype(BF16)
    c = (rest - b.astype(F32)).astype(BF16)
    return jnp.concatenate([a, b, c], axis=0)


def parts2(x):
    a = x.astype(BF16)
    return jnp.concatenate([a, (x - a.astype(F32)).astype(BF16)], axis=0)


def fold2(y):
    n = y.shape[0] // 2
    return y[n:] + y[:n]


def fold3(y):
    n = y.shape[0] // 3
    return (y[2 * n :] + y[n : 2 * n]) + y[:n]


def pack(x):
    half = ROWS // 2
    side, used = x[:, 128:], ROWS - 128
    lane = iota((half, 128), 1)
    folded = jnp.where(lane < used, side[:half], pltpu.roll(side[half:], used, 1))
    return jnp.concatenate([x[:, :128], folded], axis=0)


def unpack(x):
    half, used = ROWS // 2, ROWS - 128
    folded = x[ROWS:]
    lane = iota((half, 128), 1)
    zero = jnp.zeros((half, 128), x.dtype)
    first = jnp.where(lane < used, folded, zero)
    last = jnp.where(lane < used, pltpu.roll(folded, 128 - used, 1), zero)
    return jnp.concatenate([x[:ROWS], jnp.concatenate([first, last], axis=0)], axis=1)


def turn(upper, swap):
    return block_swap(mm(upper, swap).astype(BF16))


def upper_product(crossed, crossed_m):
    product = mm(crossed_m, crossed, NT).astype(BF16)
    return block_swap(widen(product))


def upper_part(upper, swap):
    row_swap = swap[:ROWS, :ROWS]
    crossed_m = block_swap(mm(row_swap, upper).astype(BF16))
    return upper_product(mm(row_swap, crossed_m).astype(BF16), crossed_m)


def lower_part(lower, swap):
    row_swap = swap[:ROWS, :ROWS]
    lower_m = mm(row_swap, lower).astype(BF16)
    product = mm(lower_m, lower, NT).astype(BF16)
    product = block_swap(widen(product))
    return mm(row_swap, product).astype(BF16)


def outer_part(high, low):
    outer = mm(high, low, NT).astype(BF16)
    return block_swap(widen(outer))


def start_body(start, swap):
    start = jnp.concatenate([start, jnp.zeros((PAD - CHI, CHI * CHI), F32)], axis=0)
    pieces = parts3(start)
    spread = spread_matrix(False)
    plain = mm(pieces, spread)
    turned = mm(plain.astype(BF16), swap)
    return fold3(plain), fold3(turned)


def orthonormal(y):
    pieces = parts2(y)
    high, low = pieces[:PAD], pieces[PAD:]
    gram = fold2(mm(pieces, high, NT)) + mm(high, low, NT)
    width = y.shape[1]
    row = iota((PAD, 128), 0)
    cols = [jnp.broadcast_to(gram[:, k : k + 1], (PAD, 128)) for k in range(CHI)]
    floors = [jnp.broadcast_to(cols[k][k : k + 1, :], (PAD, 128)) * PIVOT for k in range(CHI)]
    scale = jnp.zeros((PAD, 128), F32)
    good = jnp.ones((PAD, 128), F32)
    for k in range(CHI):
        pivot = jnp.broadcast_to(cols[k][k : k + 1, :], (PAD, 128))
        good = jnp.where(pivot >= floors[k], good, 0.0)
        inverse = lax.rsqrt(pivot)
        scale = jnp.where(row == k, inverse, scale)
        factor = jnp.where(row > k, cols[k] * (inverse * inverse), 0.0)
        for j in range(k + 1, CHI):
            cols[j] = cols[j] - factor * jnp.broadcast_to(cols[j][k : k + 1, :], (PAD, 128))
        wide = jnp.concatenate([factor] * (width // 128), axis=1)
        y = y - wide * jnp.broadcast_to(y[k : k + 1, :], (PAD, width))
    return y * jnp.concatenate([scale] * (width // 128), axis=1), good


def exact_iso(own, other, start, start_turned, shift, swap):
    pieces = parts3(start)
    image = fold3(mm(pieces, own, NT) + mm(pieces, other, NT))
    basis, _ = orthonormal(widen(image) + shift * start_turned)
    pieces = parts3(basis)
    image = fold3(mm(pieces[:, :ROWS], own) + mm(pieces[:, :ROWS], other))
    basis, _ = orthonormal(image + shift * fold3(mm(pieces, swap)))
    return basis


def iso_kernel(own, other, starts, iso_o):
    own, other = unpack(own[...]), unpack(other[...])
    start, start_turned = starts[:PAD], starts[PAD:]
    swap = swap_matrix()
    total = own.astype(F32) + other.astype(F32)
    i, j = iota((ROWS, LANES), 0), iota((ROWS, LANES), 1)
    diagonal = (group(i) == minor(j)) & (minor(i) == group(j))
    trace = jnp.sum(jnp.where(diagonal, total, 0.0), axis=0, keepdims=True)
    shift = jnp.sum(trace, axis=1, keepdims=True) / (CHI * CHI)
    unit = 1.0 / shift
    pieces = parts2(start)
    image = fold2(mm(pieces, own, NT) + mm(pieces, other, NT))
    image = widen(image) * unit + start_turned
    pieces = parts2(image)
    image = fold2(mm(pieces[:, :ROWS], own) + mm(pieces[:, :ROWS], other)) * unit
    basis, good = orthonormal(image + fold2(mm(pieces, swap)))
    iso_o[...] = basis.astype(BF16)

    @pl.when(jnp.logical_not(jnp.min(good[:1]) > 0.5))
    def _():
        iso_o[...] = exact_iso(own, other, start, start_turned, shift, swap).astype(BF16)


def first_second(turned, lower, left, second_ref):
    lane = iota((PAD, LANES), 1)
    masked = [jnp.where(group(lane) == k, left.astype(F32), 0.0) for k in range(CHI)]
    masked = jnp.concatenate(masked, axis=0).astype(BF16)
    i, j = iota((LANES, LANES), 0), iota((LANES, LANES), 1)
    values = mm(masked, one_hot(minor(i) == group(j)))
    eye = minor(lane) == iota((PAD, LANES), 0)
    for a in range(CHI):
        blocks = []
        for k in range(CHI):
            line = jnp.broadcast_to(values[k * PAD + a : k * PAD + a + 1, :], (PAD, LANES))
            blocks.append(jnp.where(eye, line, 0.0).astype(BF16))
        kron = jnp.concatenate(blocks, axis=0)
        first = mm(turned[:, :ROWS], kron).astype(BF16)
        second = mm(first[:, :ROWS], lower).astype(BF16)
        for k in range(CHI):
            second_ref[a * PAD : (a + 1) * PAD, k * LANES : (k + 1) * LANES] = second[
                k * PAD : (k + 1) * PAD, :
            ]


def third(second_ref, right, kron_ref):
    tile = one_hot(minor(iota((PAD, LANES), 1)) == iota((PAD, LANES), 0))
    values = mm(right, tile, TN)
    lane_group = group(iota((PAD, LANES), 1))
    for k in range(CHI):
        block = values[k * PAD : (k + 1) * PAD, :]
        for d in range(PAD):
            kept = jnp.where(lane_group == d, block, 0.0) if d < CHI else jnp.zeros_like(block)
            start = k * LANES + d * PAD
            kron_ref[start : start + PAD, :] = kept.astype(BF16)
    return mm(second_ref[...], kron_ref[...])


def placed(site, mirror, turned):
    spaced = mm(row_spread(turned), site).astype(BF16)
    return block_swap(mm(spaced, spread_matrix(mirror)).astype(BF16))


def pick(is_upper, own, other):
    return jnp.where(is_upper, own, other), jnp.where(is_upper, other, own)


def cast_kernel(own, cast_o):
    cast_o[...] = own[...].astype(BF16)


def first_gram_kernel(role, own, other, lower_o, gram_o):
    swap = swap_matrix()
    mirror = role[0] != 0
    upper, lower = pick(role[1] != 0, own[...], other[...].astype(BF16))
    crossed = placed(upper, mirror, False)
    crossed_m = mm(swap[:ROWS, :ROWS], crossed).astype(BF16)
    lower = placed(lower, mirror, True)
    lower_o[...] = lower
    high = upper_product(crossed, crossed_m)
    gram_o[...] = pack(outer_part(high, lower_part(lower, swap)))


def first_turn_kernel(role, own, other, start, turned_o, starts_o):
    swap = swap_matrix()
    upper, _ = pick(role[1] != 0, own[...], other[...].astype(BF16))
    turned_o[...] = turn(placed(upper, role[0] != 0, True), swap)
    for level in range(LEVELS):
        plain, turned = start_body(start[level], swap)
        starts_o[level, :PAD], starts_o[level, PAD:] = plain, turned


def own_kernel(role, own, wide_o, product_o):
    swap = swap_matrix()
    wide = unpack(own[...])
    wide_o[...] = wide

    @pl.when(role[0] != 0)
    def _():
        product_o[...] = upper_part(wide, swap)

    @pl.when(role[0] == 0)
    def _():
        product_o[...] = lower_part(wide, swap)


def gram_kernel(role, wide, product, other, upper_o, lower_o, gram_o, high, low):
    swap = swap_matrix()
    theirs = unpack(other[...])

    @pl.when(role[0] != 0)
    def _():
        upper_o[...], lower_o[...] = wide[...], theirs
        high[...], low[...] = product[...], lower_part(theirs, swap)

    @pl.when(role[0] == 0)
    def _():
        upper_o[...], lower_o[...] = theirs, wide[...]
        high[...], low[...] = upper_part(theirs, swap), product[...]

    gram_o[...] = pack(outer_part(high[...], low[...]))


def turn_kernel(upper, turned_o):
    turned_o[...] = turn(upper[...], swap_matrix())


def second_kernel(turned, lower, left, second_o):
    first_second(turned[...], lower[...], left[...], second_o)


def mean_square(merged):
    total = jnp.sum(jnp.sum(merged * merged, axis=0, keepdims=True), axis=1, keepdims=True)
    return total / (CHI**4) + 1e-06


def third_kernel(second, right, log_in, next_o, log_o, kron):
    merged = third(second, right[...], kron)
    mean = mean_square(merged)
    next_o[...] = pack((merged * lax.rsqrt(mean)).astype(BF16))
    log_o[...] = log_in[...] + 0.5 * jnp.log(mean)


def last_kernel(role, second, right, log_in, coarse_o, log_o, kron):
    merged = third(second, right[...], kron)
    mean = mean_square(merged)
    log_o[...] = log_in[...] + 0.5 * jnp.log(mean)
    wide = block_swap(merged.astype(BF16))
    narrow = mm(wide, spread_matrix(role[0] != 0), NT).astype(BF16)
    coarse_o[...] = mm(row_spread(True), narrow, TN) * lax.rsqrt(mean)


def call(kernel, outs, places, scratch=()):
    return pl.pallas_call(
        kernel,
        out_shape=[jax.ShapeDtypeStruct(s, d) for s, d in outs],
        in_specs=[pl.BlockSpec(memory_space=place) for place in places],
        out_specs=[pl.BlockSpec(memory_space=pltpu.VMEM)] * len(outs),
        scratch_shapes=list(scratch),
        compiler_params=pltpu.CompilerParams(vmem_limit_bytes=VMEM_BYTES),
        cost_estimate=pl.CostEstimate(flops=10**8, bytes_accessed=10**6, transcendentals=0),
    )


def from_partner(array, flip):
    count = lax.axis_size("row")
    return lax.ppermute(array, "row", [(i, i ^ flip) for i in range(count)])


def mirrored(row):
    parity = row * 0
    for bit in range(LEVELS):
        parity = parity ^ (row >> bit & 1)
    return parity


def from_bond(array):
    rows, cols = lax.axis_size("row"), lax.axis_size("col")
    pairs = []
    for i in range(rows):
        for c in range(cols):
            target = (c + 1) % cols if mirrored(i) else (c - 1) % cols
            pairs.append((i * cols + c, (i ^ 1) * cols + target))
    return lax.ppermute(array, ("row", "col"), pairs)


def per_device(site_tensors, start_basis):
    square = CHI * CHI
    row = lax.axis_index("row")
    mirror = mirrored(row)
    vmem, smem = pltpu.VMEM, pltpu.SMEM
    mat, packed = ((ROWS, LANES), BF16), ((ROWS * 3 // 2, 128), BF16)
    kron = [vmem((CHI * LANES, LANES), BF16)]
    log_total = jnp.zeros((1, 1), F32)
    own = site_tensors[0, 0]
    for level in range(LEVELS):
        is_upper = 1 - (row >> level & 1)
        if level == 0:
            other = from_partner(own, 1)
            role = jnp.stack([mirror, is_upper]).astype(jnp.int32)
            (own,) = call(cast_kernel, [((square, square), BF16)], [vmem])(own)
            lower, gram = call(first_gram_kernel, [mat, packed], [smem, vmem, vmem])(
                role, own, other
            )
            gram_other = from_bond(gram)
            turned, starts = call(
                first_turn_kernel,
                [mat, ((LEVELS, 2 * PAD, LANES), F32)],
                [smem, vmem, vmem, vmem],
            )(role, own, other, start_basis)
        else:
            other = from_partner(own, 1 << level | 1)
            role = is_upper.reshape(1).astype(jnp.int32)
            wide, product = call(own_kernel, [mat, mat], [smem, vmem])(role, own)
            upper, lower, gram = call(
                gram_kernel,
                [mat, mat, packed],
                [smem, vmem, vmem, vmem],
                [vmem(*mat), vmem(*mat)],
            )(role, wide, product, other)
            gram_other = from_bond(gram)
            (turned,) = call(turn_kernel, [mat], [vmem])(upper)
        (left,) = call(iso_kernel, [((PAD, LANES), BF16)], [vmem] * 3)(
            gram, gram_other, starts[level]
        )
        right = from_partner(left, 1)
        (second,) = call(second_kernel, [((ROWS, CHI * LANES), BF16)], [vmem] * 3)(
            turned, lower, left
        )
        if level < LEVELS - 1:
            own, log_total = call(third_kernel, [packed, ((1, 1), F32)], [vmem] * 3, kron)(
                second, right, log_total
            )
        else:
            role = mirror.reshape(1).astype(jnp.int32)
            coarse, log_total = call(
                last_kernel, [((square, square), F32), ((1, 1), F32)], [smem] + [vmem] * 3, kron
            )(role, second, right, log_total)
    return (coarse[None, None], log_total)


def solution(mesh):
    return jax.shard_map(
        per_device,
        mesh=mesh,
        in_specs=(P("row", "col", None, None), P()),
        out_specs=(P("row", "col", None, None), P("row", "col")),
        check_vma=False,
    )
```

```python
import functools

import functools

import jax
import jax.numpy as jnp
from jax import lax
from jax.experimental import pallas as pl
from jax.experimental.pallas import tpu as pltpu
from jax.sharding import PartitionSpec as P

CHI = 12
LEVELS = 3
SWEEPS = 2
PAD = 16
SHIFT = 4
ROWS = CHI * PAD
LANES = PAD * PAD
VMEM_BYTES = 8 << 20
PIVOT = 1.0 / 64
F32 = jnp.float32
BF16 = jnp.bfloat16

NN = (((1,), (0,)), ((), ()))
NT = (((1,), (1,)), ((), ()))
TN = (((0,), (0,)), ((), ()))


def mm(a, b, dims=NN):
    return lax.dot_general(a, b, dims, preferred_element_type=F32)


def iota(shape, dim):
    return lax.broadcasted_iota(jnp.int32, shape, dim)


def group(index):
    return lax.shift_right_logical(index, SHIFT)


def minor(index):
    return lax.bitwise_and(index, PAD - 1)


def one_hot(mask):
    return jnp.where(mask, 1.0, 0.0).astype(BF16)


def swap_matrix(rows=LANES):
    i, j = iota((rows, LANES), 0), iota((rows, LANES), 1)
    return one_hot((group(i) == minor(j)) & (minor(i) == group(j)))


def spread_matrix(mirror):
    i, j = iota((CHI * CHI, LANES), 0), iota((CHI * CHI, LANES), 1)
    s, t = group(j), minor(j)
    source = jnp.where(mirror, t * CHI + s, s * CHI + t)
    return one_hot((i == source) & (s < CHI) & (t < CHI))


def row_spread(turn):
    i, j = iota((ROWS, CHI * CHI), 0), iota((ROWS, CHI * CHI), 1)
    s, t = group(i), minor(i)
    source = jnp.where(turn, t * CHI + s, s * CHI + t)
    return one_hot((j == source) & (t < CHI))


def block_swap(x):
    lane_group = group(iota((PAD, 128), 1))
    zero = jnp.zeros((PAD, 128), x.dtype)
    tiles = {}
    for p in range(PAD):
        for t in range(2):
            src, src_tile = (p & 7) | (t << 3), p >> 3
            if src < CHI:
                tiles[p, t] = x[src * PAD : (src + 1) * PAD, src_tile * 128 : (src_tile + 1) * 128]
            else:
                tiles[p, t] = None
    for bit in range(3):
        step = 1 << bit
        low = lax.bitwise_and(lane_group, step) == 0
        new = {}
        for p in range(PAD):
            if p & step:
                continue
            for t in range(2):
                a, b = tiles[p, t], tiles[p | step, t]
                if a is None and b is None:
                    new[p, t] = new[p | step, t] = None
                    continue
                a_moved = zero if a is None else pltpu.roll(a, 128 - step * PAD, 1)
                b_moved = zero if b is None else pltpu.roll(b, step * PAD, 1)
                a = zero if a is None else a
                b = zero if b is None else b
                new[p, t] = jnp.where(low, a, b_moved)
                new[p | step, t] = jnp.where(low, a_moved, b)
        tiles = new
    rows = []
    for p in range(CHI):
        pair = [zero if tiles[p, t] is None else tiles[p, t] for t in range(2)]
        rows.append(jnp.concatenate(pair, axis=1))
    return jnp.concatenate(rows, axis=0)


def widen(x):
    return jnp.concatenate([x, jnp.zeros((x.shape[0], LANES - x.shape[1]), x.dtype)], axis=1)


def parts3(x):
    a = x.astype(BF16)
    rest = x - a.astype(F32)
    b = rest.astype(BF16)
    c = (rest - b.astype(F32)).astype(BF16)
    return jnp.concatenate([a, b, c], axis=0)


def parts2(x):
    a = x.astype(BF16)
    return jnp.concatenate([a, (x - a.astype(F32)).astype(BF16)], axis=0)


def fold2(y):
    n = y.shape[0] // 2
    return y[n:] + y[:n]


def fold3(y):
    n = y.shape[0] // 3
    return (y[2 * n :] + y[n : 2 * n]) + y[:n]


def pack(x):
    half = ROWS // 2
    side, used = x[:, 128:], ROWS - 128
    lane = iota((half, 128), 1)
    folded = jnp.where(lane < used, side[:half], pltpu.roll(side[half:], used, 1))
    return jnp.concatenate([x[:, :128], folded], axis=0)


def unpack(x):
    half, used = ROWS // 2, ROWS - 128
    folded = x[ROWS:]
    lane = iota((half, 128), 1)
    zero = jnp.zeros((half, 128), x.dtype)
    first = jnp.where(lane < used, folded, zero)
    last = jnp.where(lane < used, pltpu.roll(folded, 128 - used, 1), zero)
    return jnp.concatenate([x[:ROWS], jnp.concatenate([first, last], axis=0)], axis=1)


def row_swap(x):
    legs = x.astype(F32).reshape(CHI, PAD, x.shape[1])[:, :CHI]
    turned = jnp.transpose(legs, (1, 0, 2))
    rest = jnp.zeros((CHI, PAD - CHI, x.shape[1]), F32)
    return jnp.concatenate([turned, rest], axis=1).reshape(x.shape).astype(BF16)


def product_part(x):
    product = mm(row_swap(x), x, NT).astype(BF16)
    return block_swap(widen(product))


def outer_part(first, second):
    outer = mm(first, row_swap(second), NT).astype(BF16)
    return block_swap(widen(outer))


def turn(first):
    return widen(row_swap(first.T[:ROWS]))


def start_body(start, swap):
    start = jnp.concatenate([start, jnp.zeros((PAD - CHI, CHI * CHI), F32)], axis=0)
    pieces = parts3(start)
    spread = spread_matrix(False)
    plain = mm(pieces, spread)
    turned = mm(plain.astype(BF16), swap)
    return fold3(plain), fold3(turned)


def orthonormal(y):
    pieces = parts2(y)
    high, low = pieces[:PAD], pieces[PAD:]
    gram = fold2(mm(pieces, high, NT)) + mm(high, low, NT)
    width = y.shape[1]
    row = iota((PAD, 128), 0)
    cols = [jnp.broadcast_to(gram[:, k : k + 1], (PAD, 128)) for k in range(CHI)]
    floors = [jnp.broadcast_to(cols[k][k : k + 1, :], (PAD, 128)) * PIVOT for k in range(CHI)]
    scale = jnp.zeros((PAD, 128), F32)
    good = jnp.ones((PAD, 128), F32)
    for k in range(CHI):
        pivot = jnp.broadcast_to(cols[k][k : k + 1, :], (PAD, 128))
        good = jnp.where(pivot >= floors[k], good, 0.0)
        inverse = lax.rsqrt(pivot)
        scale = jnp.where(row == k, inverse, scale)
        factor = jnp.where(row > k, cols[k] * (inverse * inverse), 0.0)
        for j in range(k + 1, CHI):
            cols[j] = cols[j] - factor * jnp.broadcast_to(cols[j][k : k + 1, :], (PAD, 128))
        wide = jnp.concatenate([factor] * (width // 128), axis=1)
        y = y - wide * jnp.broadcast_to(y[k : k + 1, :], (PAD, width))
    return y * jnp.concatenate([scale] * (width // 128), axis=1), good


def exact_iso(own, other, start, start_turned, shift, swap):
    pieces = parts3(start)
    image = fold3(mm(pieces, own, NT) + mm(pieces, other, NT))
    basis, _ = orthonormal(widen(image) + shift * start_turned)
    pieces = parts3(basis)
    image = fold3(mm(pieces[:, :ROWS], own) + mm(pieces[:, :ROWS], other))
    basis, _ = orthonormal(image + shift * fold3(mm(pieces, swap)))
    return basis


def iso_kernel(own, other, starts, iso_o):
    own, other = unpack(own[...]), unpack(other[...])
    start, start_turned = starts[:PAD], starts[PAD:]
    swap = swap_matrix()
    total = own.astype(F32) + other.astype(F32)
    i, j = iota((ROWS, LANES), 0), iota((ROWS, LANES), 1)
    diagonal = (group(i) == minor(j)) & (minor(i) == group(j))
    trace = jnp.sum(jnp.where(diagonal, total, 0.0), axis=0, keepdims=True)
    shift = jnp.sum(trace, axis=1, keepdims=True) / (CHI * CHI)
    unit = 1.0 / shift
    pieces = parts2(start)
    image = fold2(mm(pieces, own, NT) + mm(pieces, other, NT))
    image = widen(image) * unit + start_turned
    pieces = parts2(image)
    image = fold2(mm(pieces[:, :ROWS], own) + mm(pieces[:, :ROWS], other)) * unit
    basis, good = orthonormal(image + fold2(mm(pieces, swap)))
    iso_o[...] = basis.astype(BF16)

    @pl.when(jnp.logical_not(jnp.min(good[:1]) > 0.5))
    def _():
        iso_o[...] = exact_iso(own, other, start, start_turned, shift, swap).astype(BF16)


def first_second(turned, lower, left, second_ref):
    lane = iota((PAD, LANES), 1)
    masked = [jnp.where(group(lane) == k, left.astype(F32), 0.0) for k in range(CHI)]
    masked = jnp.concatenate(masked, axis=0).astype(BF16)
    i, j = iota((LANES, LANES), 0), iota((LANES, LANES), 1)
    values = mm(masked, one_hot(minor(i) == group(j)))
    eye = minor(lane) == iota((PAD, LANES), 0)
    for a in range(CHI):
        blocks = []
        for k in range(CHI):
            line = jnp.broadcast_to(values[k * PAD + a : k * PAD + a + 1, :], (PAD, LANES))
            blocks.append(jnp.where(eye, line, 0.0).astype(BF16))
        kron = jnp.concatenate(blocks, axis=0)
        first = mm(turned[:, :ROWS], kron).astype(BF16)
        second = mm(first[:, :ROWS], lower).astype(BF16)
        for k in range(CHI):
            second_ref[a * PAD : (a + 1) * PAD, k * LANES : (k + 1) * LANES] = second[
                k * PAD : (k + 1) * PAD, :
            ]


def third(second_ref, right, kron_ref):
    tile = one_hot(minor(iota((PAD, LANES), 1)) == iota((PAD, LANES), 0))
    values = mm(right, tile, TN)
    lane_group = group(iota((PAD, LANES), 1))
    for k in range(CHI):
        block = values[k * PAD : (k + 1) * PAD, :]
        for d in range(PAD):
            kept = jnp.where(lane_group == d, block, 0.0) if d < CHI else jnp.zeros_like(block)
            start = k * LANES + d * PAD
            kron_ref[start : start + PAD, :] = kept.astype(BF16)
    return mm(second_ref[...], kron_ref[...])


def placed(site, mirror, lower):
    spaced = mm(row_spread(lower), site).astype(BF16)
    return block_swap(mm(spaced, spread_matrix(mirror)).astype(BF16))


def pick(own_first, own, other):
    return jnp.where(own_first, own, other), jnp.where(own_first, other, own)


def cast_kernel(own, cast_o):
    cast_o[...] = own[...].astype(BF16)


def first_gram_kernel(role, own, other, first_o, second_o, gram_o):
    own_first, own_lower, mirror = role[0] != 0, role[2] != 0, role[3] != 0
    mine = placed(own[...], mirror, own_lower)
    theirs = placed(other[...].astype(BF16), mirror, jnp.logical_not(own_lower))
    first_o[...], second_o[...] = pick(own_first, mine, theirs)
    products = pick(own_first, product_part(mine), product_part(theirs))
    gram_o[...] = pack(outer_part(*products))


def own_kernel(own, wide_o, product_o):
    wide = unpack(own[...])
    wide_o[...] = wide
    product_o[...] = product_part(wide)


def gram_kernel(role, wide, product, other, first_o, second_o, gram_o):
    own_first = role[0] != 0
    theirs = unpack(other[...])
    products = pick(own_first, product[...], product_part(theirs))
    gram_o[...] = pack(outer_part(*products))
    first_o[...], second_o[...] = pick(own_first, wide[...], theirs)


def turn_kernel(level, role, first, start, turned_o, starts_o):
    turned_o[...] = turn(first[...])
    plain, turned = start_body(start[level], swap_matrix())
    first_upper = role[1] != 0
    starts_o[:PAD] = jnp.where(first_upper, plain, turned)
    starts_o[PAD:] = jnp.where(first_upper, turned, plain)


def second_kernel(turned, lower, left, second_o):
    first_second(turned[...], lower[...], left[...], second_o)


def mean_square(merged):
    total = jnp.sum(jnp.sum(merged * merged, axis=0, keepdims=True), axis=1, keepdims=True)
    return total / (CHI**4) + 1e-06


def third_kernel(second, right, log_in, next_o, log_o, kron):
    merged = third(second, right[...], kron)
    mean = mean_square(merged)
    next_o[...] = pack((merged * lax.rsqrt(mean)).astype(BF16))
    log_o[...] = log_in[...] + 0.5 * jnp.log(mean)


def last_kernel(role, second, right, log_in, coarse_o, log_o, kron):
    merged = third(second, right[...], kron)
    mean = mean_square(merged)
    log_o[...] = (log_in[...] + 0.5 * jnp.log(mean))[:1, :1]
    wide = block_swap(merged.astype(BF16))
    narrow = mm(wide, spread_matrix(role[3] != 0), NT).astype(BF16)
    coarse_o[...] = mm(row_spread(True), narrow, TN) * lax.rsqrt(mean)


def call(kernel, outs, places, scratch=()):
    return pl.pallas_call(
        kernel,
        out_shape=[jax.ShapeDtypeStruct(s, d) for s, d in outs],
        in_specs=[pl.BlockSpec(memory_space=place) for place in places],
        out_specs=[pl.BlockSpec(memory_space=pltpu.VMEM)] * len(outs),
        scratch_shapes=list(scratch),
        compiler_params=pltpu.CompilerParams(vmem_limit_bytes=VMEM_BYTES),
        cost_estimate=pl.CostEstimate(flops=10**8, bytes_accessed=10**6, transcendentals=0),
    )


def from_partner(array, flip):
    count = lax.axis_size("row")
    return lax.ppermute(array, "row", [(i, i ^ flip) for i in range(count)])


def mirrored(row):
    parity = row * 0
    for bit in range(LEVELS):
        parity = parity ^ (row >> bit & 1)
    return parity


def from_bond(array):
    rows, cols = lax.axis_size("row"), lax.axis_size("col")
    pairs = []
    for i in range(rows):
        for c in range(cols):
            target = (c + 1) % cols if mirrored(i) else (c - 1) % cols
            pairs.append((i * cols + c, (i ^ 1) * cols + target))
    return lax.ppermute(array, ("row", "col"), pairs)


def per_device(site_tensors, start_basis):
    square = CHI * CHI
    row = lax.axis_index("row")
    mirror = mirrored(row)
    vmem, smem = pltpu.VMEM, pltpu.SMEM
    mat, packed, logs = ((ROWS, LANES), BF16), ((ROWS * 3 // 2, 128), BF16), ((8, 128), F32)
    kron = [vmem((CHI * LANES, LANES), BF16)]
    log_total = jnp.zeros(*logs)
    own = site_tensors[0, 0]
    for level in range(LEVELS):
        own_lower = row >> level & 1
        first_upper = row >> level + 1 & 1 if level < LEVELS - 1 else row * 0 + 1
        role = jnp.stack([own_lower ^ first_upper, first_upper, own_lower, mirror]).astype(jnp.int32)
        if level == 0:
            other = from_partner(own, 1)
            (own,) = call(cast_kernel, [((square, square), BF16)], [vmem])(own)
            first, lower, gram = call(first_gram_kernel, [mat, mat, packed], [smem, vmem, vmem])(
                role, own, other
            )
        else:
            other = from_partner(own, 1 << level | 1)
            wide, product = call(own_kernel, [mat, mat], [vmem])(own)
            first, lower, gram = call(gram_kernel, [mat, mat, packed], [smem, vmem, vmem, vmem])(
                role, wide, product, other
            )
        gram_other = from_bond(gram)
        turned, starts = call(
            functools.partial(turn_kernel, level),
            [mat, ((2 * PAD, LANES), F32)],
            [smem, vmem, vmem],
        )(role, first, start_basis)
        (left,) = call(iso_kernel, [((PAD, LANES), BF16)], [vmem] * 3)(gram, gram_other, starts)
        right = from_partner(left, 1)
        (second,) = call(second_kernel, [((ROWS, CHI * LANES), BF16)], [vmem] * 3)(
            turned, lower, left
        )
        if level < LEVELS - 1:
            own, log_total = call(third_kernel, [packed, logs], [vmem] * 3, kron)(
                second, right, log_total
            )
        else:
            coarse, log_total = call(
                last_kernel, [((square, square), F32), ((1, 1), F32)], [smem] + [vmem] * 3, kron
            )(role, second, right, log_total)
    return (coarse[None, None], log_total)


def solution(mesh):
    return jax.shard_map(
        per_device,
        mesh=mesh,
        in_specs=(P("row", "col", None, None), P()),
        out_specs=(P("row", "col", None, None), P("row", "col")),
        check_vma=False,
    )
```

```python
import functools

import functools

import jax
import jax.numpy as jnp
from jax import lax
from jax.experimental import pallas as pl
from jax.experimental.pallas import tpu as pltpu
from jax.sharding import PartitionSpec as P

CHI = 12
LEVELS = 3
SWEEPS = 2
PAD = 16
SHIFT = 4
ROWS = CHI * PAD
LANES = PAD * PAD
VMEM_BYTES = 8 << 20
PIVOT = 1.0 / 64
F32 = jnp.float32
BF16 = jnp.bfloat16

NN = (((1,), (0,)), ((), ()))
NT = (((1,), (1,)), ((), ()))
TN = (((0,), (0,)), ((), ()))


def mm(a, b, dims=NN):
    return lax.dot_general(a, b, dims, preferred_element_type=F32)


def iota(shape, dim):
    return lax.broadcasted_iota(jnp.int32, shape, dim)


def group(index):
    return lax.shift_right_logical(index, SHIFT)


def minor(index):
    return lax.bitwise_and(index, PAD - 1)


def one_hot(mask):
    return jnp.where(mask, 1.0, 0.0).astype(BF16)


def swap_matrix(rows=LANES):
    i, j = iota((rows, LANES), 0), iota((rows, LANES), 1)
    return one_hot((group(i) == minor(j)) & (minor(i) == group(j)))


def spread_matrix(mirror):
    i, j = iota((CHI * CHI, LANES), 0), iota((CHI * CHI, LANES), 1)
    s, t = group(j), minor(j)
    source = jnp.where(mirror, t * CHI + s, s * CHI + t)
    return one_hot((i == source) & (s < CHI) & (t < CHI))


def row_spread(turn):
    i, j = iota((ROWS, CHI * CHI), 0), iota((ROWS, CHI * CHI), 1)
    s, t = group(i), minor(i)
    source = jnp.where(turn, t * CHI + s, s * CHI + t)
    return one_hot((j == source) & (t < CHI))


def block_swap(x):
    lane_group = group(iota((PAD, 128), 1))
    zero = jnp.zeros((PAD, 128), x.dtype)
    tiles = {}
    for p in range(PAD):
        for t in range(2):
            src, src_tile = (p & 7) | (t << 3), p >> 3
            if src < CHI:
                tiles[p, t] = x[src * PAD : (src + 1) * PAD, src_tile * 128 : (src_tile + 1) * 128]
            else:
                tiles[p, t] = None
    for bit in range(3):
        step = 1 << bit
        low = lax.bitwise_and(lane_group, step) == 0
        new = {}
        for p in range(PAD):
            if p & step:
                continue
            for t in range(2):
                a, b = tiles[p, t], tiles[p | step, t]
                if a is None and b is None:
                    new[p, t] = new[p | step, t] = None
                    continue
                a_moved = zero if a is None else pltpu.roll(a, 128 - step * PAD, 1)
                b_moved = zero if b is None else pltpu.roll(b, step * PAD, 1)
                a = zero if a is None else a
                b = zero if b is None else b
                new[p, t] = jnp.where(low, a, b_moved)
                new[p | step, t] = jnp.where(low, a_moved, b)
        tiles = new
    rows = []
    for p in range(CHI):
        pair = [zero if tiles[p, t] is None else tiles[p, t] for t in range(2)]
        rows.append(jnp.concatenate(pair, axis=1))
    return jnp.concatenate(rows, axis=0)


def widen(x):
    return jnp.concatenate([x, jnp.zeros((x.shape[0], LANES - x.shape[1]), x.dtype)], axis=1)


def parts3(x):
    a = x.astype(BF16)
    rest = x - a.astype(F32)
    b = rest.astype(BF16)
    c = (rest - b.astype(F32)).astype(BF16)
    return jnp.concatenate([a, b, c], axis=0)


def parts2(x):
    a = x.astype(BF16)
    return jnp.concatenate([a, (x - a.astype(F32)).astype(BF16)], axis=0)


def fold2(y):
    n = y.shape[0] // 2
    return y[n:] + y[:n]


def fold3(y):
    n = y.shape[0] // 3
    return (y[2 * n :] + y[n : 2 * n]) + y[:n]


def pack(x):
    half = ROWS // 2
    side, used = x[:, 128:], ROWS - 128
    lane = iota((half, 128), 1)
    folded = jnp.where(lane < used, side[:half], pltpu.roll(side[half:], used, 1))
    return jnp.concatenate([x[:, :128], folded], axis=0)


def unpack(x):
    half, used = ROWS // 2, ROWS - 128
    folded = x[ROWS:]
    lane = iota((half, 128), 1)
    zero = jnp.zeros((half, 128), x.dtype)
    first = jnp.where(lane < used, folded, zero)
    last = jnp.where(lane < used, pltpu.roll(folded, 128 - used, 1), zero)
    return jnp.concatenate([x[:ROWS], jnp.concatenate([first, last], axis=0)], axis=1)


def row_swap(x):
    legs = x.astype(F32).reshape(CHI, PAD, x.shape[1])[:, :CHI]
    turned = jnp.transpose(legs, (1, 0, 2))
    rest = jnp.zeros((CHI, PAD - CHI, x.shape[1]), F32)
    return jnp.concatenate([turned, rest], axis=1).reshape(x.shape).astype(BF16)


def product_part(x):
    product = mm(row_swap(x), x, NT).astype(BF16)
    return block_swap(widen(product))


def outer_part(first, second):
    outer = mm(first, row_swap(second), NT).astype(BF16)
    return block_swap(widen(outer))


def turn(first):
    return widen(row_swap(first.T[:ROWS]))


def start_body(start, swap):
    start = jnp.concatenate([start, jnp.zeros((PAD - CHI, CHI * CHI), F32)], axis=0)
    pieces = parts3(start)
    spread = spread_matrix(False)
    plain = mm(pieces, spread)
    turned = mm(plain.astype(BF16), swap)
    return fold3(plain), fold3(turned)


def orthonormal(y):
    pieces = parts2(y)
    high, low = pieces[:PAD], pieces[PAD:]
    gram = fold2(mm(pieces, high, NT)) + mm(high, low, NT)
    width = y.shape[1]
    row = iota((PAD, 128), 0)
    cols = [jnp.broadcast_to(gram[:, k : k + 1], (PAD, 128)) for k in range(CHI)]
    floors = [jnp.broadcast_to(cols[k][k : k + 1, :], (PAD, 128)) * PIVOT for k in range(CHI)]
    scale = jnp.zeros((PAD, 128), F32)
    good = jnp.ones((PAD, 128), F32)
    for k in range(CHI):
        pivot = jnp.broadcast_to(cols[k][k : k + 1, :], (PAD, 128))
        good = jnp.where(pivot >= floors[k], good, 0.0)
        inverse = lax.rsqrt(pivot)
        scale = jnp.where(row == k, inverse, scale)
        factor = jnp.where(row > k, cols[k] * (inverse * inverse), 0.0)
        for j in range(k + 1, CHI):
            cols[j] = cols[j] - factor * jnp.broadcast_to(cols[j][k : k + 1, :], (PAD, 128))
        wide = jnp.concatenate([factor] * (width // 128), axis=1)
        y = y - wide * jnp.broadcast_to(y[k : k + 1, :], (PAD, width))
    return y * jnp.concatenate([scale] * (width // 128), axis=1), good


def exact_iso(own, other, start, start_turned, shift, swap):
    pieces = parts3(start)
    image = fold3(mm(pieces, own, NT) + mm(pieces, other, NT))
    basis, _ = orthonormal(widen(image) + shift * start_turned)
    pieces = parts3(basis)
    image = fold3(mm(pieces[:, :ROWS], own) + mm(pieces[:, :ROWS], other))
    basis, _ = orthonormal(image + shift * fold3(mm(pieces, swap)))
    return basis


def iso_kernel(own, other, starts, iso_o):
    own, other = unpack(own[...]), unpack(other[...])
    start, start_turned = starts[:PAD], starts[PAD:]
    swap = swap_matrix()
    total = own.astype(F32) + other.astype(F32)
    i, j = iota((ROWS, LANES), 0), iota((ROWS, LANES), 1)
    diagonal = (group(i) == minor(j)) & (minor(i) == group(j))
    trace = jnp.sum(jnp.where(diagonal, total, 0.0), axis=0, keepdims=True)
    shift = jnp.sum(trace, axis=1, keepdims=True) / (CHI * CHI)
    unit = 1.0 / shift
    pieces = parts2(start)
    image = fold2(mm(pieces, own, NT) + mm(pieces, other, NT))
    image = widen(image) * unit + start_turned
    pieces = parts2(image)
    image = fold2(mm(pieces[:, :ROWS], own) + mm(pieces[:, :ROWS], other)) * unit
    basis, good = orthonormal(image + fold2(mm(pieces, swap)))
    iso_o[...] = basis.astype(BF16)

    @pl.when(jnp.logical_not(jnp.min(good[:1]) > 0.5))
    def _():
        iso_o[...] = exact_iso(own, other, start, start_turned, shift, swap).astype(BF16)


def first_second(turned, lower, left, second_ref):
    lane = iota((PAD, LANES), 1)
    masked = [jnp.where(group(lane) == k, left.astype(F32), 0.0) for k in range(CHI)]
    masked = jnp.concatenate(masked, axis=0).astype(BF16)
    i, j = iota((LANES, LANES), 0), iota((LANES, LANES), 1)
    values = mm(masked, one_hot(minor(i) == group(j)))
    eye = minor(lane) == iota((PAD, LANES), 0)
    for a in range(CHI):
        blocks = []
        for k in range(CHI):
            line = jnp.broadcast_to(values[k * PAD + a : k * PAD + a + 1, :], (PAD, LANES))
            blocks.append(jnp.where(eye, line, 0.0).astype(BF16))
        kron = jnp.concatenate(blocks, axis=0)
        first = mm(turned[:, :ROWS], kron).astype(BF16)
        second = mm(first[:, :ROWS], lower).astype(BF16)
        for k in range(CHI):
            second_ref[a * PAD : (a + 1) * PAD, k * LANES : (k + 1) * LANES] = second[
                k * PAD : (k + 1) * PAD, :
            ]


def third(second_ref, right, kron_ref):
    tile = one_hot(minor(iota((PAD, LANES), 1)) == iota((PAD, LANES), 0))
    values = mm(right, tile, TN)
    lane_group = group(iota((PAD, LANES), 1))
    for k in range(CHI):
        block = values[k * PAD : (k + 1) * PAD, :]
        for d in range(PAD):
            kept = jnp.where(lane_group == d, block, 0.0) if d < CHI else jnp.zeros_like(block)
            start = k * LANES + d * PAD
            kron_ref[start : start + PAD, :] = kept.astype(BF16)
    return mm(second_ref[...], kron_ref[...])


def placed(site, mirror, lower):
    spaced = mm(row_spread(lower), site).astype(BF16)
    return block_swap(mm(spaced, spread_matrix(mirror)).astype(BF16))


def pick(own_first, own, other):
    return jnp.where(own_first, own, other), jnp.where(own_first, other, own)


def roles(level):
    row = lax.axis_index("row")
    own_lower = row >> level & 1
    first_upper = row >> level + 1 & 1 if level < LEVELS - 1 else row * 0 + 1
    flags = own_lower ^ first_upper, first_upper, own_lower, mirrored(row)
    return [flag != 0 for flag in flags]


def cast_kernel(own, cast_o):
    cast_o[...] = own[...].astype(BF16)


def first_gram_kernel(own, other, first_o, second_o, gram_o):
    own_first, _, own_lower, mirror = roles(0)
    mine = placed(own[...], mirror, own_lower)
    theirs = placed(other[...].astype(BF16), mirror, jnp.logical_not(own_lower))
    first_o[...], second_o[...] = pick(own_first, mine, theirs)
    products = pick(own_first, product_part(mine), product_part(theirs))
    gram_o[...] = pack(outer_part(*products))


def own_kernel(own, wide_o, product_o):
    wide = unpack(own[...])
    wide_o[...] = wide
    product_o[...] = product_part(wide)


def gram_kernel(level, wide, product, other, first_o, second_o, gram_o):
    own_first = roles(level)[0]
    theirs = unpack(other[...])
    products = pick(own_first, product[...], product_part(theirs))
    gram_o[...] = pack(outer_part(*products))
    first_o[...], second_o[...] = pick(own_first, wide[...], theirs)


def turn_kernel(level, first, start, turned_o, starts_o):
    turned_o[...] = turn(first[...])
    plain, turned = start_body(start[level], swap_matrix())
    first_upper = roles(level)[1]
    starts_o[:PAD] = jnp.where(first_upper, plain, turned)
    starts_o[PAD:] = jnp.where(first_upper, turned, plain)


def second_kernel(turned, lower, left, second_o):
    first_second(turned[...], lower[...], left[...], second_o)


def mean_square(merged):
    total = jnp.sum(jnp.sum(merged * merged, axis=0, keepdims=True), axis=1, keepdims=True)
    return total / (CHI**4) + 1e-06


def third_kernel(second, right, log_in, next_o, log_o, kron):
    merged = third(second, right[...], kron)
    mean = mean_square(merged)
    next_o[...] = pack((merged * lax.rsqrt(mean)).astype(BF16))
    log_o[...] = log_in[...] + 0.5 * jnp.log(mean)


def last_kernel(second, right, log_in, coarse_o, log_o, kron):
    merged = third(second, right[...], kron)
    mean = mean_square(merged)
    log_o[...] = (log_in[...] + 0.5 * jnp.log(mean))[:1, :1]
    wide = block_swap(merged.astype(BF16))
    narrow = mm(wide, spread_matrix(roles(LEVELS - 1)[3]), NT).astype(BF16)
    coarse_o[...] = mm(row_spread(True), narrow, TN) * lax.rsqrt(mean)


def call(kernel, outs, scratch=()):
    vmem = pl.BlockSpec(memory_space=pltpu.VMEM)

    def run(*args):
        return pl.pallas_call(
            kernel,
            out_shape=[jax.ShapeDtypeStruct(s, d) for s, d in outs],
            in_specs=[vmem] * len(args),
            out_specs=[vmem] * len(outs),
            scratch_shapes=list(scratch),
            compiler_params=pltpu.CompilerParams(vmem_limit_bytes=VMEM_BYTES),
            cost_estimate=pl.CostEstimate(flops=10**8, bytes_accessed=10**6, transcendentals=0),
        )(*args)

    return run


def from_partner(array, flip):
    count = lax.axis_size("row")
    return lax.ppermute(array, "row", [(i, i ^ flip) for i in range(count)])


def mirrored(row):
    parity = row * 0
    for bit in range(LEVELS):
        parity = parity ^ (row >> bit & 1)
    return parity


def from_bond(array):
    rows, cols = lax.axis_size("row"), lax.axis_size("col")
    pairs = []
    for i in range(rows):
        for c in range(cols):
            target = (c + 1) % cols if mirrored(i) else (c - 1) % cols
            pairs.append((i * cols + c, (i ^ 1) * cols + target))
    return lax.ppermute(array, ("row", "col"), pairs)


def per_device(site_tensors, start_basis):
    square = CHI * CHI
    mat, packed, logs = ((ROWS, LANES), BF16), ((ROWS * 3 // 2, 128), BF16), ((8, 128), F32)
    kron = [pltpu.VMEM((CHI * LANES, LANES), BF16)]
    log_total = jnp.zeros(*logs)
    own = site_tensors[0, 0]
    for level in range(LEVELS):
        if level == 0:
            other = from_partner(own, 1)
            (own,) = call(cast_kernel, [((square, square), BF16)])(own)
            first, lower, gram = call(first_gram_kernel, [mat, mat, packed])(own, other)
        else:
            other = from_partner(own, 1 << level | 1)
            wide, product = call(own_kernel, [mat, mat])(own)
            first, lower, gram = call(
                functools.partial(gram_kernel, level), [mat, mat, packed]
            )(wide, product, other)
        gram_other = from_bond(gram)
        turned, starts = call(
            functools.partial(turn_kernel, level), [mat, ((2 * PAD, LANES), F32)]
        )(first, start_basis)
        (left,) = call(iso_kernel, [((PAD, LANES), BF16)])(gram, gram_other, starts)
        right = from_partner(left, 1)
        (second,) = call(second_kernel, [((ROWS, CHI * LANES), BF16)])(turned, lower, left)
        if level < LEVELS - 1:
            own, log_total = call(third_kernel, [packed, logs], kron)(second, right, log_total)
        else:
            coarse, log_total = call(last_kernel, [((square, square), F32), ((1, 1), F32)], kron)(
                second, right, log_total
            )
    return (coarse[None, None], log_total)


def solution(mesh):
    return jax.shard_map(
        per_device,
        mesh=mesh,
        in_specs=(P("row", "col", None, None), P()),
        out_specs=(P("row", "col", None, None), P("row", "col")),
        check_vma=False,
    )
```

```python
import functools

import functools

import jax
import jax.numpy as jnp
from jax import lax
from jax.experimental import pallas as pl
from jax.experimental.pallas import tpu as pltpu
from jax.sharding import PartitionSpec as P

CHI = 12
LEVELS = 3
SWEEPS = 2
PAD = 16
SHIFT = 4
ROWS = CHI * PAD
LANES = PAD * PAD
VMEM_BYTES = 8 << 20
SECOND = (CHI + 2) * 128
PIVOT = 1.0 / 64
F32 = jnp.float32
BF16 = jnp.bfloat16

NN = (((1,), (0,)), ((), ()))
NT = (((1,), (1,)), ((), ()))
TN = (((0,), (0,)), ((), ()))


def mm(a, b, dims=NN):
    return lax.dot_general(a, b, dims, preferred_element_type=F32)


def iota(shape, dim):
    return lax.broadcasted_iota(jnp.int32, shape, dim)


def group(index):
    return lax.shift_right_logical(index, SHIFT)


def minor(index):
    return lax.bitwise_and(index, PAD - 1)


def one_hot(mask):
    return jnp.where(mask, 1.0, 0.0).astype(BF16)


def swap_matrix(rows=LANES):
    i, j = iota((rows, LANES), 0), iota((rows, LANES), 1)
    return one_hot((group(i) == minor(j)) & (minor(i) == group(j)))


def spread_matrix(mirror):
    i, j = iota((CHI * CHI, LANES), 0), iota((CHI * CHI, LANES), 1)
    s, t = group(j), minor(j)
    source = jnp.where(mirror, t * CHI + s, s * CHI + t)
    return one_hot((i == source) & (s < CHI) & (t < CHI))


def row_spread(turn):
    i, j = iota((ROWS, CHI * CHI), 0), iota((ROWS, CHI * CHI), 1)
    s, t = group(i), minor(i)
    source = jnp.where(turn, t * CHI + s, s * CHI + t)
    return one_hot((j == source) & (t < CHI))


def block_swap(x):
    lane_group = group(iota((PAD, 128), 1))
    zero = jnp.zeros((PAD, 128), x.dtype)
    tiles = {}
    for p in range(PAD):
        for t in range(2):
            src, src_tile = (p & 7) | (t << 3), p >> 3
            if src < CHI:
                tiles[p, t] = x[src * PAD : (src + 1) * PAD, src_tile * 128 : (src_tile + 1) * 128]
            else:
                tiles[p, t] = None
    for bit in range(3):
        step = 1 << bit
        low = lax.bitwise_and(lane_group, step) == 0
        new = {}
        for p in range(PAD):
            if p & step:
                continue
            for t in range(2):
                a, b = tiles[p, t], tiles[p | step, t]
                if a is None and b is None:
                    new[p, t] = new[p | step, t] = None
                    continue
                a_moved = zero if a is None else pltpu.roll(a, 128 - step * PAD, 1)
                b_moved = zero if b is None else pltpu.roll(b, step * PAD, 1)
                a = zero if a is None else a
                b = zero if b is None else b
                new[p, t] = jnp.where(low, a, b_moved)
                new[p | step, t] = jnp.where(low, a_moved, b)
        tiles = new
    rows = []
    for p in range(CHI):
        pair = [zero if tiles[p, t] is None else tiles[p, t] for t in range(2)]
        rows.append(jnp.concatenate(pair, axis=1))
    return jnp.concatenate(rows, axis=0)


def widen(x):
    return jnp.concatenate([x, jnp.zeros((x.shape[0], LANES - x.shape[1]), x.dtype)], axis=1)


def parts3(x):
    a = x.astype(BF16)
    rest = x - a.astype(F32)
    b = rest.astype(BF16)
    c = (rest - b.astype(F32)).astype(BF16)
    return jnp.concatenate([a, b, c], axis=0)


def parts2(x):
    a = x.astype(BF16)
    return jnp.concatenate([a, (x - a.astype(F32)).astype(BF16)], axis=0)


def fold2(y):
    n = y.shape[0] // 2
    return y[n:] + y[:n]


def fold3(y):
    n = y.shape[0] // 3
    return (y[2 * n :] + y[n : 2 * n]) + y[:n]


def pack(x):
    half = ROWS // 2
    side, used = x[:, 128:], ROWS - 128
    lane = iota((half, 128), 1)
    folded = jnp.where(lane < used, side[:half], pltpu.roll(side[half:], used, 1))
    return jnp.concatenate([x[:, :128], folded], axis=0)


def unpack(x):
    half, used = ROWS // 2, ROWS - 128
    folded = x[ROWS:]
    lane = iota((half, 128), 1)
    zero = jnp.zeros((half, 128), x.dtype)
    first = jnp.where(lane < used, folded, zero)
    last = jnp.where(lane < used, pltpu.roll(folded, 128 - used, 1), zero)
    return jnp.concatenate([x[:ROWS], jnp.concatenate([first, last], axis=0)], axis=1)


def row_swap(x):
    legs = x.astype(F32).reshape(CHI, PAD, x.shape[1])[:, :CHI]
    turned = jnp.transpose(legs, (1, 0, 2))
    rest = jnp.zeros((CHI, PAD - CHI, x.shape[1]), F32)
    return jnp.concatenate([turned, rest], axis=1).reshape(x.shape).astype(BF16)


def product_part(x):
    product = mm(row_swap(x), x, NT).astype(BF16)
    return block_swap(widen(product))


def outer_part(first, second):
    outer = mm(first, row_swap(second), NT).astype(BF16)
    return block_swap(widen(outer))


def turn(first):
    return widen(row_swap(first.T[:ROWS]))


def start_body(start, swap):
    start = jnp.concatenate([start, jnp.zeros((PAD - CHI, CHI * CHI), F32)], axis=0)
    pieces = parts3(start)
    spread = spread_matrix(False)
    plain = mm(pieces, spread)
    turned = mm(plain.astype(BF16), swap)
    return fold3(plain), fold3(turned)


def orthonormal(y):
    pieces = parts2(y)
    high, low = pieces[:PAD], pieces[PAD:]
    gram = fold2(mm(pieces, high, NT)) + mm(high, low, NT)
    width = y.shape[1]
    row = iota((PAD, 128), 0)
    cols = [jnp.broadcast_to(gram[:, k : k + 1], (PAD, 128)) for k in range(CHI)]
    floors = [jnp.broadcast_to(cols[k][k : k + 1, :], (PAD, 128)) * PIVOT for k in range(CHI)]
    scale = jnp.zeros((PAD, 128), F32)
    good = jnp.ones((PAD, 128), F32)
    for k in range(CHI):
        pivot = jnp.broadcast_to(cols[k][k : k + 1, :], (PAD, 128))
        good = jnp.where(pivot >= floors[k], good, 0.0)
        inverse = lax.rsqrt(pivot)
        scale = jnp.where(row == k, inverse, scale)
        factor = jnp.where(row > k, cols[k] * (inverse * inverse), 0.0)
        for j in range(k + 1, CHI):
            cols[j] = cols[j] - factor * jnp.broadcast_to(cols[j][k : k + 1, :], (PAD, 128))
        wide = jnp.concatenate([factor] * (width // 128), axis=1)
        y = y - wide * jnp.broadcast_to(y[k : k + 1, :], (PAD, width))
    return y * jnp.concatenate([scale] * (width // 128), axis=1), good


def exact_iso(own, other, start, start_turned, shift, swap):
    pieces = parts3(start)
    image = fold3(mm(pieces, own, NT) + mm(pieces, other, NT))
    basis, _ = orthonormal(widen(image) + shift * start_turned)
    pieces = parts3(basis)
    image = fold3(mm(pieces[:, :ROWS], own) + mm(pieces[:, :ROWS], other))
    basis, _ = orthonormal(image + shift * fold3(mm(pieces, swap)))
    return basis


def iso_kernel(own, other, starts, iso_o):
    own, other = unpack(own[...]), unpack(other[...])
    start, start_turned = starts[:PAD], starts[PAD:]
    swap = swap_matrix()
    total = own.astype(F32) + other.astype(F32)
    i, j = iota((ROWS, LANES), 0), iota((ROWS, LANES), 1)
    diagonal = (group(i) == minor(j)) & (minor(i) == group(j))
    trace = jnp.sum(jnp.where(diagonal, total, 0.0), axis=0, keepdims=True)
    shift = jnp.sum(trace, axis=1, keepdims=True) / (CHI * CHI)
    unit = 1.0 / shift
    pieces = parts2(start)
    image = fold2(mm(pieces, own, NT) + mm(pieces, other, NT))
    image = widen(image) * unit + start_turned
    pieces = parts2(image)
    image = fold2(mm(pieces[:, :ROWS], own) + mm(pieces[:, :ROWS], other)) * unit
    basis, good = orthonormal(image + fold2(mm(pieces, swap)))
    iso_o[...] = basis.astype(BF16)

    @pl.when(jnp.logical_not(jnp.min(good[:1]) > 0.5))
    def _():
        iso_o[...] = exact_iso(own, other, start, start_turned, shift, swap).astype(BF16)


def packed_pair(index):
    entry = jnp.where(index < 128, index, 128 + minor(index))
    s = lax.shift_right_logical(entry * 171, 11)
    return s, entry - s * CHI


def packing():
    s, t = packed_pair(iota((LANES, ROWS), 0))
    j = iota((LANES, ROWS), 1)
    return one_hot((group(j) == s) & (minor(j) == t))


def first_second(turned, lower, left, second_ref):
    lane = iota((PAD, LANES), 1)
    masked = [jnp.where(group(lane) == k, left.astype(F32), 0.0) for k in range(CHI)]
    masked = jnp.concatenate(masked, axis=0).astype(BF16)
    i, j = iota((LANES, LANES), 0), iota((LANES, LANES), 1)
    values = mm(masked, one_hot(minor(i) == packed_pair(j)[0]))
    eye = packed_pair(lane)[1] == iota((PAD, LANES), 0)
    lane_group = group(iota((PAD, 128), 1))
    turned = turned[:, :ROWS]

    def line(k, a, side):
        at = k * PAD + a
        return jnp.broadcast_to(values[at : at + 1, side * 128 : side * 128 + 128], (PAD, 128))

    rests = []
    for k in range(CHI):
        pair = []
        for side in range(2):
            rest = jnp.zeros((PAD, 128), F32)
            for a in range(side * 8, min(side * 8 + 8, CHI)):
                rest = jnp.where(lane_group == a - side * 8, line(k, a, 1), rest)
            pair.append(jnp.where(eye[:, 128:], rest, 0.0).astype(BF16))
        rests.append(jnp.concatenate(pair, axis=1))
    rest = mm(turned, jnp.concatenate(rests, axis=0)).astype(BF16)
    row_group = group(iota((ROWS, 128), 1))
    zero = jnp.zeros((PAD, 128), BF16)
    for half in range(CHI // 2):
        blocks = []
        for k in range(CHI):
            pair = [
                jnp.where(eye[:, :128], line(k, a, 0), 0.0).astype(BF16)
                for a in (2 * half, 2 * half + 1)
            ]
            blocks.append(jnp.concatenate(pair, axis=1))
        both = mm(turned, jnp.concatenate(blocks, axis=0)).astype(BF16)
        for a in (2 * half, 2 * half + 1):
            tail = rest[:, (a >> 3) * 128 : (a >> 3) * 128 + 128]
            tail = jnp.where(row_group == (a & 7), tail, jnp.zeros_like(tail))
            head = both[:, (a & 1) * 128 : (a & 1) * 128 + 128]
            second = mm(jnp.concatenate([head, tail], axis=1), lower).astype(BF16)
            rows = slice(a * PAD, (a + 1) * PAD)
            tails = [zero, zero]
            for k in range(CHI):
                block = second[k * PAD : (k + 1) * PAD]
                second_ref[rows, k * 128 : (k + 1) * 128] = block[:, :128]
                tails[k >> 3] = jnp.where(lane_group == (k & 7), block[:, 128:], tails[k >> 3])
            for side in range(2):
                at = (CHI + side) * 128
                second_ref[rows, at : at + 128] = tails[side]


def third(second_ref, right, kron_ref):
    tile = one_hot(minor(iota((PAD, LANES), 1)) == iota((PAD, LANES), 0))
    values = mm(right, tile, TN)
    lane_group = group(iota((CHI * CHI, LANES), 1))
    entry = iota((CHI * CHI, LANES), 0)
    kept = lax.shift_right_logical(entry * 171, 11) == lane_group
    for k in range(CHI):
        block = values[k * PAD : k * PAD + CHI, :]
        tall = jnp.concatenate([block] * CHI, axis=0)
        tall = jnp.where(kept, tall, 0.0).astype(BF16)
        kron_ref[k * 128 : (k + 1) * 128, :] = tall[:128]
        at = CHI * 128 + k * PAD
        kron_ref[at : at + PAD, :] = tall[128:]
    used = CHI * 128 + CHI * PAD
    kron_ref[used:, :] = jnp.zeros((SECOND - used, LANES), BF16)
    return mm(second_ref[...], kron_ref[...])


def placed(site, mirror, lower):
    spaced = mm(row_spread(lower), site).astype(BF16)
    return block_swap(mm(spaced, spread_matrix(mirror)).astype(BF16))


def pick(own_first, own, other):
    return jnp.where(own_first, own, other), jnp.where(own_first, other, own)


def roles(level):
    row = lax.axis_index("row")
    own_lower = row >> level & 1
    first_upper = row >> level + 1 & 1 if level < LEVELS - 1 else row * 0 + 1
    flags = own_lower ^ first_upper, first_upper, own_lower, mirrored(row)
    return [flag != 0 for flag in flags]


def cast_kernel(own, cast_o):
    cast_o[...] = own[...].astype(BF16)


def first_gram_kernel(own, other, first_o, second_o, gram_o):
    own_first, _, own_lower, mirror = roles(0)
    mine = placed(own[...], mirror, own_lower)
    theirs = placed(other[...].astype(BF16), mirror, jnp.logical_not(own_lower))
    first_o[...], second_o[...] = pick(own_first, mine, theirs)
    products = pick(own_first, product_part(mine), product_part(theirs))
    gram_o[...] = pack(outer_part(*products))


def own_kernel(own, wide_o, product_o):
    wide = unpack(own[...])
    wide_o[...] = wide
    product_o[...] = product_part(wide)


def gram_kernel(level, wide, product, other, first_o, second_o, gram_o):
    own_first = roles(level)[0]
    theirs = unpack(other[...])
    products = pick(own_first, product[...], product_part(theirs))
    gram_o[...] = pack(outer_part(*products))
    first_o[...], second_o[...] = pick(own_first, wide[...], theirs)


def turn_kernel(level, first, second, start, turned_o, lower_o, starts_o):
    turned_o[...] = turn(first[...])
    packer = packing()
    lower = mm(packer, second[...]).astype(BF16)
    lower_o[...] = mm(lower[:, :ROWS], packer, NT).astype(BF16)
    plain, turned = start_body(start[level], swap_matrix())
    first_upper = roles(level)[1]
    starts_o[:PAD] = jnp.where(first_upper, plain, turned)
    starts_o[PAD:] = jnp.where(first_upper, turned, plain)


def second_kernel(turned, lower, left, second_o):
    first_second(turned[...], lower[...], left[...], second_o)


def mean_square(merged):
    total = jnp.sum(jnp.sum(merged * merged, axis=0, keepdims=True), axis=1, keepdims=True)
    return total / (CHI**4) + 1e-06


def third_kernel(second, right, log_in, next_o, log_o, kron):
    merged = third(second, right[...], kron)
    mean = mean_square(merged)
    next_o[...] = pack((merged * lax.rsqrt(mean)).astype(BF16))
    log_o[...] = log_in[...] + 0.5 * jnp.log(mean)


def last_kernel(second, right, log_in, coarse_o, log_o, kron):
    merged = third(second, right[...], kron)
    mean = mean_square(merged)
    log_o[...] = (log_in[...] + 0.5 * jnp.log(mean))[:1, :1]
    wide = block_swap(merged.astype(BF16))
    narrow = mm(wide, spread_matrix(roles(LEVELS - 1)[3]), NT).astype(BF16)
    coarse_o[...] = mm(row_spread(True), narrow, TN) * lax.rsqrt(mean)


def call(kernel, outs, scratch=()):
    vmem = pl.BlockSpec(memory_space=pltpu.VMEM)

    def run(*args):
        return pl.pallas_call(
            kernel,
            out_shape=[jax.ShapeDtypeStruct(s, d) for s, d in outs],
            in_specs=[vmem] * len(args),
            out_specs=[vmem] * len(outs),
            scratch_shapes=list(scratch),
            compiler_params=pltpu.CompilerParams(vmem_limit_bytes=VMEM_BYTES),
            cost_estimate=pl.CostEstimate(flops=10**8, bytes_accessed=10**6, transcendentals=0),
        )(*args)

    return run


def from_partner(array, flip):
    count = lax.axis_size("row")
    return lax.ppermute(array, "row", [(i, i ^ flip) for i in range(count)])


def mirrored(row):
    parity = row * 0
    for bit in range(LEVELS):
        parity = parity ^ (row >> bit & 1)
    return parity


def from_bond(array):
    rows, cols = lax.axis_size("row"), lax.axis_size("col")
    pairs = []
    for i in range(rows):
        for c in range(cols):
            target = (c + 1) % cols if mirrored(i) else (c - 1) % cols
            pairs.append((i * cols + c, (i ^ 1) * cols + target))
    return lax.ppermute(array, ("row", "col"), pairs)


def per_device(site_tensors, start_basis):
    square = CHI * CHI
    mat, packed, logs = ((ROWS, LANES), BF16), ((ROWS * 3 // 2, 128), BF16), ((8, 128), F32)
    square_mat = ((LANES, LANES), BF16)
    kron = [pltpu.VMEM((SECOND, LANES), BF16)]
    log_total = jnp.zeros(*logs)
    own = site_tensors[0, 0]
    for level in range(LEVELS):
        if level == 0:
            other = from_partner(own, 1)
            (own,) = call(cast_kernel, [((square, square), BF16)])(own)
            first, lower, gram = call(first_gram_kernel, [mat, mat, packed])(own, other)
        else:
            other = from_partner(own, 1 << level | 1)
            wide, product = call(own_kernel, [mat, mat])(own)
            first, lower, gram = call(
                functools.partial(gram_kernel, level), [mat, mat, packed]
            )(wide, product, other)
        gram_other = from_bond(gram)
        turned, lower, starts = call(
            functools.partial(turn_kernel, level), [mat, square_mat, ((2 * PAD, LANES), F32)]
        )(first, lower, start_basis)
        (left,) = call(iso_kernel, [((PAD, LANES), BF16)])(gram, gram_other, starts)
        right = from_partner(left, 1)
        (second,) = call(second_kernel, [((ROWS, SECOND), BF16)])(turned, lower, left)
        if level < LEVELS - 1:
            own, log_total = call(third_kernel, [packed, logs], kron)(second, right, log_total)
        else:
            coarse, log_total = call(last_kernel, [((square, square), F32), ((1, 1), F32)], kron)(
                second, right, log_total
            )
    return (coarse[None, None], log_total)


def solution(mesh):
    return jax.shard_map(
        per_device,
        mesh=mesh,
        in_specs=(P("row", "col", None, None), P()),
        out_specs=(P("row", "col", None, None), P("row", "col")),
        check_vma=False,
    )
```

```python
import functools

import functools

import jax
import jax.numpy as jnp
from jax import lax
from jax.experimental import pallas as pl
from jax.experimental.pallas import tpu as pltpu
from jax.sharding import PartitionSpec as P

CHI = 12
LEVELS = 3
SWEEPS = 2
PAD = 16
SHIFT = 4
ROWS = CHI * PAD
LANES = PAD * PAD
VMEM_BYTES = 8 << 20
SECOND = (CHI + 2) * 128
FOLD = 64
PIVOT = 1.0 / 64
F32 = jnp.float32
BF16 = jnp.bfloat16

NN = (((1,), (0,)), ((), ()))
NT = (((1,), (1,)), ((), ()))
TN = (((0,), (0,)), ((), ()))


def mm(a, b, dims=NN):
    return lax.dot_general(a, b, dims, preferred_element_type=F32)


def iota(shape, dim):
    return lax.broadcasted_iota(jnp.int32, shape, dim)


def group(index):
    return lax.shift_right_logical(index, SHIFT)


def minor(index):
    return lax.bitwise_and(index, PAD - 1)


def one_hot(mask):
    return jnp.where(mask, 1.0, 0.0).astype(BF16)


def swap_matrix(rows=LANES):
    i, j = iota((rows, LANES), 0), iota((rows, LANES), 1)
    return one_hot((group(i) == minor(j)) & (minor(i) == group(j)))


def spread_matrix(mirror):
    i, j = iota((CHI * CHI, LANES), 0), iota((CHI * CHI, LANES), 1)
    s, t = group(j), minor(j)
    source = jnp.where(mirror, t * CHI + s, s * CHI + t)
    return one_hot((i == source) & (s < CHI) & (t < CHI))


def row_spread(turn):
    i, j = iota((ROWS, CHI * CHI), 0), iota((ROWS, CHI * CHI), 1)
    s, t = group(i), minor(i)
    source = jnp.where(turn, t * CHI + s, s * CHI + t)
    return one_hot((j == source) & (t < CHI))


def swapped_tiles(x, fold):
    lane_group = group(iota((PAD, 128), 1))
    zero = jnp.zeros((PAD, 128), x.dtype)
    tiles = []
    for s in range(CHI):
        pair = []
        for side in range(2):
            lift = FOLD // PAD if fold and side and s >= CHI // 2 else 0
            tile = zero
            for p in range(side * 8, min(side * 8 + 8, CHI)):
                at = (s >> 3) * 128
                piece = x[p * PAD : (p + 1) * PAD, at : at + 128]
                shift = (p + lift - s) % 8 * PAD
                piece = pltpu.roll(piece, shift, 1) if shift else piece
                tile = jnp.where(lane_group == (p & 7) + lift, piece, tile)
            pair.append(tile)
        tiles.append(pair)
    return tiles


def block_swap(x):
    return jnp.concatenate([jnp.concatenate(pair, axis=1) for pair in swapped_tiles(x, False)], axis=0)


def widen(x):
    return jnp.concatenate([x, jnp.zeros((x.shape[0], LANES - x.shape[1]), x.dtype)], axis=1)


def parts3(x):
    a = x.astype(BF16)
    rest = x - a.astype(F32)
    b = rest.astype(BF16)
    c = (rest - b.astype(F32)).astype(BF16)
    return jnp.concatenate([a, b, c], axis=0)


def parts2(x):
    a = x.astype(BF16)
    return jnp.concatenate([a, (x - a.astype(F32)).astype(BF16)], axis=0)


def fold2(y):
    n = y.shape[0] // 2
    return y[n:] + y[:n]


def fold3(y):
    n = y.shape[0] // 3
    return (y[2 * n :] + y[n : 2 * n]) + y[:n]


def folded(first, last):
    return jnp.where(iota(first.shape, 1) < FOLD, first, last)


def compact(x):
    blocks = x.shape[0] // PAD
    legs = x.astype(F32).reshape(blocks, PAD, 128)[:, :CHI]
    return legs.reshape(blocks * CHI, 128).astype(BF16)


def spaced(x):
    blocks = x.shape[0] // CHI
    legs = x.astype(F32).reshape(blocks, CHI, 128)
    rest = jnp.zeros((blocks, PAD - CHI, 128), F32)
    return jnp.concatenate([legs, rest], axis=1).reshape(blocks * PAD, 128).astype(BF16)


def unfold(x):
    side = x[ROWS:]
    low = iota(side.shape, 1) < FOLD
    zero = jnp.zeros_like(side)
    first = jnp.where(low, side, zero)
    last = jnp.where(low, pltpu.roll(side, 128 - FOLD, 1), zero)
    return jnp.concatenate([x[:ROWS], jnp.concatenate([first, last], axis=0)], axis=1)


def row_swap(x):
    legs = x.astype(F32).reshape(CHI, PAD, x.shape[1])[:, :CHI]
    turned = jnp.transpose(legs, (1, 0, 2))
    rest = jnp.zeros((CHI, PAD - CHI, x.shape[1]), F32)
    return jnp.concatenate([turned, rest], axis=1).reshape(x.shape).astype(BF16)


def product_part(x):
    product = mm(row_swap(x), x, NT).astype(BF16)
    return block_swap(widen(product))


def outer_part(first, second):
    outer = mm(first, row_swap(second), NT).astype(BF16)
    tiles = swapped_tiles(widen(outer), True)
    half = CHI // 2
    side = folded(*(jnp.concatenate([t[1] for t in part], axis=0) for part in (tiles[:half], tiles[half:])))
    return compact(jnp.concatenate([t[0] for t in tiles] + [side], axis=0))


def turn(first):
    return widen(row_swap(first.T[:ROWS]))


def start_body(start, swap):
    start = jnp.concatenate([start, jnp.zeros((PAD - CHI, CHI * CHI), F32)], axis=0)
    pieces = parts3(start)
    spread = spread_matrix(False)
    plain = mm(pieces, spread)
    turned = mm(plain.astype(BF16), swap)
    return fold3(plain), fold3(turned)


def orthonormal(y):
    pieces = parts2(y)
    high, low = pieces[:PAD], pieces[PAD:]
    gram = fold2(mm(pieces, high, NT)) + mm(high, low, NT)
    width = y.shape[1]
    row = iota((PAD, 128), 0)
    cols = [jnp.broadcast_to(gram[:, k : k + 1], (PAD, 128)) for k in range(CHI)]
    floors = [jnp.broadcast_to(cols[k][k : k + 1, :], (PAD, 128)) * PIVOT for k in range(CHI)]
    scale = jnp.zeros((PAD, 128), F32)
    good = jnp.ones((PAD, 128), F32)
    for k in range(CHI):
        pivot = jnp.broadcast_to(cols[k][k : k + 1, :], (PAD, 128))
        good = jnp.where(pivot >= floors[k], good, 0.0)
        inverse = lax.rsqrt(pivot)
        scale = jnp.where(row == k, inverse, scale)
        factor = jnp.where(row > k, cols[k] * (inverse * inverse), 0.0)
        for j in range(k + 1, CHI):
            cols[j] = cols[j] - factor * jnp.broadcast_to(cols[j][k : k + 1, :], (PAD, 128))
        wide = jnp.concatenate([factor] * (width // 128), axis=1)
        y = y - wide * jnp.broadcast_to(y[k : k + 1, :], (PAD, width))
    return y * jnp.concatenate([scale] * (width // 128), axis=1), good


def exact_iso(own, other, start, start_turned, shift, swap):
    pieces = parts3(start)
    image = fold3(mm(pieces, own, NT) + mm(pieces, other, NT))
    basis, _ = orthonormal(widen(image) + shift * start_turned)
    pieces = parts3(basis)
    image = fold3(mm(pieces[:, :ROWS], own) + mm(pieces[:, :ROWS], other))
    basis, _ = orthonormal(image + shift * fold3(mm(pieces, swap)))
    return basis


def iso_kernel(own, other, starts, pieces, iso_o):
    swap = swap_matrix()
    grams = [spaced(own[...]), spaced(other[...])]
    doubled = [
        jnp.concatenate([g[:ROWS], jnp.concatenate([g[ROWS:]] * 2, axis=0)], axis=1) for g in grams
    ]
    total = doubled[0].astype(F32) + doubled[1].astype(F32)
    i, j = iota((ROWS, LANES), 0), iota((ROWS, LANES), 1)
    place = jnp.where(j < 128, j, 128 + lax.bitwise_and(j, FOLD - 1))
    valid = (j < 128) | ((lax.bitwise_and(j, 127) < FOLD) == (i < ROWS // 2))
    diagonal = valid & (group(i) == minor(place)) & (minor(i) == group(place))
    trace = jnp.sum(jnp.where(diagonal, total, 0.0), axis=0, keepdims=True)
    shift = jnp.sum(trace, axis=1, keepdims=True) / (CHI * CHI)
    unit = 1.0 / shift
    image = mm(pieces[...], doubled[0], NT) + mm(pieces[...], doubled[1], NT)
    lane = iota((2 * PAD, ROWS), 1)
    image = jnp.where(lane < ROWS // 2, image[: 2 * PAD], image[2 * PAD :])
    image = widen(fold2(image)) * unit + starts[PAD:]
    parts = parts2(image)
    own, other = unfold(grams[0]), unfold(grams[1])
    image = fold2(mm(parts[:, :ROWS], own) + mm(parts[:, :ROWS], other)) * unit
    basis, good = orthonormal(image + fold2(mm(parts, swap)))
    iso_o[...] = basis.astype(BF16)

    @pl.when(jnp.logical_not(jnp.min(good[:1]) > 0.5))
    def _():
        basis = exact_iso(own, other, starts[:PAD], starts[PAD:], shift, swap)
        iso_o[...] = basis.astype(BF16)


def packed_pair(index):
    entry = jnp.where(index < 128, index, 128 + minor(index))
    s = lax.shift_right_logical(entry * 171, 11)
    return s, entry - s * CHI


def packing():
    s, t = packed_pair(iota((LANES, ROWS), 0))
    j = iota((LANES, ROWS), 1)
    return one_hot((group(j) == s) & (minor(j) == t))


def first_second(turned, lower, left, second_ref, first_ref):
    lane = iota((PAD, LANES), 1)
    masked = [jnp.where(group(lane) == k, left.astype(F32), 0.0) for k in range(CHI)]
    masked = jnp.concatenate(masked, axis=0).astype(BF16)
    i, j = iota((LANES, LANES), 0), iota((LANES, LANES), 1)
    values = mm(masked, one_hot(minor(i) == group(j)))
    eye = minor(lane) == iota((PAD, LANES), 0)
    for a in range(CHI):
        blocks = []
        for k in range(CHI):
            line = jnp.broadcast_to(values[k * PAD + a : k * PAD + a + 1, :], (PAD, LANES))
            blocks.append(jnp.where(eye, line, 0.0).astype(BF16))
        kron = jnp.concatenate(blocks, axis=0)
        first = mm(turned[:, :ROWS], kron)
        first_ref[a * ROWS : (a + 1) * ROWS, :] = first.astype(BF16)
    second = mm(first_ref[:, :ROWS], lower).astype(BF16)
    lane_group = group(iota((PAD, 128), 1))
    for a in range(CHI):
        rows = slice(a * PAD, (a + 1) * PAD)
        tails = [jnp.zeros((PAD, 128), BF16)] * 2
        for k in range(CHI):
            block = second[a * ROWS + k * PAD : a * ROWS + (k + 1) * PAD]
            second_ref[rows, k * 128 : (k + 1) * 128] = block[:, :128]
            tails[k >> 3] = jnp.where(lane_group == (k & 7), block[:, 128:], tails[k >> 3])
        for side in range(2):
            at = (CHI + side) * 128
            second_ref[rows, at : at + 128] = tails[side]


def third(second_ref, right, kron_ref):
    tile = one_hot(minor(iota((PAD, LANES), 1)) == iota((PAD, LANES), 0))
    values = mm(right, tile, TN)
    lane_group = group(iota((CHI * CHI, LANES), 1))
    lane_group = jnp.where(lane_group < CHI, lane_group, lane_group - FOLD // PAD)
    entry = iota((CHI * CHI, LANES), 0)
    kept = lax.shift_right_logical(entry * 171, 11) == lane_group
    for k in range(CHI):
        block = values[k * PAD : k * PAD + CHI, :]
        tall = jnp.concatenate([block] * CHI, axis=0)
        tall = jnp.where(kept, tall, 0.0).astype(BF16)
        kron_ref[k * 128 : (k + 1) * 128, :] = tall[:128]
        at = CHI * 128 + k * PAD
        kron_ref[at : at + PAD, :] = tall[128:]
    used = CHI * 128 + CHI * PAD
    kron_ref[used:, :] = jnp.zeros((SECOND - used, LANES), BF16)
    return mm(second_ref[...], kron_ref[...])


def placed(site, mirror, lower):
    spaced = mm(row_spread(lower), site).astype(BF16)
    return block_swap(mm(spaced, spread_matrix(mirror)).astype(BF16))


def pick(own_first, own, other):
    return jnp.where(own_first, own, other), jnp.where(own_first, other, own)


def roles(level):
    row = lax.axis_index("row")
    own_lower = row >> level & 1
    first_upper = row >> level + 1 & 1 if level < LEVELS - 1 else row * 0 + 1
    flags = own_lower ^ first_upper, first_upper, own_lower, mirrored(row)
    return [flag != 0 for flag in flags]


def cast_kernel(own, cast_o):
    cast_o[...] = own[...].astype(BF16)


def first_gram_kernel(own, other, first_o, second_o, gram_o):
    own_first, _, own_lower, mirror = roles(0)
    mine = placed(own[...], mirror, own_lower)
    theirs = placed(other[...].astype(BF16), mirror, jnp.logical_not(own_lower))
    first_o[...], second_o[...] = pick(own_first, mine, theirs)
    products = pick(own_first, product_part(mine), product_part(theirs))
    gram_o[...] = outer_part(*products)


def own_kernel(own, wide_o, product_o):
    wide = unfold(spaced(own[...]))
    wide_o[...] = wide
    product_o[...] = product_part(wide)


def gram_kernel(level, wide, product, other, first_o, second_o, gram_o):
    own_first = roles(level)[0]
    theirs = unfold(spaced(other[...]))
    products = pick(own_first, product[...], product_part(theirs))
    gram_o[...] = outer_part(*products)
    first_o[...], second_o[...] = pick(own_first, wide[...], theirs)


def turn_kernel(level, first, second, start, turned_o, lower_o, starts_o, pieces_o):
    turned_o[...] = turn(first[...])
    lower_o[...] = mm(second[:, :ROWS], packing(), NT).astype(BF16)
    plain, turned = start_body(start[level], swap_matrix())
    first_upper = roles(level)[1]
    here = jnp.where(first_upper, plain, turned)
    starts_o[:PAD] = here
    starts_o[PAD:] = jnp.where(first_upper, turned, plain)
    pieces = parts2(here)
    pieces_o[: 2 * PAD] = pieces
    lifted = pltpu.roll(pieces[:, 128:], FOLD, 1)
    pieces_o[2 * PAD :] = jnp.concatenate([pieces[:, :128], lifted], axis=1)


def second_kernel(turned, lower, left, second_o, first):
    first_second(turned[...], lower[...], left[...], second_o, first)


def mean_square(merged):
    lines = jnp.sum(merged * merged, axis=0, keepdims=True)
    total = jnp.sum(lines[:, :128] + 0.5 * lines[:, 128:], axis=1, keepdims=True)
    return total / (CHI**4) + 1e-06


def third_kernel(second, right, log_in, next_o, log_o, kron):
    merged = third(second, right[...], kron)
    mean = mean_square(merged)
    half = ROWS // 2
    side = folded(merged[:half, 128:], merged[half:, 128:])
    next_o[...] = compact(jnp.concatenate([merged[:, :128], side], axis=0) * lax.rsqrt(mean))
    log_o[...] = log_in[...] + 0.5 * jnp.log(mean)


def last_kernel(second, right, log_in, coarse_o, log_o, kron):
    merged = third(second, right[...], kron)
    mean = mean_square(merged)
    log_o[...] = (log_in[...] + 0.5 * jnp.log(mean))[:1, :1]
    wide = block_swap(merged.astype(BF16))
    narrow = mm(wide, spread_matrix(roles(LEVELS - 1)[3]), NT).astype(BF16)
    coarse_o[...] = mm(row_spread(True), narrow, TN) * lax.rsqrt(mean)


def call(kernel, outs, scratch=()):
    vmem = pl.BlockSpec(memory_space=pltpu.VMEM)

    def run(*args):
        return pl.pallas_call(
            kernel,
            out_shape=[jax.ShapeDtypeStruct(s, d) for s, d in outs],
            in_specs=[vmem] * len(args),
            out_specs=[vmem] * len(outs),
            scratch_shapes=list(scratch),
            compiler_params=pltpu.CompilerParams(vmem_limit_bytes=VMEM_BYTES),
            cost_estimate=pl.CostEstimate(flops=10**8, bytes_accessed=10**6, transcendentals=0),
        )(*args)

    return run


def from_partner(array, flip):
    count = lax.axis_size("row")
    return lax.ppermute(array, "row", [(i, i ^ flip) for i in range(count)])


def mirrored(row):
    parity = row * 0
    for bit in range(LEVELS):
        parity = parity ^ (row >> bit & 1)
    return parity


def from_bond(array):
    rows, cols = lax.axis_size("row"), lax.axis_size("col")
    pairs = []
    for i in range(rows):
        for c in range(cols):
            target = (c + 1) % cols if mirrored(i) else (c - 1) % cols
            pairs.append((i * cols + c, (i ^ 1) * cols + target))
    return lax.ppermute(array, ("row", "col"), pairs)


def per_device(site_tensors, start_basis):
    square = CHI * CHI
    mat, packed, logs = ((ROWS, LANES), BF16), ((CHI * CHI * 3 // 2, 128), BF16), ((8, 128), F32)
    kron, firsts = [pltpu.VMEM((SECOND, LANES), BF16)], [pltpu.VMEM((CHI * ROWS, LANES), BF16)]
    log_total = jnp.zeros(*logs)
    own = site_tensors[0, 0]
    for level in range(LEVELS):
        if level == 0:
            other = from_partner(own, 1)
            (own,) = call(cast_kernel, [((square, square), BF16)])(own)
            first, lower, gram = call(first_gram_kernel, [mat, mat, packed])(own, other)
        else:
            other = from_partner(own, 1 << level | 1)
            wide, product = call(own_kernel, [mat, mat])(own)
            first, lower, gram = call(
                functools.partial(gram_kernel, level), [mat, mat, packed]
            )(wide, product, other)
        gram_other = from_bond(gram)
        turned, lower, starts, pieces = call(
            functools.partial(turn_kernel, level),
            [mat, mat, ((2 * PAD, LANES), F32), ((4 * PAD, LANES), BF16)],
        )(first, lower, start_basis)
        (left,) = call(iso_kernel, [((PAD, LANES), BF16)])(gram, gram_other, starts, pieces)
        right = from_partner(left, 1)
        (second,) = call(second_kernel, [((ROWS, SECOND), BF16)], firsts)(turned, lower, left)
        if level < LEVELS - 1:
            own, log_total = call(third_kernel, [packed, logs], kron)(second, right, log_total)
        else:
            coarse, log_total = call(last_kernel, [((square, square), F32), ((1, 1), F32)], kron)(
                second, right, log_total
            )
    return (coarse[None, None], log_total)


def solution(mesh):
    return jax.shard_map(
        per_device,
        mesh=mesh,
        in_specs=(P("row", "col", None, None), P()),
        out_specs=(P("row", "col", None, None), P("row", "col")),
        check_vma=False,
    )
```

```python
import functools

import functools

import jax
import jax.numpy as jnp
from jax import lax
from jax.experimental import pallas as pl
from jax.experimental.pallas import tpu as pltpu
from jax.sharding import PartitionSpec as P

CHI = 12
LEVELS = 3
SWEEPS = 2
PAD = 16
SHIFT = 4
ROWS = CHI * PAD
LANES = PAD * PAD
VMEM_BYTES = 8 << 20
SECOND = (CHI + 2) * 128
FOLD = 64
PIVOT = 1.0 / 64
F32 = jnp.float32
BF16 = jnp.bfloat16

NN = (((1,), (0,)), ((), ()))
NT = (((1,), (1,)), ((), ()))
TN = (((0,), (0,)), ((), ()))


def mm(a, b, dims=NN):
    return lax.dot_general(a, b, dims, preferred_element_type=F32)


def iota(shape, dim):
    return lax.broadcasted_iota(jnp.int32, shape, dim)


def group(index):
    return lax.shift_right_logical(index, SHIFT)


def minor(index):
    return lax.bitwise_and(index, PAD - 1)


def one_hot(mask):
    return jnp.where(mask, 1.0, 0.0).astype(BF16)


def swap_matrix(rows=LANES):
    i, j = iota((rows, LANES), 0), iota((rows, LANES), 1)
    return one_hot((group(i) == minor(j)) & (minor(i) == group(j)))


def spread_matrix(mirror):
    i, j = iota((CHI * CHI, LANES), 0), iota((CHI * CHI, LANES), 1)
    s, t = group(j), minor(j)
    source = jnp.where(mirror, t * CHI + s, s * CHI + t)
    return one_hot((i == source) & (s < CHI) & (t < CHI))


def swapped_tiles(x, fold, other=None):
    lane_group = group(iota((PAD, 128), 1))
    zero = jnp.zeros((PAD, 128), x.dtype)

    def tile(array, p, side):
        return array[p * PAD : (p + 1) * PAD, side * 128 : side * 128 + 128] if p < CHI else zero

    sources, span = {}, 8 if other is None else 4
    high = lax.bitwise_and(lane_group, 4) != 0
    for p in range(CHI if other is None else PAD):
        for side in range(2):
            if other is None:
                sources[p, side] = tile(x, p, side)
            elif p & 4:
                sources[p, side] = jnp.where(high, tile(x, p, side), tile(other, p ^ 4, side))
            else:
                sources[p, side] = jnp.where(high, tile(other, p ^ 4, side), tile(x, p, side))
    tiles = []
    for s in range(CHI):
        pair = []
        for side in range(2):
            lift = FOLD // PAD if fold and side and s >= CHI // 2 else 0
            out = zero
            for p in range(span):
                source = (side * 8 + (s & 7 & -span)) | p
                if other is None and source >= CHI:
                    continue
                shift = (p + lift - s % span) % 8 * PAD
                piece = sources[source, s >> 3]
                piece = pltpu.roll(piece, shift, 1) if shift else piece
                here = lax.bitwise_and(lane_group, span - 1) == p
                if lift:
                    here = lane_group == p + lift
                out = jnp.where(here, piece, out)
            pair.append(out)
        tiles.append(pair)
    return tiles


def block_swap(x, other=None):
    tiles = swapped_tiles(x, False, other)
    return jnp.concatenate([jnp.concatenate(pair, axis=1) for pair in tiles], axis=0)


def product_both(a, b):
    zero = jnp.zeros((PAD, b.shape[1]), b.dtype)
    blocks = [b[s * PAD : (s + 1) * PAD] if s < CHI else zero for s in range(PAD)]
    plain = mm(a, jnp.concatenate(blocks, axis=0), NT)
    moved = mm(a, jnp.concatenate([blocks[s ^ 4] for s in range(PAD)], axis=0), NT)
    return plain.astype(BF16), moved.astype(BF16)


def widen(x):
    return jnp.concatenate([x, jnp.zeros((x.shape[0], LANES - x.shape[1]), x.dtype)], axis=1)


def parts3(x):
    a = x.astype(BF16)
    rest = x - a.astype(F32)
    b = rest.astype(BF16)
    c = (rest - b.astype(F32)).astype(BF16)
    return jnp.concatenate([a, b, c], axis=0)


def parts2(x):
    a = x.astype(BF16)
    return jnp.concatenate([a, (x - a.astype(F32)).astype(BF16)], axis=0)


def fold2(y):
    n = y.shape[0] // 2
    return y[n:] + y[:n]


def fold3(y):
    n = y.shape[0] // 3
    return (y[2 * n :] + y[n : 2 * n]) + y[:n]


def folded(first, last):
    return jnp.where(iota(first.shape, 1) < FOLD, first, last)


def compact(x):
    blocks = x.shape[0] // PAD
    legs = x.astype(F32).reshape(blocks, PAD, 128)[:, :CHI]
    return legs.reshape(blocks * CHI, 128).astype(BF16)


def spaced(x):
    blocks = x.shape[0] // CHI
    legs = x.astype(F32).reshape(blocks, CHI, 128)
    rest = jnp.zeros((blocks, PAD - CHI, 128), F32)
    return jnp.concatenate([legs, rest], axis=1).reshape(blocks * PAD, 128).astype(BF16)


def unfold(x):
    side = x[ROWS:]
    low = iota(side.shape, 1) < FOLD
    zero = jnp.zeros_like(side)
    first = jnp.where(low, side, zero)
    last = jnp.where(low, pltpu.roll(side, 128 - FOLD, 1), zero)
    return jnp.concatenate([x[:ROWS], jnp.concatenate([first, last], axis=0)], axis=1)


def row_swap(x):
    legs = x.astype(F32).reshape(CHI, PAD, x.shape[1])[:, :CHI]
    turned = jnp.transpose(legs, (1, 0, 2))
    rest = jnp.zeros((CHI, PAD - CHI, x.shape[1]), F32)
    return jnp.concatenate([turned, rest], axis=1).reshape(x.shape).astype(BF16)


def product_part(x):
    return block_swap(*product_both(row_swap(x), x))


def outer_part(first, second):
    outer, moved = product_both(first, row_swap(second))
    tiles = swapped_tiles(outer, True, moved)
    half = CHI // 2
    side = folded(*(jnp.concatenate([t[1] for t in part], axis=0) for part in (tiles[:half], tiles[half:])))
    return compact(jnp.concatenate([t[0] for t in tiles] + [side], axis=0))


def turn(first):
    return widen(row_swap(first.T[:ROWS]))


def start_body(start, swap):
    start = jnp.concatenate([start, jnp.zeros((PAD - CHI, CHI * CHI), F32)], axis=0)
    pieces = parts3(start)
    spread = spread_matrix(False)
    plain = mm(pieces, spread)
    turned = mm(plain.astype(BF16), swap)
    return fold3(plain), fold3(turned)


def orthonormal(y):
    pieces = parts2(y)
    high, low = pieces[:PAD], pieces[PAD:]
    gram = fold2(mm(pieces, high, NT)) + mm(high, low, NT)
    width = y.shape[1]
    row = iota((PAD, 128), 0)
    cols = [jnp.broadcast_to(gram[:, k : k + 1], (PAD, 128)) for k in range(CHI)]
    floors = [jnp.broadcast_to(cols[k][k : k + 1, :], (PAD, 128)) * PIVOT for k in range(CHI)]
    scale = jnp.zeros((PAD, 128), F32)
    good = jnp.ones((PAD, 128), F32)
    for k in range(CHI):
        pivot = jnp.broadcast_to(cols[k][k : k + 1, :], (PAD, 128))
        good = jnp.where(pivot >= floors[k], good, 0.0)
        inverse = lax.rsqrt(pivot)
        scale = jnp.where(row == k, inverse, scale)
        factor = jnp.where(row > k, cols[k] * (inverse * inverse), 0.0)
        for j in range(k + 1, CHI):
            cols[j] = cols[j] - factor * jnp.broadcast_to(cols[j][k : k + 1, :], (PAD, 128))
        wide = jnp.concatenate([factor] * (width // 128), axis=1)
        y = y - wide * jnp.broadcast_to(y[k : k + 1, :], (PAD, width))
    return y * jnp.concatenate([scale] * (width // 128), axis=1), good


def exact_iso(own, other, start, start_turned, shift, swap):
    pieces = parts3(start)
    image = fold3(mm(pieces, own, NT) + mm(pieces, other, NT))
    basis, _ = orthonormal(widen(image) + shift * start_turned)
    pieces = parts3(basis)
    image = fold3(mm(pieces[:, :ROWS], own) + mm(pieces[:, :ROWS], other))
    basis, _ = orthonormal(image + shift * fold3(mm(pieces, swap)))
    return basis


def iso_kernel(own, other, starts, pieces, iso_o):
    swap = swap_matrix()
    grams = [spaced(own[...]), spaced(other[...])]
    doubled = [
        jnp.concatenate([g[:ROWS], jnp.concatenate([g[ROWS:]] * 2, axis=0)], axis=1) for g in grams
    ]
    total = doubled[0].astype(F32) + doubled[1].astype(F32)
    i, j = iota((ROWS, LANES), 0), iota((ROWS, LANES), 1)
    place = jnp.where(j < 128, j, 128 + lax.bitwise_and(j, FOLD - 1))
    valid = (j < 128) | ((lax.bitwise_and(j, 127) < FOLD) == (i < ROWS // 2))
    diagonal = valid & (group(i) == minor(place)) & (minor(i) == group(place))
    trace = jnp.sum(jnp.where(diagonal, total, 0.0), axis=0, keepdims=True)
    shift = jnp.sum(trace, axis=1, keepdims=True) / (CHI * CHI)
    unit = 1.0 / shift
    image = mm(pieces[...], doubled[0], NT) + mm(pieces[...], doubled[1], NT)
    lane = iota((2 * PAD, ROWS), 1)
    image = jnp.where(lane < ROWS // 2, image[: 2 * PAD], image[2 * PAD :])
    image = widen(fold2(image)) * unit + starts[PAD:]
    parts = parts2(image)
    own, other = unfold(grams[0]), unfold(grams[1])
    image = fold2(mm(parts[:, :ROWS], own) + mm(parts[:, :ROWS], other)) * unit
    basis, good = orthonormal(image + fold2(mm(parts, swap)))
    iso_o[...] = basis.astype(BF16)

    @pl.when(jnp.logical_not(jnp.min(good[:1]) > 0.5))
    def _():
        basis = exact_iso(own, other, starts[:PAD], starts[PAD:], shift, swap)
        iso_o[...] = basis.astype(BF16)


def packed_pair(index):
    entry = jnp.where(index < 128, index, 128 + minor(index))
    s = lax.shift_right_logical(entry * 171, 11)
    return s, entry - s * CHI


def packing():
    s, t = packed_pair(iota((LANES, ROWS), 0))
    j = iota((LANES, ROWS), 1)
    return one_hot((group(j) == s) & (minor(j) == t))


def first_second(turned, lower, left, second_ref, first_ref):
    lane = iota((PAD, LANES), 1)
    masked = [jnp.where(group(lane) == k, left.astype(F32), 0.0) for k in range(CHI)]
    masked = jnp.concatenate(masked, axis=0).astype(BF16)
    i, j = iota((LANES, LANES), 0), iota((LANES, LANES), 1)
    values = mm(masked, one_hot(minor(i) == group(j)))
    eye = minor(lane) == iota((PAD, LANES), 0)
    for a in range(CHI):
        blocks = []
        for k in range(CHI):
            line = jnp.broadcast_to(values[k * PAD + a : k * PAD + a + 1, :], (PAD, LANES))
            blocks.append(jnp.where(eye, line, 0.0).astype(BF16))
        kron = jnp.concatenate(blocks, axis=0)
        first = mm(turned[:, :ROWS], kron)
        first_ref[a * ROWS : (a + 1) * ROWS, :] = first.astype(BF16)
    second = mm(first_ref[:, :ROWS], lower).astype(BF16)
    lane_group = group(iota((PAD, 128), 1))
    for a in range(CHI):
        rows = slice(a * PAD, (a + 1) * PAD)
        tails = [jnp.zeros((PAD, 128), BF16)] * 2
        for k in range(CHI):
            block = second[a * ROWS + k * PAD : a * ROWS + (k + 1) * PAD]
            second_ref[rows, k * 128 : (k + 1) * 128] = block[:, :128]
            tails[k >> 3] = jnp.where(lane_group == (k & 7), block[:, 128:], tails[k >> 3])
        for side in range(2):
            at = (CHI + side) * 128
            second_ref[rows, at : at + 128] = tails[side]


def third(second_ref, right, kron_ref):
    values = jnp.concatenate([right] * PAD, axis=0).T.astype(F32)
    lane_group = group(iota((CHI * CHI, LANES), 1))
    lane_group = jnp.where(lane_group < CHI, lane_group, lane_group - FOLD // PAD)
    entry = iota((CHI * CHI, LANES), 0)
    kept = lax.shift_right_logical(entry * 171, 11) == lane_group
    for k in range(CHI):
        block = values[k * PAD : k * PAD + CHI, :]
        tall = jnp.concatenate([block] * CHI, axis=0)
        tall = jnp.where(kept, tall, 0.0).astype(BF16)
        kron_ref[k * 128 : (k + 1) * 128, :] = tall[:128]
        at = CHI * 128 + k * PAD
        kron_ref[at : at + PAD, :] = tall[128:]
    used = CHI * 128 + CHI * PAD
    kron_ref[used:, :] = jnp.zeros((SECOND - used, LANES), BF16)
    return mm(second_ref[...], kron_ref[...])


def placed(site, mirror, lower):
    legs = site.astype(F32).reshape(CHI, CHI, CHI * CHI)
    legs = jnp.where(lower, jnp.transpose(legs, (1, 0, 2)), legs)
    rest = jnp.zeros((CHI, PAD - CHI, CHI * CHI), F32)
    rows = jnp.concatenate([legs, rest], axis=1).reshape(ROWS, CHI * CHI).astype(BF16)
    return block_swap(mm(rows, spread_matrix(mirror)).astype(BF16))


def pick(own_first, own, other):
    return jnp.where(own_first, own, other), jnp.where(own_first, other, own)


def roles(level):
    row = lax.axis_index("row")
    own_lower = row >> level & 1
    first_upper = row >> level + 1 & 1 if level < LEVELS - 1 else row * 0 + 1
    flags = own_lower ^ first_upper, first_upper, own_lower, mirrored(row)
    return [flag != 0 for flag in flags]


def cast_kernel(own, cast_o):
    cast_o[...] = own[...].astype(BF16)


def first_gram_kernel(own, other, first_o, second_o, gram_o):
    own_first, _, own_lower, mirror = roles(0)
    mine = placed(own[...], mirror, own_lower)
    theirs = placed(other[...].astype(BF16), mirror, jnp.logical_not(own_lower))
    first_o[...], second_o[...] = pick(own_first, mine, theirs)
    products = pick(own_first, product_part(mine), product_part(theirs))
    gram_o[...] = outer_part(*products)


def own_kernel(own, wide_o, product_o):
    wide = unfold(spaced(own[...]))
    wide_o[...] = wide
    product_o[...] = product_part(wide)


def gram_kernel(level, wide, product, other, first_o, second_o, gram_o):
    own_first = roles(level)[0]
    theirs = unfold(spaced(other[...]))
    products = pick(own_first, product[...], product_part(theirs))
    gram_o[...] = outer_part(*products)
    first_o[...], second_o[...] = pick(own_first, wide[...], theirs)


def turn_kernel(level, first, second, start, turned_o, lower_o, starts_o, pieces_o):
    turned_o[...] = turn(first[...])
    lower_o[...] = mm(second[:, :ROWS], packing(), NT).astype(BF16)
    plain, turned = start_body(start[level], swap_matrix())
    first_upper = roles(level)[1]
    here = jnp.where(first_upper, plain, turned)
    starts_o[:PAD] = here
    starts_o[PAD:] = jnp.where(first_upper, turned, plain)
    pieces = parts2(here)
    pieces_o[: 2 * PAD] = pieces
    lifted = pltpu.roll(pieces[:, 128:], FOLD, 1)
    pieces_o[2 * PAD :] = jnp.concatenate([pieces[:, :128], lifted], axis=1)


def second_kernel(turned, lower, left, second_o, first):
    first_second(turned[...], lower[...], left[...], second_o, first)


def mean_square(merged):
    lines = jnp.sum(merged * merged, axis=0, keepdims=True)
    total = jnp.sum(lines[:, :128] + 0.5 * lines[:, 128:], axis=1, keepdims=True)
    return total / (CHI**4) + 1e-06


def third_kernel(second, right, log_in, next_o, log_o, kron):
    merged = third(second, right[...], kron)
    mean = mean_square(merged)
    half = ROWS // 2
    side = folded(merged[:half, 128:], merged[half:, 128:])
    next_o[...] = compact(jnp.concatenate([merged[:, :128], side], axis=0) * lax.rsqrt(mean))
    log_o[...] = log_in[...] + 0.5 * jnp.log(mean)


def last_kernel(second, right, log_in, coarse_o, log_o, kron):
    merged = third(second, right[...], kron)
    mean = mean_square(merged)
    log_o[...] = (log_in[...] + 0.5 * jnp.log(mean))[:1, :1]
    wide = block_swap(merged.astype(BF16))
    narrow = mm(wide, spread_matrix(roles(LEVELS - 1)[3]), NT) * lax.rsqrt(mean)
    legs = jnp.transpose(narrow.reshape(CHI, PAD, CHI * CHI)[:, :CHI], (1, 0, 2))
    coarse_o[...] = legs.reshape(CHI * CHI, CHI * CHI)


def call(kernel, outs, scratch=()):
    vmem = pl.BlockSpec(memory_space=pltpu.VMEM)

    def run(*args):
        return pl.pallas_call(
            kernel,
            out_shape=[jax.ShapeDtypeStruct(s, d) for s, d in outs],
            in_specs=[vmem] * len(args),
            out_specs=[vmem] * len(outs),
            scratch_shapes=list(scratch),
            compiler_params=pltpu.CompilerParams(vmem_limit_bytes=VMEM_BYTES),
            cost_estimate=pl.CostEstimate(flops=10**8, bytes_accessed=10**6, transcendentals=0),
        )(*args)

    return run


def from_partner(array, flip):
    count = lax.axis_size("row")
    return lax.ppermute(array, "row", [(i, i ^ flip) for i in range(count)])


def mirrored(row):
    parity = row * 0
    for bit in range(LEVELS):
        parity = parity ^ (row >> bit & 1)
    return parity


def from_bond(array):
    rows, cols = lax.axis_size("row"), lax.axis_size("col")
    pairs = []
    for i in range(rows):
        for c in range(cols):
            target = (c + 1) % cols if mirrored(i) else (c - 1) % cols
            pairs.append((i * cols + c, (i ^ 1) * cols + target))
    return lax.ppermute(array, ("row", "col"), pairs)


def per_device(site_tensors, start_basis):
    square = CHI * CHI
    mat, packed, logs = ((ROWS, LANES), BF16), ((CHI * CHI * 3 // 2, 128), BF16), ((8, 128), F32)
    kron, firsts = [pltpu.VMEM((SECOND, LANES), BF16)], [pltpu.VMEM((CHI * ROWS, LANES), BF16)]
    log_total = jnp.zeros(*logs)
    own = site_tensors[0, 0]
    for level in range(LEVELS):
        if level == 0:
            other = from_partner(own, 1)
            (own,) = call(cast_kernel, [((square, square), BF16)])(own)
            first, lower, gram = call(first_gram_kernel, [mat, mat, packed])(own, other)
        else:
            other = from_partner(own, 1 << level | 1)
            wide, product = call(own_kernel, [mat, mat])(own)
            first, lower, gram = call(
                functools.partial(gram_kernel, level), [mat, mat, packed]
            )(wide, product, other)
        gram_other = from_bond(gram)
        turned, lower, starts, pieces = call(
            functools.partial(turn_kernel, level),
            [mat, mat, ((2 * PAD, LANES), F32), ((4 * PAD, LANES), BF16)],
        )(first, lower, start_basis)
        (left,) = call(iso_kernel, [((PAD, LANES), BF16)])(gram, gram_other, starts, pieces)
        right = from_partner(left, 1)
        (second,) = call(second_kernel, [((ROWS, SECOND), BF16)], firsts)(turned, lower, left)
        if level < LEVELS - 1:
            own, log_total = call(third_kernel, [packed, logs], kron)(second, right, log_total)
        else:
            coarse, log_total = call(last_kernel, [((square, square), F32), ((1, 1), F32)], kron)(
                second, right, log_total
            )
    return (coarse[None, None], log_total)


def solution(mesh):
    return jax.shard_map(
        per_device,
        mesh=mesh,
        in_specs=(P("row", "col", None, None), P()),
        out_specs=(P("row", "col", None, None), P("row", "col")),
        check_vma=False,
    )
```

```python
import functools

import functools

import jax
import jax.numpy as jnp
from jax import lax
from jax.experimental import pallas as pl
from jax.experimental.pallas import tpu as pltpu
from jax.sharding import PartitionSpec as P

CHI = 12
LEVELS = 3
SWEEPS = 2
PAD = 16
SHIFT = 4
ROWS = CHI * PAD
LANES = PAD * PAD
VMEM_BYTES = 8 << 20
SECOND = (CHI + 2) * 128
FOLD = 64
PIVOT = 1.0 / 64
F32 = jnp.float32
BF16 = jnp.bfloat16

NN = (((1,), (0,)), ((), ()))
NT = (((1,), (1,)), ((), ()))
TN = (((0,), (0,)), ((), ()))


def mm(a, b, dims=NN):
    return lax.dot_general(a, b, dims, preferred_element_type=F32)


def iota(shape, dim):
    return lax.broadcasted_iota(jnp.int32, shape, dim)


def group(index):
    return lax.shift_right_logical(index, SHIFT)


def minor(index):
    return lax.bitwise_and(index, PAD - 1)


def one_hot(mask):
    return jnp.where(mask, 1.0, 0.0).astype(BF16)


def swap_matrix(rows=LANES):
    i, j = iota((rows, LANES), 0), iota((rows, LANES), 1)
    return one_hot((group(i) == minor(j)) & (minor(i) == group(j)))


def spread_matrix(mirror):
    i, j = iota((CHI * CHI, LANES), 0), iota((CHI * CHI, LANES), 1)
    s, t = group(j), minor(j)
    source = jnp.where(mirror, t * CHI + s, s * CHI + t)
    return one_hot((i == source) & (s < CHI) & (t < CHI))


def swapped_tiles(x, fold, other=None):
    lane_group = group(iota((PAD, 128), 1))
    zero = jnp.zeros((PAD, 128), x.dtype)

    def tile(array, p, side):
        return array[p * PAD : (p + 1) * PAD, side * 128 : side * 128 + 128] if p < CHI else zero

    sources, span = {}, 8 if other is None else 4
    high = lax.bitwise_and(lane_group, 4) != 0
    for p in range(CHI if other is None else PAD):
        for side in range(2):
            if other is None:
                sources[p, side] = tile(x, p, side)
            elif p & 4:
                sources[p, side] = jnp.where(high, tile(x, p, side), tile(other, p ^ 4, side))
            else:
                sources[p, side] = jnp.where(high, tile(other, p ^ 4, side), tile(x, p, side))
    tiles = []
    for s in range(CHI):
        pair = []
        for side in range(2):
            lift = FOLD // PAD if fold and side and s >= CHI // 2 else 0
            out = zero
            for p in range(span):
                source = (side * 8 + (s & 7 & -span)) | p
                if other is None and source >= CHI:
                    continue
                shift = (p + lift - s % span) % 8 * PAD
                piece = sources[source, s >> 3]
                piece = pltpu.roll(piece, shift, 1) if shift else piece
                here = lax.bitwise_and(lane_group, span - 1) == p
                if lift:
                    here = lane_group == p + lift
                out = jnp.where(here, piece, out)
            pair.append(out)
        tiles.append(pair)
    return tiles


def block_swap(x, other=None):
    tiles = swapped_tiles(x, False, other)
    return jnp.concatenate([jnp.concatenate(pair, axis=1) for pair in tiles], axis=0)


def product_both(a, b, scale=None):
    zero = jnp.zeros((PAD, b.shape[1]), b.dtype)
    blocks = [b[s * PAD : (s + 1) * PAD] if s < CHI else zero for s in range(PAD)]
    plain = mm(a, jnp.concatenate(blocks, axis=0), NT)
    moved = mm(a, jnp.concatenate([blocks[s ^ 4] for s in range(PAD)], axis=0), NT)
    if scale is not None:
        plain, moved = plain * scale, moved * scale
    return plain.astype(BF16), moved.astype(BF16)


def widen(x):
    return jnp.concatenate([x, jnp.zeros((x.shape[0], LANES - x.shape[1]), x.dtype)], axis=1)


def parts3(x):
    a = x.astype(BF16)
    rest = x - a.astype(F32)
    b = rest.astype(BF16)
    c = (rest - b.astype(F32)).astype(BF16)
    return jnp.concatenate([a, b, c], axis=0)


def parts2(x):
    a = x.astype(BF16)
    return jnp.concatenate([a, (x - a.astype(F32)).astype(BF16)], axis=0)


def fold2(y):
    n = y.shape[0] // 2
    return y[n:] + y[:n]


def fold3(y):
    n = y.shape[0] // 3
    return (y[2 * n :] + y[n : 2 * n]) + y[:n]


def folded(first, last):
    return jnp.where(iota(first.shape, 1) < FOLD, first, last)


def compact(x):
    blocks = x.shape[0] // PAD
    legs = x.astype(F32).reshape(blocks, PAD, 128)[:, :CHI]
    return legs.reshape(blocks * CHI, 128).astype(BF16)


def spaced(x):
    blocks = x.shape[0] // CHI
    legs = x.astype(F32).reshape(blocks, CHI, 128)
    rest = jnp.zeros((blocks, PAD - CHI, 128), F32)
    return jnp.concatenate([legs, rest], axis=1).reshape(blocks * PAD, 128).astype(BF16)


def unfold(x):
    side = x[ROWS:]
    low = iota(side.shape, 1) < FOLD
    zero = jnp.zeros_like(side)
    first = jnp.where(low, side, zero)
    last = jnp.where(low, pltpu.roll(side, 128 - FOLD, 1), zero)
    return jnp.concatenate([x[:ROWS], jnp.concatenate([first, last], axis=0)], axis=1)


def row_swap(x):
    legs = x.astype(F32).reshape(CHI, PAD, x.shape[1])[:, :CHI]
    turned = jnp.transpose(legs, (1, 0, 2))
    rest = jnp.zeros((CHI, PAD - CHI, x.shape[1]), F32)
    return jnp.concatenate([turned, rest], axis=1).reshape(x.shape).astype(BF16)


def product_part(x, scale=None):
    return block_swap(*product_both(row_swap(x), x, scale))


def outer_part(first, second):
    outer, moved = product_both(first, row_swap(second))
    tiles = swapped_tiles(outer, True, moved)
    half = CHI // 2
    side = folded(*(jnp.concatenate([t[1] for t in part], axis=0) for part in (tiles[:half], tiles[half:])))
    return compact(jnp.concatenate([t[0] for t in tiles] + [side], axis=0))


def turn(first):
    return widen(row_swap(first.T[:ROWS]))


def start_body(start, swap):
    start = jnp.concatenate([start, jnp.zeros((PAD - CHI, CHI * CHI), F32)], axis=0)
    pieces = parts3(start)
    spread = spread_matrix(False)
    plain = mm(pieces, spread)
    turned = mm(plain.astype(BF16), swap)
    return fold3(plain), fold3(turned)


def row_products(y):
    pieces = parts2(y)
    high, low = pieces[:PAD], pieces[PAD:]
    gram = fold2(mm(pieces, high, NT)) + mm(high, low, NT)
    return [jnp.broadcast_to(gram[:, k : k + 1], (PAD, 128)) for k in range(CHI)]


def line(x, k):
    return jnp.broadcast_to(x[k : k + 1, :], x.shape)


def twice(x, width):
    return jnp.concatenate([x] * (width // 128), axis=1)


def exact_orthonormal(y):
    cols = row_products(y)
    row = iota((PAD, 128), 0)
    scale = jnp.zeros((PAD, 128), F32)
    for k in range(CHI):
        inverse = lax.rsqrt(line(cols[k], k))
        scale = jnp.where(row == k, inverse, scale)
        factor = jnp.where(row > k, cols[k] * (inverse * inverse), 0.0)
        for j in range(k + 1, CHI):
            cols[j] = cols[j] - factor * line(cols[j], k)
        y = y - twice(factor, y.shape[1]) * line(y, k)
    return y * twice(scale, y.shape[1])


def orthonormal(y):
    cols = row_products(y)
    width = y.shape[1]
    row = iota((PAD, 128), 0)
    floors = [line(cols[k], k) * PIVOT for k in range(CHI)]
    scale, inner = jnp.zeros((PAD, 128), F32), jnp.zeros((PAD, 128), F32)
    good = jnp.ones((PAD, 128), F32)
    for k in range(0, CHI, 2):
        here, after = cols[k], cols[k + 1]
        top, side, low = line(here, k), line(here, k + 1), line(after, k + 1)
        det = top * low - side * side
        good = jnp.where((top >= floors[k]) & (det >= floors[k + 1] * top), good, 0.0)
        over, rest = 1.0 / det, row > k + 1
        first = jnp.where(rest, (low * here - side * after) * over, 0.0)
        second = jnp.where(rest, (top * after - side * here) * over, 0.0)
        for j in range(k + 2, CHI):
            cols[j] = cols[j] - first * line(cols[j], k) - second * line(cols[j], k + 1)
        y = y - twice(first, width) * line(y, k) - twice(second, width) * line(y, k + 1)
        scale = jnp.where(row == k, lax.rsqrt(top), scale)
        scale = jnp.where(row == k + 1, lax.rsqrt(det / top), scale)
        inner = jnp.where(row == k + 1, side / top, inner)
    y = y - twice(inner, width) * pltpu.roll(y, 1, 0)
    return y * twice(scale, width), good


def exact_iso(own, other, start, start_turned, shift, swap):
    pieces = parts3(start)
    image = fold3(mm(pieces, own, NT) + mm(pieces, other, NT))
    basis = exact_orthonormal(widen(image) + shift * start_turned)
    pieces = parts3(basis)
    image = fold3(mm(pieces[:, :ROWS], own) + mm(pieces[:, :ROWS], other))
    return exact_orthonormal(image + shift * fold3(mm(pieces, swap)))


def iso_kernel(own, other, starts, pieces, iso_o):
    swap = swap_matrix()
    grams = [spaced(own[...]), spaced(other[...])]
    doubled = [
        jnp.concatenate([g[:ROWS], jnp.concatenate([g[ROWS:]] * 2, axis=0)], axis=1) for g in grams
    ]
    total = doubled[0].astype(F32) + doubled[1].astype(F32)
    i, j = iota((ROWS, LANES), 0), iota((ROWS, LANES), 1)
    place = jnp.where(j < 128, j, 128 + lax.bitwise_and(j, FOLD - 1))
    valid = (j < 128) | ((lax.bitwise_and(j, 127) < FOLD) == (i < ROWS // 2))
    diagonal = valid & (group(i) == minor(place)) & (minor(i) == group(place))
    trace = jnp.sum(jnp.where(diagonal, total, 0.0), axis=0, keepdims=True)
    shift = jnp.sum(trace, axis=1, keepdims=True) / (CHI * CHI)
    unit = 1.0 / shift
    image = mm(pieces[...], doubled[0], NT) + mm(pieces[...], doubled[1], NT)
    lane = iota((2 * PAD, ROWS), 1)
    image = jnp.where(lane < ROWS // 2, image[: 2 * PAD], image[2 * PAD :])
    image = widen(fold2(image)) * unit + starts[PAD:]
    parts = parts2(image)
    own, other = unfold(grams[0]), unfold(grams[1])
    image = fold2(mm(parts[:, :ROWS], own) + mm(parts[:, :ROWS], other)) * unit
    basis, good = orthonormal(image + fold2(mm(parts, swap)))
    iso_o[...] = basis.astype(BF16)

    @pl.when(jnp.logical_not(good[0, 0] > 0.5))
    def _():
        basis = exact_iso(own, other, starts[:PAD], starts[PAD:], shift, swap)
        iso_o[...] = basis.astype(BF16)


def packed_pair(index):
    entry = jnp.where(index < 128, index, 128 + minor(index))
    s = lax.shift_right_logical(entry * 171, 11)
    return s, entry - s * CHI


def packing():
    s, t = packed_pair(iota((LANES, ROWS), 0))
    j = iota((LANES, ROWS), 1)
    return one_hot((group(j) == s) & (minor(j) == t))


def first_second(turned, lower, left, second_ref, first_ref):
    lane = iota((PAD, LANES), 1)
    masked = [jnp.where(group(lane) == k, left.astype(F32), 0.0) for k in range(CHI)]
    masked = jnp.concatenate(masked, axis=0).astype(BF16)
    i, j = iota((LANES, LANES), 0), iota((LANES, LANES), 1)
    values = mm(masked, one_hot(minor(i) == group(j)))
    eye = minor(lane) == iota((PAD, LANES), 0)
    for a in range(CHI):
        blocks = []
        for k in range(CHI):
            line = jnp.broadcast_to(values[k * PAD + a : k * PAD + a + 1, :], (PAD, LANES))
            blocks.append(jnp.where(eye, line, 0.0).astype(BF16))
        kron = jnp.concatenate(blocks, axis=0)
        first = mm(turned[:, :ROWS], kron)
        first_ref[a * ROWS : (a + 1) * ROWS, :] = first.astype(BF16)
    second = mm(first_ref[:, :ROWS], lower).astype(BF16)
    lane_group = group(iota((PAD, 128), 1))
    for a in range(CHI):
        rows = slice(a * PAD, (a + 1) * PAD)
        tails = [jnp.zeros((PAD, 128), BF16)] * 2
        for k in range(CHI):
            block = second[a * ROWS + k * PAD : a * ROWS + (k + 1) * PAD]
            second_ref[rows, k * 128 : (k + 1) * 128] = block[:, :128]
            tails[k >> 3] = jnp.where(lane_group == (k & 7), block[:, 128:], tails[k >> 3])
        for side in range(2):
            at = (CHI + side) * 128
            second_ref[rows, at : at + 128] = tails[side]


def third(second_ref, right, kron_ref):
    values = jnp.concatenate([right] * PAD, axis=0).T.astype(F32)
    lane_group = group(iota((CHI * CHI, LANES), 1))
    lane_group = jnp.where(lane_group < CHI, lane_group, lane_group - FOLD // PAD)
    entry = iota((CHI * CHI, LANES), 0)
    kept = lax.shift_right_logical(entry * 171, 11) == lane_group
    for k in range(CHI):
        block = values[k * PAD : k * PAD + CHI, :]
        tall = jnp.concatenate([block] * CHI, axis=0)
        tall = jnp.where(kept, tall, 0.0).astype(BF16)
        kron_ref[k * 128 : (k + 1) * 128, :] = tall[:128]
        at = CHI * 128 + k * PAD
        kron_ref[at : at + PAD, :] = tall[128:]
    used = CHI * 128 + CHI * PAD
    kron_ref[used:, :] = jnp.zeros((SECOND - used, LANES), BF16)
    return mm(second_ref[...], kron_ref[...])


def placed(site, mirror, lower):
    legs = site.astype(F32).reshape(CHI, CHI, CHI * CHI)
    legs = jnp.where(lower, jnp.transpose(legs, (1, 0, 2)), legs)
    rest = jnp.zeros((CHI, PAD - CHI, CHI * CHI), F32)
    rows = jnp.concatenate([legs, rest], axis=1).reshape(ROWS, CHI * CHI).astype(BF16)
    return block_swap(mm(rows, spread_matrix(mirror)).astype(BF16))


def pick(own_first, own, other):
    return jnp.where(own_first, own, other), jnp.where(own_first, other, own)


def roles(level):
    row = lax.axis_index("row")
    own_lower = row >> level & 1
    first_upper = row >> level + 1 & 1 if level < LEVELS - 1 else row * 0 + 1
    flags = own_lower ^ first_upper, first_upper, own_lower, mirrored(row)
    return [flag != 0 for flag in flags]


def cast_kernel(own, cast_o):
    cast_o[...] = own[...].astype(BF16)


def first_gram_kernel(own, other, first_o, second_o, gram_o):
    own_first, _, own_lower, mirror = roles(0)
    mine = placed(own[...], mirror, own_lower)
    theirs = placed(other[...].astype(BF16), mirror, jnp.logical_not(own_lower))
    first_o[...], second_o[...] = pick(own_first, mine, theirs)
    products = pick(own_first, product_part(mine), product_part(theirs))
    gram_o[...] = outer_part(*products)


def mean_square(lines):
    mean = jnp.sum(lines, axis=1, keepdims=True) / (CHI**4) + 1e-06
    return jnp.broadcast_to(mean, (8, 128))


def scaled_product(x):
    mean = mean_square(jnp.sum(jnp.square(x.astype(F32)), axis=0, keepdims=True))
    return product_part(x, twice(1.0 / mean[:1], LANES)), mean


def own_kernel(own, wide_o, product_o, mean_o):
    wide = unfold(spaced(own[...]))
    wide_o[...] = wide
    product_o[...], mean_o[...] = scaled_product(wide)


def gram_kernel(level, wide, product, mean, other, first_o, second_o, gram_o, scale_o):
    own_first = roles(level)[0]
    theirs = unfold(spaced(other[...]))
    other_product, other_mean = scaled_product(theirs)
    gram_o[...] = outer_part(*pick(own_first, product[...], other_product))
    first_o[...], second_o[...] = pick(own_first, wide[...], theirs)
    scale_o[...] = lax.rsqrt(mean[...]) * lax.rsqrt(other_mean)


def turn_kernel(level, first, second, start, turned_o, lower_o, starts_o, pieces_o):
    turned_o[...] = turn(first[...])
    lower_o[...] = mm(second[:, :ROWS], packing(), NT).astype(BF16)
    plain, turned = start_body(start[level], swap_matrix())
    first_upper = roles(level)[1]
    here = jnp.where(first_upper, plain, turned)
    starts_o[:PAD] = here
    starts_o[PAD:] = jnp.where(first_upper, turned, plain)
    pieces = parts2(here)
    pieces_o[: 2 * PAD] = pieces
    lifted = pltpu.roll(pieces[:, 128:], FOLD, 1)
    pieces_o[2 * PAD :] = jnp.concatenate([pieces[:, :128], lifted], axis=1)


def second_kernel(turned, lower, left, second_o, first):
    first_second(turned[...], lower[...], left[...], second_o, first)


def third_kernel(second, right, *refs):
    *scales, next_o, kron = refs
    merged = third(second, right[...], kron)
    half = ROWS // 2
    side = folded(merged[:half, 128:], merged[half:, 128:])
    merged = jnp.concatenate([merged[:, :128], side], axis=0)
    for scale in scales:
        merged = merged * scale[:1]
    next_o[...] = compact(merged)


def last_kernel(second, right, scale, *refs):
    *means, coarse_o, log_o, kron = refs
    merged = third(second, right[...], kron) * twice(scale[:1], LANES)
    lines = jnp.sum(merged * merged, axis=0, keepdims=True)
    mean = mean_square(lines[:, :128] + 0.5 * lines[:, 128:])
    log_o[...] = 0.5 * sum(jnp.log(m[:1, :1]) for m in [*means, mean])
    wide = block_swap(merged.astype(BF16))
    narrow = mm(wide, spread_matrix(roles(LEVELS - 1)[3]), NT)
    narrow = narrow * twice(lax.rsqrt(mean[:1]), LANES)[:, : CHI * CHI]
    legs = jnp.transpose(narrow.reshape(CHI, PAD, CHI * CHI)[:, :CHI], (1, 0, 2))
    coarse_o[...] = legs.reshape(CHI * CHI, CHI * CHI)


def call(kernel, outs, scratch=()):
    vmem = pl.BlockSpec(memory_space=pltpu.VMEM)

    def run(*args):
        return pl.pallas_call(
            kernel,
            out_shape=[jax.ShapeDtypeStruct(s, d) for s, d in outs],
            in_specs=[vmem] * len(args),
            out_specs=[vmem] * len(outs),
            scratch_shapes=list(scratch),
            compiler_params=pltpu.CompilerParams(vmem_limit_bytes=VMEM_BYTES),
            cost_estimate=pl.CostEstimate(flops=10**8, bytes_accessed=10**6, transcendentals=0),
        )(*args)

    return run


def from_partner(array, flip):
    count = lax.axis_size("row")
    return lax.ppermute(array, "row", [(i, i ^ flip) for i in range(count)])


def mirrored(row):
    parity = row * 0
    for bit in range(LEVELS):
        parity = parity ^ (row >> bit & 1)
    return parity


def from_bond(array):
    rows, cols = lax.axis_size("row"), lax.axis_size("col")
    pairs = []
    for i in range(rows):
        for c in range(cols):
            target = (c + 1) % cols if mirrored(i) else (c - 1) % cols
            pairs.append((i * cols + c, (i ^ 1) * cols + target))
    return lax.ppermute(array, ("row", "col"), pairs)


def per_device(site_tensors, start_basis):
    square = CHI * CHI
    mat, packed, one = ((ROWS, LANES), BF16), ((CHI * CHI * 3 // 2, 128), BF16), ((8, 128), F32)
    kron, firsts = [pltpu.VMEM((SECOND, LANES), BF16)], [pltpu.VMEM((CHI * ROWS, LANES), BF16)]
    scales, means = [], []
    own = site_tensors[0, 0]
    for level in range(LEVELS):
        if level == 0:
            other = from_partner(own, 1)
            (own,) = call(cast_kernel, [((square, square), BF16)])(own)
            first, lower, gram = call(first_gram_kernel, [mat, mat, packed])(own, other)
        else:
            other = from_partner(own, 1 << level | 1)
            wide, product, mean = call(own_kernel, [mat, mat, one])(own)
            first, lower, gram, scale = call(
                functools.partial(gram_kernel, level), [mat, mat, packed, one]
            )(wide, product, mean, other)
            scales, means = [scale], [*means, mean]
        gram_other = from_bond(gram)
        turned, lower, starts, pieces = call(
            functools.partial(turn_kernel, level),
            [mat, mat, ((2 * PAD, LANES), F32), ((4 * PAD, LANES), BF16)],
        )(first, lower, start_basis)
        (left,) = call(iso_kernel, [((PAD, LANES), BF16)])(gram, gram_other, starts, pieces)
        right = from_partner(left, 1)
        (second,) = call(second_kernel, [((ROWS, SECOND), BF16)], firsts)(turned, lower, left)
        if level < LEVELS - 1:
            (own,) = call(third_kernel, [packed], kron)(second, right, *scales)
        else:
            coarse, log_total = call(last_kernel, [((square, square), F32), ((1, 1), F32)], kron)(
                second, right, *scales, *means
            )
    return (coarse[None, None], log_total)


def solution(mesh):
    return jax.shard_map(
        per_device,
        mesh=mesh,
        in_specs=(P("row", "col", None, None), P()),
        out_specs=(P("row", "col", None, None), P("row", "col")),
        check_vma=False,
    )
```

```python
import functools

import functools

import jax
import jax.numpy as jnp
from jax import lax
from jax.experimental import pallas as pl
from jax.experimental.pallas import tpu as pltpu
from jax.sharding import PartitionSpec as P

CHI = 12
LEVELS = 3
SWEEPS = 2
PAD = 16
SHIFT = 4
ROWS = CHI * PAD
LANES = PAD * PAD
VMEM_BYTES = 8 << 20
SECOND = (CHI + 2) * 128
FOLD = 64
PIVOT = 1.0 / 64
F32 = jnp.float32
BF16 = jnp.bfloat16

NN = (((1,), (0,)), ((), ()))
NT = (((1,), (1,)), ((), ()))
TN = (((0,), (0,)), ((), ()))


def mm(a, b, dims=NN):
    return lax.dot_general(a, b, dims, preferred_element_type=F32)


def iota(shape, dim):
    return lax.broadcasted_iota(jnp.int32, shape, dim)


def group(index):
    return lax.shift_right_logical(index, SHIFT)


def minor(index):
    return lax.bitwise_and(index, PAD - 1)


def one_hot(mask):
    return jnp.where(mask, 1.0, 0.0).astype(BF16)


def swap_matrix(rows=LANES):
    i, j = iota((rows, LANES), 0), iota((rows, LANES), 1)
    return one_hot((group(i) == minor(j)) & (minor(i) == group(j)))


def spread_matrix(mirror):
    i, j = iota((CHI * CHI, LANES), 0), iota((CHI * CHI, LANES), 1)
    s, t = group(j), minor(j)
    source = jnp.where(mirror, t * CHI + s, s * CHI + t)
    return one_hot((i == source) & (s < CHI) & (t < CHI))


def gather_matrix(mirror):
    i, j = iota((LANES, CHI * CHI), 0), iota((LANES, CHI * CHI), 1)
    s, t = group(i), minor(i)
    source = jnp.where(mirror, t * CHI + s, s * CHI + t)
    return one_hot((j == source) & (s < CHI) & (t < CHI))


def swapped_tiles(x, fold, other=None):
    lane_group = group(iota((PAD, 128), 1))
    zero = jnp.zeros((PAD, 128), x.dtype)

    def tile(array, p, side):
        return array[p * PAD : (p + 1) * PAD, side * 128 : side * 128 + 128] if p < CHI else zero

    sources, span = {}, 8 if other is None else 4
    high = lax.bitwise_and(lane_group, 4) != 0
    for p in range(CHI if other is None else PAD):
        for side in range(2):
            if other is None:
                sources[p, side] = tile(x, p, side)
            elif p & 4:
                sources[p, side] = jnp.where(high, tile(x, p, side), tile(other, p ^ 4, side))
            else:
                sources[p, side] = jnp.where(high, tile(other, p ^ 4, side), tile(x, p, side))
    tiles = []
    for s in range(CHI):
        pair = []
        for side in range(2):
            lift = FOLD // PAD if fold and side and s >= CHI // 2 else 0
            out = zero
            for p in range(span):
                source = (side * 8 + (s & 7 & -span)) | p
                if other is None and source >= CHI:
                    continue
                shift = (p + lift - s % span) % 8 * PAD
                piece = sources[source, s >> 3]
                piece = pltpu.roll(piece, shift, 1) if shift else piece
                here = lax.bitwise_and(lane_group, span - 1) == p
                if lift:
                    here = lane_group == p + lift
                out = jnp.where(here, piece, out)
            pair.append(out)
        tiles.append(pair)
    return tiles


def block_swap(x, other=None):
    tiles = swapped_tiles(x, False, other)
    return jnp.concatenate([jnp.concatenate(pair, axis=1) for pair in tiles], axis=0)


def joined(x):
    x = spaced(x)
    lane = iota((PAD, 128), 1)
    sides = []
    for k in range(CHI):
        at = ROWS + (k >> 3) * PAD
        shift = -(k & 7) * PAD % 128
        side = pltpu.roll(x[at : at + PAD], shift, 1) if shift else x[at : at + PAD]
        sides.append(jnp.where(lane < PAD, side, jnp.zeros_like(side)))
    return jnp.concatenate([x[:ROWS], jnp.concatenate(sides, axis=0)], axis=1)


def split(x):
    lane_group = group(iota((PAD, 128), 1))
    tails = [jnp.zeros((PAD, 128), x.dtype)] * 2
    for k in range(CHI):
        block = x[k * PAD : (k + 1) * PAD, 128:]
        tails[k >> 3] = jnp.where(lane_group == (k & 7), block, tails[k >> 3])
    return jnp.concatenate([x[:, :128], *tails], axis=0)


def product_both(a, b, scale=None):
    zero = jnp.zeros((PAD, b.shape[1]), b.dtype)
    blocks = [b[s * PAD : (s + 1) * PAD] if s < CHI else zero for s in range(PAD)]
    plain = mm(a, jnp.concatenate(blocks, axis=0), NT)
    moved = mm(a, jnp.concatenate([blocks[s ^ 4] for s in range(PAD)], axis=0), NT)
    if scale is not None:
        plain, moved = plain * scale, moved * scale
    return plain.astype(BF16), moved.astype(BF16)


def widen(x):
    return jnp.concatenate([x, jnp.zeros((x.shape[0], LANES - x.shape[1]), x.dtype)], axis=1)


def parts3(x):
    a = x.astype(BF16)
    rest = x - a.astype(F32)
    b = rest.astype(BF16)
    c = (rest - b.astype(F32)).astype(BF16)
    return jnp.concatenate([a, b, c], axis=0)


def parts2(x):
    a = x.astype(BF16)
    return jnp.concatenate([a, (x - a.astype(F32)).astype(BF16)], axis=0)


def fold2(y):
    n = y.shape[0] // 2
    return y[n:] + y[:n]


def fold3(y):
    n = y.shape[0] // 3
    return (y[2 * n :] + y[n : 2 * n]) + y[:n]


def folded(first, last):
    return jnp.where(iota(first.shape, 1) < FOLD, first, last)


def compact(x):
    blocks = x.shape[0] // PAD
    legs = x.astype(F32).reshape(blocks, PAD, 128)[:, :CHI]
    return legs.reshape(blocks * CHI, 128).astype(BF16)


def spaced(x):
    blocks = x.shape[0] // CHI
    legs = x.astype(F32).reshape(blocks, CHI, 128)
    rest = jnp.zeros((blocks, PAD - CHI, 128), F32)
    return jnp.concatenate([legs, rest], axis=1).reshape(blocks * PAD, 128).astype(BF16)


def unfold(x):
    side = x[ROWS:]
    low = iota(side.shape, 1) < FOLD
    zero = jnp.zeros_like(side)
    first = jnp.where(low, side, zero)
    last = jnp.where(low, pltpu.roll(side, 128 - FOLD, 1), zero)
    return jnp.concatenate([x[:ROWS], jnp.concatenate([first, last], axis=0)], axis=1)


def row_swap(x):
    legs = x.astype(F32).reshape(CHI, PAD, x.shape[1])[:, :CHI]
    turned = jnp.transpose(legs, (1, 0, 2))
    rest = jnp.zeros((CHI, PAD - CHI, x.shape[1]), F32)
    return jnp.concatenate([turned, rest], axis=1).reshape(x.shape).astype(BF16)


def product_part(x, scale=None):
    return block_swap(*product_both(row_swap(x), x, scale))


def outer_part(first, second):
    outer, moved = product_both(first, row_swap(second))
    tiles = swapped_tiles(outer, True, moved)
    half = CHI // 2
    side = folded(*(jnp.concatenate([t[1] for t in part], axis=0) for part in (tiles[:half], tiles[half:])))
    return compact(jnp.concatenate([t[0] for t in tiles] + [side], axis=0))


def turn(first, compact_lanes):
    if not compact_lanes:
        return widen(row_swap(first.T[:ROWS]))
    legs = first.T[: CHI * CHI].astype(F32).reshape(CHI, CHI, ROWS)
    rest = jnp.zeros((CHI, PAD - CHI, ROWS), F32)
    legs = jnp.concatenate([jnp.transpose(legs, (1, 0, 2)), rest], axis=1)
    return widen(legs.reshape(ROWS, ROWS).astype(BF16))


def start_body(start, swap):
    start = jnp.concatenate([start, jnp.zeros((PAD - CHI, CHI * CHI), F32)], axis=0)
    pieces = parts3(start)
    spread = spread_matrix(False)
    plain = mm(pieces, spread)
    turned = mm(plain.astype(BF16), swap)
    return fold3(plain), fold3(turned)


def row_products(y):
    pieces = parts2(y)
    high, low = pieces[:PAD], pieces[PAD:]
    gram = fold2(mm(pieces, high, NT)) + mm(high, low, NT)
    return [jnp.broadcast_to(gram[:, k : k + 1], (PAD, 128)) for k in range(CHI)]


def line(x, k):
    return jnp.broadcast_to(x[k : k + 1, :], x.shape)


def twice(x, width):
    return jnp.concatenate([x] * (width // 128), axis=1)


def exact_orthonormal(y):
    cols = row_products(y)
    row = iota((PAD, 128), 0)
    scale = jnp.zeros((PAD, 128), F32)
    for k in range(CHI):
        inverse = lax.rsqrt(line(cols[k], k))
        scale = jnp.where(row == k, inverse, scale)
        factor = jnp.where(row > k, cols[k] * (inverse * inverse), 0.0)
        for j in range(k + 1, CHI):
            cols[j] = cols[j] - factor * line(cols[j], k)
        y = y - twice(factor, y.shape[1]) * line(y, k)
    return y * twice(scale, y.shape[1])


def orthonormal(y):
    cols = row_products(y)
    width = y.shape[1]
    row = iota((PAD, 128), 0)
    floors = [line(cols[k], k) * PIVOT for k in range(CHI)]
    scale, inner = jnp.zeros((PAD, 128), F32), jnp.zeros((PAD, 128), F32)
    good = jnp.ones((PAD, 128), F32)
    for k in range(0, CHI, 2):
        here, after = cols[k], cols[k + 1]
        top, side, low = line(here, k), line(here, k + 1), line(after, k + 1)
        det = top * low - side * side
        good = jnp.where((top >= floors[k]) & (det >= floors[k + 1] * top), good, 0.0)
        over, rest = 1.0 / det, row > k + 1
        first = jnp.where(rest, (low * here - side * after) * over, 0.0)
        second = jnp.where(rest, (top * after - side * here) * over, 0.0)
        for j in range(k + 2, CHI):
            cols[j] = cols[j] - first * line(cols[j], k) - second * line(cols[j], k + 1)
        y = y - twice(first, width) * line(y, k) - twice(second, width) * line(y, k + 1)
        scale = jnp.where(row == k, lax.rsqrt(top), scale)
        scale = jnp.where(row == k + 1, lax.rsqrt(det / top), scale)
        inner = jnp.where(row == k + 1, side / top, inner)
    y = y - twice(inner, width) * pltpu.roll(y, 1, 0)
    return y * twice(scale, width), good


def exact_iso(own, other, start, start_turned, shift, swap):
    pieces = parts3(start)
    image = fold3(mm(pieces, own, NT) + mm(pieces, other, NT))
    basis = exact_orthonormal(widen(image) + shift * start_turned)
    pieces = parts3(basis)
    image = fold3(mm(pieces[:, :ROWS], own) + mm(pieces[:, :ROWS], other))
    return exact_orthonormal(image + shift * fold3(mm(pieces, swap)))


def iso_kernel(own, other, starts, pieces, iso_o):
    swap = swap_matrix()
    grams = [spaced(own[...]), spaced(other[...])]
    doubled = [
        jnp.concatenate([g[:ROWS], jnp.concatenate([g[ROWS:]] * 2, axis=0)], axis=1) for g in grams
    ]
    total = doubled[0].astype(F32) + doubled[1].astype(F32)
    i, j = iota((ROWS, LANES), 0), iota((ROWS, LANES), 1)
    place = jnp.where(j < 128, j, 128 + lax.bitwise_and(j, FOLD - 1))
    valid = (j < 128) | ((lax.bitwise_and(j, 127) < FOLD) == (i < ROWS // 2))
    diagonal = valid & (group(i) == minor(place)) & (minor(i) == group(place))
    trace = jnp.sum(jnp.where(diagonal, total, 0.0), axis=0, keepdims=True)
    shift = jnp.sum(trace, axis=1, keepdims=True) / (CHI * CHI)
    unit = 1.0 / shift
    image = mm(pieces[...], doubled[0], NT) + mm(pieces[...], doubled[1], NT)
    lane = iota((2 * PAD, ROWS), 1)
    image = jnp.where(lane < ROWS // 2, image[: 2 * PAD], image[2 * PAD :])
    image = widen(fold2(image)) * unit + starts[PAD:]
    parts = parts2(image)
    own, other = unfold(grams[0]), unfold(grams[1])
    image = fold2(mm(parts[:, :ROWS], own) + mm(parts[:, :ROWS], other)) * unit
    basis, good = orthonormal(image + fold2(mm(parts, swap)))
    iso_o[...] = basis.astype(BF16)

    @pl.when(jnp.logical_not(good[0, 0] > 0.5))
    def _():
        basis = exact_iso(own, other, starts[:PAD], starts[PAD:], shift, swap)
        iso_o[...] = basis.astype(BF16)


def packed_pair(index):
    entry = jnp.where(index < 128, index, 128 + minor(index))
    s = lax.shift_right_logical(entry * 171, 11)
    return s, entry - s * CHI


def packing(compact_lanes):
    s, t = packed_pair(iota((LANES, LANES), 1))
    j = iota((LANES, LANES), 0)
    return one_hot(j == (s * CHI + t if compact_lanes else s * PAD + t))


def first_second(turned, lower, left, second_ref, first_ref):
    lane = iota((PAD, LANES), 1)
    masked = [jnp.where(group(lane) == k, left.astype(F32), 0.0) for k in range(CHI)]
    masked = jnp.concatenate(masked, axis=0).astype(BF16)
    i, j = iota((LANES, LANES), 0), iota((LANES, LANES), 1)
    values = mm(masked, one_hot(minor(i) == group(j)))
    eye = minor(lane) == iota((PAD, LANES), 0)
    for a in range(CHI):
        blocks = []
        for k in range(CHI):
            line = jnp.broadcast_to(values[k * PAD + a : k * PAD + a + 1, :], (PAD, LANES))
            blocks.append(jnp.where(eye, line, 0.0).astype(BF16))
        kron = jnp.concatenate(blocks, axis=0)
        first = mm(turned[:, :ROWS], kron)
        first_ref[a * ROWS : (a + 1) * ROWS, :] = first.astype(BF16)
    second = mm(first_ref[:, :ROWS], lower).astype(BF16)
    lane_group = group(iota((PAD, 128), 1))
    for a in range(CHI):
        rows = slice(a * PAD, (a + 1) * PAD)
        tails = [jnp.zeros((PAD, 128), BF16)] * 2
        for k in range(CHI):
            block = second[a * ROWS + k * PAD : a * ROWS + (k + 1) * PAD]
            second_ref[rows, k * 128 : (k + 1) * 128] = block[:, :128]
            tails[k >> 3] = jnp.where(lane_group == (k & 7), block[:, 128:], tails[k >> 3])
        for side in range(2):
            at = (CHI + side) * 128
            second_ref[rows, at : at + 128] = tails[side]


def third(second_ref, right, kron_ref, packed):
    lane = iota((CHI * CHI, LANES), 1)
    if packed:
        right = right.astype(F32)
        rest = jnp.concatenate([right[128 % CHI : CHI], right[:CHI]], axis=0)
        rows = [right[:CHI]] * (128 // CHI) + [right[: 128 % CHI]] + [rest] * 8
        values = jnp.concatenate(rows, axis=0).astype(BF16)
        lane_group = packed_pair(lane)[0]
    else:
        values = jnp.concatenate([right] * PAD, axis=0)
        lane_group = jnp.minimum(group(lane), CHI)
    values = values.T.astype(F32)
    entry = iota((CHI * CHI, LANES), 0)
    kept = lax.shift_right_logical(entry * 171, 11) == lane_group
    for k in range(CHI):
        block = values[k * PAD : k * PAD + CHI, :]
        tall = jnp.concatenate([block] * CHI, axis=0)
        tall = jnp.where(kept, tall, 0.0).astype(BF16)
        kron_ref[k * 128 : (k + 1) * 128, :] = tall[:128]
        at = CHI * 128 + k * PAD
        kron_ref[at : at + PAD, :] = tall[128:]
    used = CHI * 128 + CHI * PAD
    kron_ref[used:, :] = jnp.zeros((SECOND - used, LANES), BF16)
    return mm(second_ref[...], kron_ref[...])


def placed(site, mirror, lower):
    legs = site.astype(F32).reshape(CHI, CHI, CHI * CHI)
    legs = jnp.where(lower, jnp.transpose(legs, (1, 0, 2)), legs)
    rest = jnp.zeros((CHI, PAD - CHI, CHI * CHI), F32)
    rows = jnp.concatenate([legs, rest], axis=1).reshape(ROWS, CHI * CHI).astype(BF16)
    return block_swap(mm(rows, spread_matrix(mirror)).astype(BF16))


def pick(own_first, own, other):
    return jnp.where(own_first, own, other), jnp.where(own_first, other, own)


def roles(level):
    row = lax.axis_index("row")
    own_lower = row >> level & 1
    first_upper = row >> level + 1 & 1 if level < LEVELS - 1 else row * 0 + 1
    flags = own_lower ^ first_upper, first_upper, own_lower, mirrored(row)
    return [flag != 0 for flag in flags]


def cast_kernel(own, cast_o):
    cast_o[...] = own[...].astype(BF16)


def first_gram_kernel(own, other, mine_o, theirs_o, gram_o):
    own_first, _, own_lower, mirror = roles(0)
    mine = placed(own[...], mirror, own_lower)
    theirs = placed(other[...].astype(BF16), mirror, jnp.logical_not(own_lower))
    mine_o[...], theirs_o[...] = mine, theirs
    products = pick(own_first, product_part(mine), product_part(theirs))
    gram_o[...] = outer_part(*products)


def mean_square(lines):
    mean = jnp.sum(lines, axis=1, keepdims=True) / (CHI**4) + 1e-06
    return jnp.broadcast_to(mean, (8, 128))


def scaled_product(x):
    mean = mean_square(jnp.sum(jnp.square(x.astype(F32)), axis=0, keepdims=True))
    return product_part(x, twice(1.0 / mean[:1], LANES)), mean


def own_kernel(own, wide_o, product_o, mean_o):
    wide = joined(own[...])
    wide_o[...] = wide
    product_o[...], mean_o[...] = scaled_product(wide)


def gram_kernel(level, product, mean, other, gram_o, scale_o):
    other_product, other_mean = scaled_product(joined(other[...]))
    gram_o[...] = outer_part(*pick(roles(level)[0], product[...], other_product))
    scale_o[...] = lax.rsqrt(mean[...]) * lax.rsqrt(other_mean)


def turn_kernel(level, own, other, start, turned_o, lower_o, starts_o, pieces_o):
    later = level > 0
    own_first, first_upper, _, _ = roles(level)
    first, second = pick(own_first, own[...], joined(other[...]) if later else other[...])
    turned_o[...] = turn(first, later)
    lower_o[...] = mm(second, packing(later)).astype(BF16)
    plain, turned = start_body(start[level], swap_matrix())
    here = jnp.where(first_upper, plain, turned)
    starts_o[:PAD] = here
    starts_o[PAD:] = jnp.where(first_upper, turned, plain)
    pieces = parts2(here)
    pieces_o[: 2 * PAD] = pieces
    lifted = pltpu.roll(pieces[:, 128:], FOLD, 1)
    pieces_o[2 * PAD :] = jnp.concatenate([pieces[:, :128], lifted], axis=1)


def second_kernel(turned, lower, left, second_o, first):
    first_second(turned[...], lower[...], left[...], second_o, first)


def third_kernel(second, right, *refs):
    *scales, next_o, kron = refs
    merged = split(third(second, right[...], kron, True))
    for scale in scales:
        merged = merged * scale[:1]
    next_o[...] = compact(merged)


def last_kernel(second, right, scale, *refs):
    *means, coarse_o, log_o, kron = refs
    merged = third(second, right[...], kron, False) * twice(scale[:1], LANES)
    mean = mean_square(jnp.sum(merged * merged, axis=0, keepdims=True))
    log_o[...] = 0.5 * sum(jnp.log(m[:1, :1]) for m in [*means, mean])
    wide = block_swap(merged.astype(BF16))
    narrow = mm(wide, gather_matrix(roles(LEVELS - 1)[3]))
    narrow = narrow * twice(lax.rsqrt(mean[:1]), LANES)[:, : CHI * CHI]
    legs = jnp.transpose(narrow.reshape(CHI, PAD, CHI * CHI)[:, :CHI], (1, 0, 2))
    coarse_o[...] = legs.reshape(CHI * CHI, CHI * CHI)


def call(kernel, outs, scratch=()):
    vmem = pl.BlockSpec(memory_space=pltpu.VMEM)

    def run(*args):
        return pl.pallas_call(
            kernel,
            out_shape=[jax.ShapeDtypeStruct(s, d) for s, d in outs],
            in_specs=[vmem] * len(args),
            out_specs=[vmem] * len(outs),
            scratch_shapes=list(scratch),
            compiler_params=pltpu.CompilerParams(vmem_limit_bytes=VMEM_BYTES),
            cost_estimate=pl.CostEstimate(flops=10**8, bytes_accessed=10**6, transcendentals=0),
        )(*args)

    return run


def from_partner(array, flip):
    count = lax.axis_size("row")
    return lax.ppermute(array, "row", [(i, i ^ flip) for i in range(count)])


def mirrored(row):
    parity = row * 0
    for bit in range(LEVELS):
        parity = parity ^ (row >> bit & 1)
    return parity


def from_bond(array):
    rows, cols = lax.axis_size("row"), lax.axis_size("col")
    pairs = []
    for i in range(rows):
        for c in range(cols):
            target = (c + 1) % cols if mirrored(i) else (c - 1) % cols
            pairs.append((i * cols + c, (i ^ 1) * cols + target))
    return lax.ppermute(array, ("row", "col"), pairs)


def per_device(site_tensors, start_basis):
    square = CHI * CHI
    mat, one = ((ROWS, LANES), BF16), ((8, 128), F32)
    gram_shape = ((CHI * CHI * 3 // 2, 128), BF16)
    sent = ((CHI * (CHI + 2), 128), BF16)
    kron, firsts = [pltpu.VMEM((SECOND, LANES), BF16)], [pltpu.VMEM((CHI * ROWS, LANES), BF16)]
    scales, means = [], []
    own = site_tensors[0, 0]
    for level in range(LEVELS):
        if level == 0:
            other = from_partner(own, 1)
            (own,) = call(cast_kernel, [((square, square), BF16)])(own)
            own, other, gram = call(first_gram_kernel, [mat, mat, gram_shape])(own, other)
        else:
            other = from_partner(own, 1 << level | 1)
            own, product, mean = call(own_kernel, [mat, mat, one])(own)
            gram, scale = call(functools.partial(gram_kernel, level), [gram_shape, one])(
                product, mean, other
            )
            scales, means = [scale], [*means, mean]
        gram_other = from_bond(gram)
        turned, lower, starts, pieces = call(
            functools.partial(turn_kernel, level),
            [mat, mat, ((2 * PAD, LANES), F32), ((4 * PAD, LANES), BF16)],
        )(own, other, start_basis)
        (left,) = call(iso_kernel, [((PAD, LANES), BF16)])(gram, gram_other, starts, pieces)
        right = from_partner(left, 1)
        (second,) = call(second_kernel, [((ROWS, SECOND), BF16)], firsts)(turned, lower, left)
        if level < LEVELS - 1:
            (own,) = call(third_kernel, [sent], kron)(second, right, *scales)
        else:
            coarse, log_total = call(last_kernel, [((square, square), F32), ((1, 1), F32)], kron)(
                second, right, *scales, *means
            )
    return (coarse[None, None], log_total)


def solution(mesh):
    return jax.shard_map(
        per_device,
        mesh=mesh,
        in_specs=(P("row", "col", None, None), P()),
        out_specs=(P("row", "col", None, None), P("row", "col")),
        check_vma=False,
    )
```

```python
import functools

import functools

import jax
import jax.numpy as jnp
from jax import lax
from jax.experimental import pallas as pl
from jax.experimental.pallas import tpu as pltpu
from jax.sharding import PartitionSpec as P

CHI = 12
LEVELS = 3
SWEEPS = 2
PAD = 16
SHIFT = 4
ROWS = CHI * PAD
LANES = PAD * PAD
VMEM_BYTES = 8 << 20
SECOND = (CHI + 2) * 128
PIVOT = 1.0 / 64
F32 = jnp.float32
BF16 = jnp.bfloat16

NN = (((1,), (0,)), ((), ()))
NT = (((1,), (1,)), ((), ()))
TN = (((0,), (0,)), ((), ()))


def mm(a, b, dims=NN):
    return lax.dot_general(a, b, dims, preferred_element_type=F32)


def iota(shape, dim):
    return lax.broadcasted_iota(jnp.int32, shape, dim)


def group(index):
    return lax.shift_right_logical(index, SHIFT)


def minor(index):
    return lax.bitwise_and(index, PAD - 1)


def one_hot(mask):
    return jnp.where(mask, 1.0, 0.0).astype(BF16)


def spread_matrix(mirror):
    i, j = iota((CHI * CHI, LANES), 0), iota((CHI * CHI, LANES), 1)
    s, t = group(j), minor(j)
    source = jnp.where(mirror, t * CHI + s, s * CHI + t)
    return one_hot((i == source) & (s < CHI) & (t < CHI))


def gather_matrix(mirror):
    i, j = iota((LANES, CHI * CHI), 0), iota((LANES, CHI * CHI), 1)
    s, t = group(i), minor(i)
    source = jnp.where(mirror, t * CHI + s, s * CHI + t)
    return one_hot((j == source) & (s < CHI) & (t < CHI))


def swapped_tiles(x, other=None):
    lane_group = group(iota((PAD, 128), 1))
    zero = jnp.zeros((PAD, 128), x.dtype)

    def tile(array, p, side):
        return array[p * PAD : (p + 1) * PAD, side * 128 : side * 128 + 128] if p < CHI else zero

    sources, span = {}, 8 if other is None else 4
    high = lax.bitwise_and(lane_group, 4) != 0
    for p in range(CHI if other is None else PAD):
        for side in range(2):
            if other is None:
                sources[p, side] = tile(x, p, side)
            elif p & 4:
                sources[p, side] = jnp.where(high, tile(x, p, side), tile(other, p ^ 4, side))
            else:
                sources[p, side] = jnp.where(high, tile(other, p ^ 4, side), tile(x, p, side))
    tiles = []
    for s in range(CHI):
        pair = []
        for side in range(2):
            out = zero
            for p in range(span):
                source = (side * 8 + (s & 7 & -span)) | p
                if other is None and source >= CHI:
                    continue
                shift = (p - s % span) % 8 * PAD
                piece = sources[source, s >> 3]
                piece = pltpu.roll(piece, shift, 1) if shift else piece
                out = jnp.where(lax.bitwise_and(lane_group, span - 1) == p, piece, out)
            pair.append(out)
        tiles.append(pair)
    return tiles


def block_swap(x, other=None):
    tiles = swapped_tiles(x, other)
    return jnp.concatenate([jnp.concatenate(pair, axis=1) for pair in tiles], axis=0)


def joined(x):
    x = spaced(x)
    lane = iota((PAD, 128), 1)
    sides = []
    for k in range(CHI):
        at = ROWS + (k >> 3) * PAD
        shift = -(k & 7) * PAD % 128
        side = pltpu.roll(x[at : at + PAD], shift, 1) if shift else x[at : at + PAD]
        sides.append(jnp.where(lane < PAD, side, jnp.zeros_like(side)))
    return jnp.concatenate([x[:ROWS], jnp.concatenate(sides, axis=0)], axis=1)


def split(x):
    lane_group = group(iota((PAD, 128), 1))
    tails = [jnp.zeros((PAD, 128), x.dtype)] * 2
    for k in range(CHI):
        block = x[k * PAD : (k + 1) * PAD, 128:]
        tails[k >> 3] = jnp.where(lane_group == (k & 7), block, tails[k >> 3])
    return jnp.concatenate([x[:, :128], *tails], axis=0)


def product_both(a, b, scale=None):
    zero = jnp.zeros((PAD, b.shape[1]), b.dtype)
    blocks = [b[s * PAD : (s + 1) * PAD] if s < CHI else zero for s in range(PAD)]
    plain = mm(a, jnp.concatenate(blocks, axis=0), NT)
    moved = mm(a, jnp.concatenate([blocks[s ^ 4] for s in range(PAD)], axis=0), NT)
    if scale is not None:
        plain, moved = plain * scale, moved * scale
    return plain.astype(BF16), moved.astype(BF16)


def widen(x):
    return jnp.concatenate([x, jnp.zeros((x.shape[0], LANES - x.shape[1]), x.dtype)], axis=1)


def parts3(x):
    a = x.astype(BF16)
    rest = x - a.astype(F32)
    b = rest.astype(BF16)
    c = (rest - b.astype(F32)).astype(BF16)
    return jnp.concatenate([a, b, c], axis=0)


def parts2(x):
    a = x.astype(BF16)
    return jnp.concatenate([a, (x - a.astype(F32)).astype(BF16)], axis=0)


def fold2(y):
    n = y.shape[0] // 2
    return y[n:] + y[:n]


def fold3(y):
    n = y.shape[0] // 3
    return (y[2 * n :] + y[n : 2 * n]) + y[:n]


def compact(x):
    blocks = x.shape[0] // PAD
    legs = x.astype(F32).reshape(blocks, PAD, 128)[:, :CHI]
    return legs.reshape(blocks * CHI, 128).astype(BF16)


def spaced(x):
    blocks = x.shape[0] // CHI
    legs = x.astype(F32).reshape(blocks, CHI, 128)
    rest = jnp.zeros((blocks, PAD - CHI, 128), F32)
    return jnp.concatenate([legs, rest], axis=1).reshape(blocks * PAD, 128).astype(BF16)


def joined(x):
    x = spaced(x)
    lane = iota((PAD, 128), 1)
    sides = []
    for k in range(CHI):
        at = ROWS + (k >> 3) * PAD
        shift = -(k & 7) * PAD % 128
        side = pltpu.roll(x[at : at + PAD], shift, 1) if shift else x[at : at + PAD]
        sides.append(jnp.where(lane < PAD, side, jnp.zeros_like(side)))
    return jnp.concatenate([x[:ROWS], jnp.concatenate(sides, axis=0)], axis=1)


def split(x):
    lane_group = group(iota((PAD, 128), 1))
    tails = [jnp.zeros((PAD, 128), x.dtype)] * 2
    for k in range(CHI):
        block = x[k * PAD : (k + 1) * PAD, 128:]
        tails[k >> 3] = jnp.where(lane_group == (k & 7), block, tails[k >> 3])
    return jnp.concatenate([x[:, :128], *tails], axis=0)


def product_both(a, b, scale=None):
    zero = jnp.zeros((PAD, b.shape[1]), b.dtype)
    blocks = [b[s * PAD : (s + 1) * PAD] if s < CHI else zero for s in range(PAD)]
    plain = mm(a, jnp.concatenate(blocks, axis=0), NT)
    moved = mm(a, jnp.concatenate([blocks[s ^ 4] for s in range(PAD)], axis=0), NT)
    if scale is not None:
        plain, moved = plain * scale, moved * scale
    return plain.astype(BF16), moved.astype(BF16)


def widen(x):
    return jnp.concatenate([x, jnp.zeros((x.shape[0], LANES - x.shape[1]), x.dtype)], axis=1)


def parts3(x):
    a = x.astype(BF16)
    rest = x - a.astype(F32)
    b = rest.astype(BF16)
    c = (rest - b.astype(F32)).astype(BF16)
    return jnp.concatenate([a, b, c], axis=0)


def parts2(x):
    a = x.astype(BF16)
    return jnp.concatenate([a, (x - a.astype(F32)).astype(BF16)], axis=0)


def fold2(y):
    n = y.shape[0] // 2
    return y[n:] + y[:n]


def fold3(y):
    n = y.shape[0] // 3
    return (y[2 * n :] + y[n : 2 * n]) + y[:n]


def compact(x):
    blocks = x.shape[0] // PAD
    legs = x.astype(F32).reshape(blocks, PAD, 128)[:, :CHI]
    return legs.reshape(blocks * CHI, 128).astype(BF16)


def spaced(x):
    blocks = x.shape[0] // CHI
    legs = x.astype(F32).reshape(blocks, CHI, 128)
    rest = jnp.zeros((blocks, PAD - CHI, 128), F32)
    return jnp.concatenate([legs, rest], axis=1).reshape(blocks * PAD, 128).astype(BF16)


def unfold(x):
    side = x[ROWS:]
    low = iota(side.shape, 1) < FOLD
    zero = jnp.zeros_like(side)
    first = jnp.where(low, side, zero)
    last = jnp.where(low, pltpu.roll(side, 128 - FOLD, 1), zero)
    return jnp.concatenate([x[:ROWS], jnp.concatenate([first, last], axis=0)], axis=1)


def row_swap(x):
    legs = x.astype(F32).reshape(CHI, PAD, x.shape[1])[:, :CHI]
    turned = jnp.transpose(legs, (1, 0, 2))
    rest = jnp.zeros((CHI, PAD - CHI, x.shape[1]), F32)
    return jnp.concatenate([turned, rest], axis=1).reshape(x.shape).astype(BF16)


def product_part(x, scale=None):
    return block_swap(*product_both(row_swap(x), x, scale))


def outer_part(first, second):
    outer = widen(mm(first, row_swap(second), NT).astype(BF16))
    lane = iota((PAD, 128), 1)
    tiles = []
    for s in range(CHI):
        tile = jnp.zeros((PAD, 128), BF16)
        for p in range(128 // CHI + 1):
            at = (s >> 3) * 128
            piece = outer[p * PAD : (p + 1) * PAD, at : at + 128]
            shift = (p * CHI - (s & 7) * PAD) % 128
            piece = pltpu.roll(piece, shift, 1) if shift else piece
            tile = jnp.where((lane >= p * CHI) & (lane < p * CHI + CHI), piece, tile)
        tiles.append(tile)
    cut = CHI * (CHI - 1) - 128
    for side in range(2):
        pieces = [outer[p * PAD : (p + 1) * PAD, side * 128 : side * 128 + 128] for p in (CHI - 2, CHI - 1)]
        before = pltpu.roll(pieces[0], (cut - CHI) % 128, 1)
        tiles.append(jnp.where(minor(lane) < cut, before, pltpu.roll(pieces[1], cut, 1)))
    return compact(jnp.concatenate(tiles, axis=0))


def turn(first, compact_lanes):
    if not compact_lanes:
        return widen(row_swap(first.T[:ROWS]))
    legs = first.T[: CHI * CHI].astype(F32).reshape(CHI, CHI, ROWS)
    rest = jnp.zeros((CHI, PAD - CHI, ROWS), F32)
    legs = jnp.concatenate([jnp.transpose(legs, (1, 0, 2)), rest], axis=1)
    return widen(legs.reshape(ROWS, ROWS).astype(BF16))


def quotient(index):
    return lax.shift_right_logical(index * 171, 11)


def natural_matrix():
    i, j = iota((LANES, LANES), 0), iota((LANES, LANES), 1)
    return one_hot((j == minor(i) * CHI + group(i)) & (minor(i) < CHI) & (group(i) < CHI))


def start_body(start, first_upper):
    start = jnp.concatenate([start, jnp.zeros((PAD - CHI, CHI * CHI), F32)], axis=0)
    pieces = parts3(start)
    i, j = iota((CHI * CHI, LANES), 0), iota((CHI * CHI, LANES), 1)
    s = quotient(j)
    swapped = fold3(mm(pieces, one_hot((i == (j - s * CHI) * CHI + s) & (s < CHI))))
    turned = fold3(mm(pieces, spread_matrix(first_upper)))
    return jnp.where(first_upper, widen(start), swapped), turned


def row_products(y):
    pieces = parts2(y)
    high, low = pieces[:PAD], pieces[PAD:]
    gram = fold2(mm(pieces, high, NT)) + mm(high, low, NT)
    return [jnp.broadcast_to(gram[:, k : k + 1], (PAD, 128)) for k in range(CHI)]


def line(x, k):
    return jnp.broadcast_to(x[k : k + 1, :], x.shape)


def twice(x, width):
    return jnp.concatenate([x] * (width // 128), axis=1)


def exact_orthonormal(y):
    cols = row_products(y)
    row = iota((PAD, 128), 0)
    scale = jnp.zeros((PAD, 128), F32)
    for k in range(CHI):
        inverse = lax.rsqrt(line(cols[k], k))
        scale = jnp.where(row == k, inverse, scale)
        factor = jnp.where(row > k, cols[k] * (inverse * inverse), 0.0)
        for j in range(k + 1, CHI):
            cols[j] = cols[j] - factor * line(cols[j], k)
        y = y - twice(factor, y.shape[1]) * line(y, k)
    return y * twice(scale, y.shape[1])


def orthonormal(y):
    cols = row_products(y)
    width = y.shape[1]
    row = iota((PAD, 128), 0)
    floors = [line(cols[k], k) * PIVOT for k in range(CHI)]
    scale, inner = jnp.zeros((PAD, 128), F32), jnp.zeros((PAD, 128), F32)
    good = jnp.ones((PAD, 128), F32)
    for k in range(0, CHI, 2):
        here, after = cols[k], cols[k + 1]
        top, side, low = line(here, k), line(here, k + 1), line(after, k + 1)
        det = top * low - side * side
        good = jnp.where((top >= floors[k]) & (det >= floors[k + 1] * top), good, 0.0)
        over, rest = 1.0 / det, row > k + 1
        first = jnp.where(rest, (low * here - side * after) * over, 0.0)
        second = jnp.where(rest, (top * after - side * here) * over, 0.0)
        for j in range(k + 2, CHI):
            cols[j] = cols[j] - first * line(cols[j], k) - second * line(cols[j], k + 1)
        y = y - twice(first, width) * line(y, k) - twice(second, width) * line(y, k + 1)
        scale = jnp.where(row == k, lax.rsqrt(top), scale)
        scale = jnp.where(row == k + 1, lax.rsqrt(det / top), scale)
        inner = jnp.where(row == k + 1, side / top, inner)
    y = y - twice(inner, width) * pltpu.roll(y, 1, 0)
    return y * twice(scale, width), good


def exact_iso(own, other, start, start_turned, shift, natural):
    pieces = parts3(start)
    image = fold3(mm(pieces, own, NT) + mm(pieces, other, NT))
    basis = exact_orthonormal(widen(image) + shift * start_turned)
    pieces = parts3(basis)
    image = fold3(mm(pieces[:, :ROWS], own) + mm(pieces[:, :ROWS], other))
    return exact_orthonormal(image + shift * fold3(mm(pieces, natural)))


def first_image(gram, pieces):
    gram = spaced(gram)
    shared = [gram[ROWS : ROWS + PAD]] * 8 + [gram[ROWS + PAD :]] * (CHI - 8)
    shared = jnp.concatenate([gram[:ROWS], jnp.concatenate(shared, axis=0)], axis=1)
    i, j = iota((ROWS, LANES), 0), iota((ROWS, LANES), 1)
    entry = minor(i) * CHI + group(i)
    place = jnp.where(entry < 128, entry, entry + lax.bitwise_and(group(i), 7) * PAD)
    diagonal = (j == place) & (minor(i) < CHI)
    trace = jnp.sum(jnp.where(diagonal, shared.astype(F32), 0.0), axis=0, keepdims=True)
    images = mm(pieces, shared, NT)
    image = images[: 2 * PAD]
    block = lax.bitwise_and(group(iota((2 * PAD, ROWS), 1)), 7)
    for k in range(1, 8):
        image = jnp.where(block == k, images[2 * PAD * k : 2 * PAD * (k + 1)], image)
    return widen(fold2(image)), jnp.sum(trace, axis=1, keepdims=True)


def iso_kernel(own, own_image, own_trace, other, starts, pieces, iso_o):
    natural = natural_matrix()
    image, trace = first_image(other[...], pieces[...])
    shift = (own_trace[:1, :1] + trace) / (CHI * CHI)
    unit = 1.0 / shift
    image = (own_image[...] + image) * unit + starts[PAD:]
    parts = parts2(image)
    own, other = own[...], joined(other[...])
    image = fold2(mm(parts[:, :ROWS], own) + mm(parts[:, :ROWS], other)) * unit
    basis, good = orthonormal(image + fold2(mm(parts, natural)))
    iso_o[...] = basis.astype(BF16)

    @pl.when(jnp.logical_not(good[0, 0] > 0.5))
    def _():
        basis = exact_iso(own, other, starts[:PAD], starts[PAD:], shift, natural)
        iso_o[...] = basis.astype(BF16)


def packed_pair(index):
    entry = jnp.where(index < 128, index, 128 + minor(index))
    s = quotient(entry)
    return s, entry - s * CHI


def packing(compact_lanes):
    s, t = packed_pair(iota((LANES, LANES), 1))
    j = iota((LANES, LANES), 0)
    return one_hot(j == (s * CHI + t if compact_lanes else s * PAD + t))


def first_second(turned, lower, left, second_ref, first_ref):
    lane = iota((PAD, LANES), 1)
    masked = [jnp.where(quotient(lane) == k, left.astype(F32), 0.0) for k in range(CHI)]
    masked = jnp.concatenate(masked, axis=0).astype(BF16)
    i, j = iota((LANES, LANES), 0), iota((LANES, LANES), 1)
    values = mm(masked, one_hot(i - quotient(i) * CHI == group(j)))
    eye = minor(lane) == iota((PAD, LANES), 0)
    for a in range(CHI):
        blocks = []
        for k in range(CHI):
            line = jnp.broadcast_to(values[k * PAD + a : k * PAD + a + 1, :], (PAD, LANES))
            blocks.append(jnp.where(eye, line, 0.0).astype(BF16))
        kron = jnp.concatenate(blocks, axis=0)
        first = mm(turned[:, :ROWS], kron)
        first_ref[a * ROWS : (a + 1) * ROWS, :] = first.astype(BF16)
    second = mm(first_ref[:, :ROWS], lower).astype(BF16)
    lane_group = group(iota((PAD, 128), 1))
    for a in range(CHI):
        rows = slice(a * PAD, (a + 1) * PAD)
        tails = [jnp.zeros((PAD, 128), BF16)] * 2
        for k in range(CHI):
            block = second[a * ROWS + k * PAD : a * ROWS + (k + 1) * PAD]
            second_ref[rows, k * 128 : (k + 1) * 128] = block[:, :128]
            tails[k >> 3] = jnp.where(lane_group == (k & 7), block[:, 128:], tails[k >> 3])
        for side in range(2):
            at = (CHI + side) * 128
            second_ref[rows, at : at + 128] = tails[side]


def third(second_ref, right, kron_ref, packed):
    lane = iota((CHI * CHI, LANES), 1)
    if packed:
        right = right.astype(F32)
        rest = jnp.concatenate([right[128 % CHI : CHI], right[:CHI]], axis=0)
        rows = [right[:CHI]] * (128 // CHI) + [right[: 128 % CHI]] + [rest] * 8
        values = jnp.concatenate(rows, axis=0).astype(BF16)
        lane_group = packed_pair(lane)[0]
    else:
        values = jnp.concatenate([right] * PAD, axis=0)
        lane_group = jnp.minimum(group(lane), CHI)
    values = values.T.astype(F32)
    entry = iota((CHI * CHI, LANES), 0)
    kept = quotient(entry) == lane_group
    for k in range(CHI):
        block = values[k * CHI : (k + 1) * CHI, :]
        tall = jnp.concatenate([block] * CHI, axis=0)
        tall = jnp.where(kept, tall, 0.0).astype(BF16)
        kron_ref[k * 128 : (k + 1) * 128, :] = tall[:128]
        at = CHI * 128 + k * PAD
        kron_ref[at : at + PAD, :] = tall[128:]
    used = CHI * 128 + CHI * PAD
    kron_ref[used:, :] = jnp.zeros((SECOND - used, LANES), BF16)
    return mm(second_ref[...], kron_ref[...])


def placed(site, mirror, lower):
    legs = site.astype(F32).reshape(CHI, CHI, CHI * CHI)
    legs = jnp.where(lower, jnp.transpose(legs, (1, 0, 2)), legs)
    rest = jnp.zeros((CHI, PAD - CHI, CHI * CHI), F32)
    rows = jnp.concatenate([legs, rest], axis=1).reshape(ROWS, CHI * CHI).astype(BF16)
    return block_swap(mm(rows, spread_matrix(mirror)).astype(BF16))


def pick(own_first, own, other):
    return jnp.where(own_first, own, other), jnp.where(own_first, other, own)


def roles(level):
    row = lax.axis_index("row")
    own_lower = row >> level & 1
    first_upper = row >> level + 1 & 1 if level < LEVELS - 1 else row * 0 + 1
    flags = own_lower ^ first_upper, first_upper, own_lower, mirrored(row)
    return [flag != 0 for flag in flags]


def cast_kernel(own, cast_o):
    cast_o[...] = own[...].astype(BF16)


def first_gram_kernel(own, other, mine_o, theirs_o, gram_o):
    own_first, _, own_lower, mirror = roles(0)
    mine = placed(own[...], mirror, own_lower)
    theirs = placed(other[...].astype(BF16), mirror, jnp.logical_not(own_lower))
    mine_o[...], theirs_o[...] = mine, theirs
    products = pick(own_first, product_part(mine), product_part(theirs))
    gram_o[...] = outer_part(*products)


def mean_square(lines):
    mean = jnp.sum(lines, axis=1, keepdims=True) / (CHI**4) + 1e-06
    return jnp.broadcast_to(mean, (8, 128))


def scaled_product(x):
    mean = mean_square(jnp.sum(jnp.square(x.astype(F32)), axis=0, keepdims=True))
    return product_part(x, twice(1.0 / mean[:1], LANES)), mean


def own_kernel(own, wide_o, product_o, mean_o):
    wide = joined(own[...])
    wide_o[...] = wide
    product_o[...], mean_o[...] = scaled_product(wide)


def gram_kernel(level, product, mean, other, gram_o, scale_o):
    other_product, other_mean = scaled_product(joined(other[...]))
    gram_o[...] = outer_part(*pick(roles(level)[0], product[...], other_product))
    scale_o[...] = lax.rsqrt(mean[...]) * lax.rsqrt(other_mean)


def turn_kernel(
    level, own, other, gram, start, turned_o, lower_o, starts_o, pieces_o, wide_o, image_o, trace_o
):
    later = level > 0
    own_first, first_upper, _, _ = roles(level)
    first, second = pick(own_first, own[...], joined(other[...]) if later else other[...])
    turned_o[...] = turn(first, later)
    lower_o[...] = mm(second, packing(later)).astype(BF16)
    here, turned = start_body(start[level], first_upper)
    starts_o[:PAD], starts_o[PAD:] = here, turned
    parts = parts2(here)
    place = iota((2 * PAD, 128), 1)
    pieces = []
    for k in range(8):
        side = pltpu.roll(parts[:, 128:], k * PAD, 1) if k else parts[:, 128:]
        side = jnp.where(group(place) == k, side, jnp.zeros_like(side))
        pieces.append(jnp.concatenate([parts[:, :128], side], axis=1))
    pieces = jnp.concatenate(pieces, axis=0)
    pieces_o[...] = pieces
    wide_o[...] = joined(gram[...])
    image_o[...], trace = first_image(gram[...], pieces)
    trace_o[...] = jnp.broadcast_to(trace, trace_o.shape)


def second_kernel(turned, lower, left, second_o, first):
    first_second(turned[...], lower[...], left[...], second_o, first)


def third_kernel(second, right, *refs):
    *scales, next_o, kron = refs
    merged = split(third(second, right[...], kron, True))
    for scale in scales:
        merged = merged * scale[:1]
    next_o[...] = compact(merged)


def last_kernel(second, right, scale, *refs):
    *means, coarse_o, log_o, kron = refs
    merged = third(second, right[...], kron, False) * twice(scale[:1], LANES)
    mean = mean_square(jnp.sum(merged * merged, axis=0, keepdims=True))
    log_o[...] = 0.5 * sum(jnp.log(m[:1, :1]) for m in [*means, mean])
    wide = block_swap(merged.astype(BF16))
    narrow = mm(wide, gather_matrix(roles(LEVELS - 1)[3]))
    narrow = narrow * twice(lax.rsqrt(mean[:1]), LANES)[:, : CHI * CHI]
    legs = jnp.transpose(narrow.reshape(CHI, PAD, CHI * CHI)[:, :CHI], (1, 0, 2))
    coarse_o[...] = legs.reshape(CHI * CHI, CHI * CHI)


def call(kernel, outs, scratch=()):
    vmem = pl.BlockSpec(memory_space=pltpu.VMEM)

    def run(*args):
        return pl.pallas_call(
            kernel,
            out_shape=[jax.ShapeDtypeStruct(s, d) for s, d in outs],
            in_specs=[vmem] * len(args),
            out_specs=[vmem] * len(outs),
            scratch_shapes=list(scratch),
            compiler_params=pltpu.CompilerParams(vmem_limit_bytes=VMEM_BYTES),
            cost_estimate=pl.CostEstimate(flops=10**8, bytes_accessed=10**6, transcendentals=0),
        )(*args)

    return run


def from_partner(array, flip):
    count = lax.axis_size("row")
    return lax.ppermute(array, "row", [(i, i ^ flip) for i in range(count)])


def mirrored(row):
    parity = row * 0
    for bit in range(LEVELS):
        parity = parity ^ (row >> bit & 1)
    return parity


def from_bond(array):
    rows, cols = lax.axis_size("row"), lax.axis_size("col")
    pairs = []
    for i in range(rows):
        for c in range(cols):
            target = (c + 1) % cols if mirrored(i) else (c - 1) % cols
            pairs.append((i * cols + c, (i ^ 1) * cols + target))
    return lax.ppermute(array, ("row", "col"), pairs)


def per_device(site_tensors, start_basis):
    square = CHI * CHI
    mat, one = ((ROWS, LANES), BF16), ((8, 128), F32)
    sent = ((CHI * (CHI + 2), 128), BF16)
    kron, firsts = [pltpu.VMEM((SECOND, LANES), BF16)], [pltpu.VMEM((CHI * ROWS, LANES), BF16)]
    scales, means = [], []
    own = site_tensors[0, 0]
    for level in range(LEVELS):
        if level == 0:
            other = from_partner(own, 1)
            (own,) = call(cast_kernel, [((square, square), BF16)])(own)
            own, other, gram = call(first_gram_kernel, [mat, mat, sent])(own, other)
        else:
            other = from_partner(own, 1 << level | 1)
            own, product, mean = call(own_kernel, [mat, mat, one])(own)
            gram, scale = call(functools.partial(gram_kernel, level), [sent, one])(
                product, mean, other
            )
            scales, means = [scale], [*means, mean]
        gram_other = from_bond(gram)
        turned, lower, starts, pieces, wide, image, trace = call(
            functools.partial(turn_kernel, level),
            [
                mat,
                mat,
                ((2 * PAD, LANES), F32),
                ((16 * PAD, LANES), BF16),
                mat,
                ((PAD, LANES), F32),
                one,
            ],
        )(own, other, gram, start_basis)
        (left,) = call(iso_kernel, [((PAD, LANES), BF16)])(
            wide, image, trace, gram_other, starts, pieces
        )
        right = from_partner(left, 1)
        (second,) = call(second_kernel, [((ROWS, SECOND), BF16)], firsts)(turned, lower, left)
        if level < LEVELS - 1:
            (own,) = call(third_kernel, [sent], kron)(second, right, *scales)
        else:
            coarse, log_total = call(last_kernel, [((square, square), F32), ((1, 1), F32)], kron)(
                second, right, *scales, *means
            )
    return (coarse[None, None], log_total)


def solution(mesh):
    return jax.shard_map(
        per_device,
        mesh=mesh,
        in_specs=(P("row", "col", None, None), P()),
        out_specs=(P("row", "col", None, None), P("row", "col")),
        check_vma=False,
    )
```

```python
import functools

import functools

import jax
import jax.numpy as jnp
from jax import lax
from jax.experimental import pallas as pl
from jax.experimental.pallas import tpu as pltpu
from jax.sharding import PartitionSpec as P

CHI = 12
LEVELS = 3
SWEEPS = 2
PAD = 16
SHIFT = 4
ROWS = CHI * PAD
LANES = PAD * PAD
VMEM_BYTES = 8 << 20
SECOND = (CHI + 2) * 128
PIVOT = 1.0 / 64
F32 = jnp.float32
BF16 = jnp.bfloat16

NN = (((1,), (0,)), ((), ()))
NT = (((1,), (1,)), ((), ()))
TN = (((0,), (0,)), ((), ()))


def mm(a, b, dims=NN):
    return lax.dot_general(a, b, dims, preferred_element_type=F32)


def iota(shape, dim):
    return lax.broadcasted_iota(jnp.int32, shape, dim)


def group(index):
    return lax.shift_right_logical(index, SHIFT)


def minor(index):
    return lax.bitwise_and(index, PAD - 1)


def one_hot(mask):
    return jnp.where(mask, 1.0, 0.0).astype(BF16)


def spread_matrix(mirror, flip=0):
    i, j = iota((CHI * CHI, LANES), 0), iota((CHI * CHI, LANES), 1)
    s, t = lax.bitwise_xor(group(j), flip), minor(j)
    source = jnp.where(mirror, t * CHI + s, s * CHI + t)
    return one_hot((i == source) & (s < CHI) & (t < CHI))


def gather_matrix(mirror):
    i, j = iota((LANES, CHI * CHI), 0), iota((LANES, CHI * CHI), 1)
    s, t = group(i), minor(i)
    source = jnp.where(mirror, t * CHI + s, s * CHI + t)
    return one_hot((j == source) & (s < CHI) & (t < CHI))


def swapped_tiles(x, other=None):
    lane_group = group(iota((PAD, 128), 1))
    zero = jnp.zeros((PAD, 128), x.dtype)

    def tile(array, p, side):
        return array[p * PAD : (p + 1) * PAD, side * 128 : side * 128 + 128] if p < CHI else zero

    sources, span = {}, 8 if other is None else 4
    high = lax.bitwise_and(lane_group, 4) != 0
    for p in range(CHI if other is None else PAD):
        for side in range(2):
            if other is None:
                sources[p, side] = tile(x, p, side)
            elif p & 4:
                sources[p, side] = jnp.where(high, tile(x, p, side), tile(other, p ^ 4, side))
            else:
                sources[p, side] = jnp.where(high, tile(other, p ^ 4, side), tile(x, p, side))
    tiles = []
    for s in range(CHI):
        pair = []
        for side in range(2):
            out = zero
            for p in range(span):
                source = (side * 8 + (s & 7 & -span)) | p
                if other is None and source >= CHI:
                    continue
                shift = (p - s % span) % 8 * PAD
                piece = sources[source, s >> 3]
                piece = pltpu.roll(piece, shift, 1) if shift else piece
                out = jnp.where(lax.bitwise_and(lane_group, span - 1) == p, piece, out)
            pair.append(out)
        tiles.append(pair)
    return tiles


def block_swap(x, other=None):
    tiles = swapped_tiles(x, other)
    return jnp.concatenate([jnp.concatenate(pair, axis=1) for pair in tiles], axis=0)


def joined(x):
    x = spaced(x)
    lane = iota((PAD, 128), 1)
    sides = []
    for k in range(CHI):
        at = ROWS + (k >> 3) * PAD
        shift = -(k & 7) * PAD % 128
        side = pltpu.roll(x[at : at + PAD], shift, 1) if shift else x[at : at + PAD]
        sides.append(jnp.where(lane < PAD, side, jnp.zeros_like(side)))
    return jnp.concatenate([x[:ROWS], jnp.concatenate(sides, axis=0)], axis=1)


def split(x):
    lane_group = group(iota((PAD, 128), 1))
    tails = [jnp.zeros((PAD, 128), x.dtype)] * 2
    for k in range(CHI):
        block = x[k * PAD : (k + 1) * PAD, 128:]
        tails[k >> 3] = jnp.where(lane_group == (k & 7), block, tails[k >> 3])
    return jnp.concatenate([x[:, :128], *tails], axis=0)


def product_both(a, b, scale=None):
    zero = jnp.zeros((PAD, b.shape[1]), b.dtype)
    blocks = [b[s * PAD : (s + 1) * PAD] if s < CHI else zero for s in range(PAD)]
    plain = mm(a, jnp.concatenate(blocks, axis=0), NT)
    moved = mm(a, jnp.concatenate([blocks[s ^ 4] for s in range(PAD)], axis=0), NT)
    if scale is not None:
        plain, moved = plain * scale, moved * scale
    return plain.astype(BF16), moved.astype(BF16)


def widen(x):
    return jnp.concatenate([x, jnp.zeros((x.shape[0], LANES - x.shape[1]), x.dtype)], axis=1)


def parts3(x):
    a = x.astype(BF16)
    rest = x - a.astype(F32)
    b = rest.astype(BF16)
    c = (rest - b.astype(F32)).astype(BF16)
    return jnp.concatenate([a, b, c], axis=0)


def parts2(x):
    a = x.astype(BF16)
    return jnp.concatenate([a, (x - a.astype(F32)).astype(BF16)], axis=0)


def fold2(y):
    n = y.shape[0] // 2
    return y[n:] + y[:n]


def fold3(y):
    n = y.shape[0] // 3
    return (y[2 * n :] + y[n : 2 * n]) + y[:n]


def compact(x):
    blocks = x.shape[0] // PAD
    legs = x.astype(F32).reshape(blocks, PAD, 128)[:, :CHI]
    return legs.reshape(blocks * CHI, 128).astype(BF16)


def spaced(x):
    blocks = x.shape[0] // CHI
    legs = x.astype(F32).reshape(blocks, CHI, 128)
    rest = jnp.zeros((blocks, PAD - CHI, 128), F32)
    return jnp.concatenate([legs, rest], axis=1).reshape(blocks * PAD, 128).astype(BF16)


def joined(x):
    x = spaced(x)
    lane = iota((PAD, 128), 1)
    sides = []
    for k in range(CHI):
        at = ROWS + (k >> 3) * PAD
        shift = -(k & 7) * PAD % 128
        side = pltpu.roll(x[at : at + PAD], shift, 1) if shift else x[at : at + PAD]
        sides.append(jnp.where(lane < PAD, side, jnp.zeros_like(side)))
    return jnp.concatenate([x[:ROWS], jnp.concatenate(sides, axis=0)], axis=1)


def split(x):
    lane_group = group(iota((PAD, 128), 1))
    tails = [jnp.zeros((PAD, 128), x.dtype)] * 2
    for k in range(CHI):
        block = x[k * PAD : (k + 1) * PAD, 128:]
        tails[k >> 3] = jnp.where(lane_group == (k & 7), block, tails[k >> 3])
    return jnp.concatenate([x[:, :128], *tails], axis=0)


def product_both(a, b, scale=None):
    zero = jnp.zeros((PAD, b.shape[1]), b.dtype)
    blocks = [b[s * PAD : (s + 1) * PAD] if s < CHI else zero for s in range(PAD)]
    plain = mm(a, jnp.concatenate(blocks, axis=0), NT)
    moved = mm(a, jnp.concatenate([blocks[s ^ 4] for s in range(PAD)], axis=0), NT)
    if scale is not None:
        plain, moved = plain * scale, moved * scale
    return plain.astype(BF16), moved.astype(BF16)


def widen(x):
    return jnp.concatenate([x, jnp.zeros((x.shape[0], LANES - x.shape[1]), x.dtype)], axis=1)


def parts3(x):
    a = x.astype(BF16)
    rest = x - a.astype(F32)
    b = rest.astype(BF16)
    c = (rest - b.astype(F32)).astype(BF16)
    return jnp.concatenate([a, b, c], axis=0)


def parts2(x):
    a = x.astype(BF16)
    return jnp.concatenate([a, (x - a.astype(F32)).astype(BF16)], axis=0)


def fold2(y):
    n = y.shape[0] // 2
    return y[n:] + y[:n]


def fold3(y):
    n = y.shape[0] // 3
    return (y[2 * n :] + y[n : 2 * n]) + y[:n]


def compact(x):
    blocks = x.shape[0] // PAD
    legs = x.astype(F32).reshape(blocks, PAD, 128)[:, :CHI]
    return legs.reshape(blocks * CHI, 128).astype(BF16)


def spaced(x):
    blocks = x.shape[0] // CHI
    legs = x.astype(F32).reshape(blocks, CHI, 128)
    rest = jnp.zeros((blocks, PAD - CHI, 128), F32)
    return jnp.concatenate([legs, rest], axis=1).reshape(blocks * PAD, 128).astype(BF16)


def unfold(x):
    side = x[ROWS:]
    low = iota(side.shape, 1) < FOLD
    zero = jnp.zeros_like(side)
    first = jnp.where(low, side, zero)
    last = jnp.where(low, pltpu.roll(side, 128 - FOLD, 1), zero)
    return jnp.concatenate([x[:ROWS], jnp.concatenate([first, last], axis=0)], axis=1)


def row_swap(x):
    legs = x.astype(F32).reshape(CHI, PAD, x.shape[1])[:, :CHI]
    turned = jnp.transpose(legs, (1, 0, 2))
    rest = jnp.zeros((CHI, PAD - CHI, x.shape[1]), F32)
    return jnp.concatenate([turned, rest], axis=1).reshape(x.shape).astype(BF16)


def product_part(x, scale=None):
    return block_swap(*product_both(row_swap(x), x, scale))


def outer_part(first, second):
    outer = widen(mm(first, row_swap(second), NT).astype(BF16))
    lane = iota((PAD, 128), 1)
    tiles = []
    for s in range(CHI):
        tile = jnp.zeros((PAD, 128), BF16)
        for p in range(128 // CHI + 1):
            at = (s >> 3) * 128
            piece = outer[p * PAD : (p + 1) * PAD, at : at + 128]
            shift = (p * CHI - (s & 7) * PAD) % 128
            piece = pltpu.roll(piece, shift, 1) if shift else piece
            tile = jnp.where((lane >= p * CHI) & (lane < p * CHI + CHI), piece, tile)
        tiles.append(tile)
    cut = CHI * (CHI - 1) - 128
    for side in range(2):
        pieces = [outer[p * PAD : (p + 1) * PAD, side * 128 : side * 128 + 128] for p in (CHI - 2, CHI - 1)]
        before = pltpu.roll(pieces[0], (cut - CHI) % 128, 1)
        tiles.append(jnp.where(minor(lane) < cut, before, pltpu.roll(pieces[1], cut, 1)))
    return compact(jnp.concatenate(tiles, axis=0))


def turn(first, compact_lanes):
    if not compact_lanes:
        return widen(row_swap(first.T[:ROWS]))
    legs = first.T[: CHI * CHI].astype(F32).reshape(CHI, CHI, ROWS)
    rest = jnp.zeros((CHI, PAD - CHI, ROWS), F32)
    legs = jnp.concatenate([jnp.transpose(legs, (1, 0, 2)), rest], axis=1)
    return widen(legs.reshape(ROWS, ROWS).astype(BF16))


def quotient(index):
    return lax.shift_right_logical(index * 171, 11)


def natural_matrix():
    i, j = iota((LANES, LANES), 0), iota((LANES, LANES), 1)
    return one_hot((j == minor(i) * CHI + group(i)) & (minor(i) < CHI) & (group(i) < CHI))


def start_body(start, first_upper):
    start = jnp.concatenate([start, jnp.zeros((PAD - CHI, CHI * CHI), F32)], axis=0)
    pieces = parts3(start)
    i, j = iota((CHI * CHI, LANES), 0), iota((CHI * CHI, LANES), 1)
    s = quotient(j)
    swapped = fold3(mm(pieces, one_hot((i == (j - s * CHI) * CHI + s) & (s < CHI))))
    turned = fold3(mm(pieces, spread_matrix(first_upper)))
    return jnp.where(first_upper, widen(start), swapped), turned


def row_products(y):
    pieces = parts2(y)
    high, low = pieces[:PAD], pieces[PAD:]
    gram = fold2(mm(pieces, high, NT)) + mm(high, low, NT)
    return [jnp.broadcast_to(gram[:, k : k + 1], (PAD, 128)) for k in range(CHI)]


def line(x, k):
    return jnp.broadcast_to(x[k : k + 1, :], x.shape)


def twice(x, width):
    return jnp.concatenate([x] * (width // 128), axis=1)


def exact_orthonormal(y):
    cols = row_products(y)
    row = iota((PAD, 128), 0)
    scale = jnp.zeros((PAD, 128), F32)
    for k in range(CHI):
        inverse = lax.rsqrt(line(cols[k], k))
        scale = jnp.where(row == k, inverse, scale)
        factor = jnp.where(row > k, cols[k] * (inverse * inverse), 0.0)
        for j in range(k + 1, CHI):
            cols[j] = cols[j] - factor * line(cols[j], k)
        y = y - twice(factor, y.shape[1]) * line(y, k)
    return y * twice(scale, y.shape[1])


def orthonormal(y):
    cols = row_products(y)
    width = y.shape[1]
    row = iota((PAD, 128), 0)
    floors = [line(cols[k], k) * PIVOT for k in range(CHI)]
    scale, inner = jnp.zeros((PAD, 128), F32), jnp.zeros((PAD, 128), F32)
    good = jnp.ones((PAD, 128), F32)
    for k in range(0, CHI, 2):
        here, after = cols[k], cols[k + 1]
        top, side, low = line(here, k), line(here, k + 1), line(after, k + 1)
        det = top * low - side * side
        good = jnp.where((top >= floors[k]) & (det >= floors[k + 1] * top), good, 0.0)
        over, rest = 1.0 / det, row > k + 1
        first = jnp.where(rest, (low * here - side * after) * over, 0.0)
        second = jnp.where(rest, (top * after - side * here) * over, 0.0)
        for j in range(k + 2, CHI):
            cols[j] = cols[j] - first * line(cols[j], k) - second * line(cols[j], k + 1)
        y = y - twice(first, width) * line(y, k) - twice(second, width) * line(y, k + 1)
        scale = jnp.where(row == k, lax.rsqrt(top), scale)
        scale = jnp.where(row == k + 1, lax.rsqrt(det / top), scale)
        inner = jnp.where(row == k + 1, side / top, inner)
    y = y - twice(inner, width) * pltpu.roll(y, 1, 0)
    return y * twice(scale, width), good


def exact_iso(own, other, start, start_turned, shift, natural):
    pieces = parts3(start)
    image = fold3(mm(pieces, own, NT) + mm(pieces, other, NT))
    basis = exact_orthonormal(widen(image) + shift * start_turned)
    pieces = parts3(basis)
    image = fold3(mm(pieces[:, :ROWS], own) + mm(pieces[:, :ROWS], other))
    return exact_orthonormal(image + shift * fold3(mm(pieces, natural)))


def first_image(gram, pieces):
    gram = spaced(gram)
    shared = [gram[ROWS : ROWS + PAD]] * 8 + [gram[ROWS + PAD :]] * (CHI - 8)
    shared = jnp.concatenate([gram[:ROWS], jnp.concatenate(shared, axis=0)], axis=1)
    i, j = iota((ROWS, LANES), 0), iota((ROWS, LANES), 1)
    entry = minor(i) * CHI + group(i)
    place = jnp.where(entry < 128, entry, entry + lax.bitwise_and(group(i), 7) * PAD)
    diagonal = (j == place) & (minor(i) < CHI)
    trace = jnp.sum(jnp.where(diagonal, shared.astype(F32), 0.0), axis=0, keepdims=True)
    images = mm(pieces, shared, NT)
    image = images[: 2 * PAD]
    block = lax.bitwise_and(group(iota((2 * PAD, ROWS), 1)), 7)
    for k in range(1, 8):
        image = jnp.where(block == k, images[2 * PAD * k : 2 * PAD * (k + 1)], image)
    return widen(fold2(image)), jnp.sum(trace, axis=1, keepdims=True)


def iso_kernel(own, own_image, own_trace, other, starts, pieces, iso_o):
    natural = natural_matrix()
    image, trace = first_image(other[...], pieces[...])
    shift = (own_trace[:1, :1] + trace) / (CHI * CHI)
    unit = 1.0 / shift
    image = (own_image[...] + image) * unit + starts[PAD:]
    parts = parts2(image)
    own, other = own[...], joined(other[...])
    image = fold2(mm(parts[:, :ROWS], own) + mm(parts[:, :ROWS], other)) * unit
    basis, good = orthonormal(image + fold2(mm(parts, natural)))
    iso_o[...] = basis.astype(BF16)

    @pl.when(jnp.logical_not(good[0, 0] > 0.5))
    def _():
        basis = exact_iso(own, other, starts[:PAD], starts[PAD:], shift, natural)
        iso_o[...] = basis.astype(BF16)


def packed_pair(index):
    entry = jnp.where(index < 128, index, 128 + minor(index))
    s = quotient(entry)
    return s, entry - s * CHI


def packing(compact_lanes):
    s, t = packed_pair(iota((LANES, LANES), 1))
    j = iota((LANES, LANES), 0)
    return one_hot(j == (s * CHI + t if compact_lanes else s * PAD + t))


def first_second(turned, lower, left, second_ref, first_ref):
    lane = iota((PAD, LANES), 1)
    masked = [jnp.where(quotient(lane) == k, left.astype(F32), 0.0) for k in range(CHI)]
    masked = jnp.concatenate(masked, axis=0).astype(BF16)
    i, j = iota((LANES, LANES), 0), iota((LANES, LANES), 1)
    values = mm(masked, one_hot(i - quotient(i) * CHI == group(j)))
    eye = minor(lane) == iota((PAD, LANES), 0)
    for a in range(CHI):
        blocks = []
        for k in range(CHI):
            line = jnp.broadcast_to(values[k * PAD + a : k * PAD + a + 1, :], (PAD, LANES))
            blocks.append(jnp.where(eye, line, 0.0).astype(BF16))
        kron = jnp.concatenate(blocks, axis=0)
        first = mm(turned[:, :ROWS], kron)
        first_ref[a * ROWS : (a + 1) * ROWS, :] = first.astype(BF16)
    second = mm(first_ref[:, :ROWS], lower).astype(BF16)
    lane_group = group(iota((PAD, 128), 1))
    for a in range(CHI):
        rows = slice(a * PAD, (a + 1) * PAD)
        tails = [jnp.zeros((PAD, 128), BF16)] * 2
        for k in range(CHI):
            block = second[a * ROWS + k * PAD : a * ROWS + (k + 1) * PAD]
            second_ref[rows, k * 128 : (k + 1) * 128] = block[:, :128]
            tails[k >> 3] = jnp.where(lane_group == (k & 7), block[:, 128:], tails[k >> 3])
        for side in range(2):
            at = (CHI + side) * 128
            second_ref[rows, at : at + 128] = tails[side]


def third(second_ref, right, kron_ref, packed):
    lane = iota((CHI * CHI, LANES), 1)
    if packed:
        right = right.astype(F32)
        rest = jnp.concatenate([right[128 % CHI : CHI], right[:CHI]], axis=0)
        rows = [right[:CHI]] * (128 // CHI) + [right[: 128 % CHI]] + [rest] * 8
        values = jnp.concatenate(rows, axis=0).astype(BF16)
        lane_group = packed_pair(lane)[0]
    else:
        values = jnp.concatenate([right] * PAD, axis=0)
        lane_group = jnp.minimum(group(lane), CHI)
    values = values.T.astype(F32)
    entry = iota((CHI * CHI, LANES), 0)
    kept = quotient(entry) == lane_group
    for k in range(CHI):
        block = values[k * CHI : (k + 1) * CHI, :]
        tall = jnp.concatenate([block] * CHI, axis=0)
        tall = jnp.where(kept, tall, 0.0).astype(BF16)
        kron_ref[k * 128 : (k + 1) * 128, :] = tall[:128]
        at = CHI * 128 + k * PAD
        kron_ref[at : at + PAD, :] = tall[128:]
    used = CHI * 128 + CHI * PAD
    kron_ref[used:, :] = jnp.zeros((SECOND - used, LANES), BF16)
    return mm(second_ref[...], kron_ref[...])


def spread(site, mirror, lower):
    legs = site.astype(F32).reshape(CHI, CHI, CHI * CHI)
    legs = jnp.where(lower, jnp.transpose(legs, (1, 0, 2)), legs)
    rest = jnp.zeros((CHI, PAD - CHI, CHI * CHI), F32)
    rows = jnp.concatenate([legs, rest], axis=1).reshape(ROWS, CHI * CHI).astype(BF16)
    plain = mm(rows, spread_matrix(mirror)).astype(BF16)
    return plain, mm(rows, spread_matrix(mirror, 4)).astype(BF16)


def pick(own_first, own, other):
    return jnp.where(own_first, own, other), jnp.where(own_first, other, own)


def roles(level):
    row = lax.axis_index("row")
    own_lower = row >> level & 1
    first_upper = row >> level + 1 & 1 if level < LEVELS - 1 else row * 0 + 1
    flags = own_lower ^ first_upper, first_upper, own_lower, mirrored(row)
    return [flag != 0 for flag in flags]


def spread_kernel(own, plain_o, flipped_o):
    _, _, own_lower, mirror = roles(0)
    plain_o[...], flipped_o[...] = spread(own[...], mirror, own_lower)


def first_gram_kernel(plain, flipped, other, mine_o, theirs_o, gram_o):
    own_first, _, own_lower, mirror = roles(0)
    mine = block_swap(plain[...], flipped[...])
    theirs = block_swap(*spread(other[...], mirror, jnp.logical_not(own_lower)))
    mine_o[...], theirs_o[...] = mine, theirs
    products = pick(own_first, product_part(mine), product_part(theirs))
    gram_o[...] = outer_part(*products)


def mean_square(lines):
    mean = jnp.sum(lines, axis=1, keepdims=True) / (CHI**4) + 1e-06
    return jnp.broadcast_to(mean, (8, 128))


def scaled_product(sent, x):
    mean = mean_square(jnp.sum(jnp.square(sent.astype(F32)), axis=0, keepdims=True))
    return product_part(x, twice(1.0 / mean[:1], LANES)), mean


def own_kernel(own, wide_o, product_o, mean_o):
    wide = joined(own[...])
    wide_o[...] = wide
    product_o[...], mean_o[...] = scaled_product(own[...], wide)


def gram_kernel(level, product, mean, other, gram_o, scale_o):
    other_product, other_mean = scaled_product(other[...], joined(other[...]))
    gram_o[...] = outer_part(*pick(roles(level)[0], product[...], other_product))
    scale_o[...] = lax.rsqrt(mean[...]) * lax.rsqrt(other_mean)


def turn_kernel(
    level, own, other, gram, start, turned_o, lower_o, starts_o, pieces_o, wide_o, image_o, trace_o
):
    later = level > 0
    own_first, first_upper, _, _ = roles(level)
    first, second = pick(own_first, own[...], joined(other[...]) if later else other[...])
    turned_o[...] = turn(first, later)
    lower_o[...] = mm(second, packing(later)).astype(BF16)
    here, turned = start_body(start[level], first_upper)
    starts_o[:PAD], starts_o[PAD:] = here, turned
    parts = parts2(here)
    place = iota((2 * PAD, 128), 1)
    pieces = []
    for k in range(8):
        side = pltpu.roll(parts[:, 128:], k * PAD, 1) if k else parts[:, 128:]
        side = jnp.where(group(place) == k, side, jnp.zeros_like(side))
        pieces.append(jnp.concatenate([parts[:, :128], side], axis=1))
    pieces = jnp.concatenate(pieces, axis=0)
    pieces_o[...] = pieces
    wide_o[...] = joined(gram[...])
    image_o[...], trace = first_image(gram[...], pieces)
    trace_o[...] = jnp.broadcast_to(trace, trace_o.shape)


def second_kernel(turned, lower, left, second_o, first):
    first_second(turned[...], lower[...], left[...], second_o, first)


def third_kernel(second, right, *refs):
    *scales, next_o, kron = refs
    merged = split(third(second, right[...], kron, True))
    for scale in scales:
        merged = merged * scale[:1]
    next_o[...] = compact(merged)


def last_kernel(second, right, scale, *refs):
    *means, coarse_o, log_o, kron = refs
    merged = third(second, right[...], kron, False) * twice(scale[:1], LANES)
    mean = mean_square(jnp.sum(merged * merged, axis=0, keepdims=True))
    log_o[...] = 0.5 * sum(jnp.log(m[:1, :1]) for m in [*means, mean])
    wide = block_swap(merged.astype(BF16))
    narrow = mm(wide, gather_matrix(roles(LEVELS - 1)[3]))
    narrow = narrow * twice(lax.rsqrt(mean[:1]), LANES)[:, : CHI * CHI]
    legs = jnp.transpose(narrow.reshape(CHI, PAD, CHI * CHI)[:, :CHI], (1, 0, 2))
    coarse_o[...] = legs.reshape(CHI * CHI, CHI * CHI)


def call(kernel, outs, scratch=()):
    vmem = pl.BlockSpec(memory_space=pltpu.VMEM)

    def run(*args):
        return pl.pallas_call(
            kernel,
            out_shape=[jax.ShapeDtypeStruct(s, d) for s, d in outs],
            in_specs=[vmem] * len(args),
            out_specs=[vmem] * len(outs),
            scratch_shapes=list(scratch),
            compiler_params=pltpu.CompilerParams(vmem_limit_bytes=VMEM_BYTES),
            cost_estimate=pl.CostEstimate(flops=10**8, bytes_accessed=10**6, transcendentals=0),
        )(*args)

    return run


def from_partner(array, flip):
    count = lax.axis_size("row")
    return lax.ppermute(array, "row", [(i, i ^ flip) for i in range(count)])


def mirrored(row):
    parity = row * 0
    for bit in range(LEVELS):
        parity = parity ^ (row >> bit & 1)
    return parity


def from_bond(array):
    rows, cols = lax.axis_size("row"), lax.axis_size("col")
    pairs = []
    for i in range(rows):
        for c in range(cols):
            target = (c + 1) % cols if mirrored(i) else (c - 1) % cols
            pairs.append((i * cols + c, (i ^ 1) * cols + target))
    return lax.ppermute(array, ("row", "col"), pairs)


def per_device(site_tensors, start_basis):
    square = CHI * CHI
    mat, one = ((ROWS, LANES), BF16), ((8, 128), F32)
    sent = ((CHI * (CHI + 2), 128), BF16)
    kron, firsts = [pltpu.VMEM((SECOND, LANES), BF16)], [pltpu.VMEM((CHI * ROWS, LANES), BF16)]
    scales, means = [], []
    own = site_tensors[0, 0]
    for level in range(LEVELS):
        if level == 0:
            other = from_partner(own, 1)
            plain, flipped = call(spread_kernel, [mat, mat])(own)
            own, other, gram = call(first_gram_kernel, [mat, mat, sent])(plain, flipped, other)
        else:
            other = from_partner(own, 1 << level | 1)
            own, product, mean = call(own_kernel, [mat, mat, one])(own)
            gram, scale = call(functools.partial(gram_kernel, level), [sent, one])(
                product, mean, other
            )
            scales, means = [scale], [*means, mean]
        gram_other = from_bond(gram)
        turned, lower, starts, pieces, wide, image, trace = call(
            functools.partial(turn_kernel, level),
            [
                mat,
                mat,
                ((2 * PAD, LANES), F32),
                ((16 * PAD, LANES), BF16),
                mat,
                ((PAD, LANES), F32),
                one,
            ],
        )(own, other, gram, start_basis)
        (left,) = call(iso_kernel, [((PAD, LANES), BF16)])(
            wide, image, trace, gram_other, starts, pieces
        )
        right = from_partner(left, 1)
        (second,) = call(second_kernel, [((ROWS, SECOND), BF16)], firsts)(turned, lower, left)
        if level < LEVELS - 1:
            (own,) = call(third_kernel, [sent], kron)(second, right, *scales)
        else:
            coarse, log_total = call(last_kernel, [((square, square), F32), ((1, 1), F32)], kron)(
                second, right, *scales, *means
            )
    return (coarse[None, None], log_total)


def solution(mesh):
    return jax.shard_map(
        per_device,
        mesh=mesh,
        in_specs=(P("row", "col", None, None), P()),
        out_specs=(P("row", "col", None, None), P("row", "col")),
        check_vma=False,
    )
```

```python
import functools

import functools

import jax
import jax.numpy as jnp
from jax import lax
from jax.experimental import pallas as pl
from jax.experimental.pallas import tpu as pltpu
from jax.sharding import PartitionSpec as P

CHI = 12
LEVELS = 3
SWEEPS = 2
PAD = 16
SHIFT = 4
ROWS = CHI * PAD
LANES = PAD * PAD
VMEM_BYTES = 8 << 20
SECOND = (CHI + 2) * 128
PIVOT = 1.0 / 64
F32 = jnp.float32
BF16 = jnp.bfloat16

NN = (((1,), (0,)), ((), ()))
NT = (((1,), (1,)), ((), ()))
TN = (((0,), (0,)), ((), ()))


def mm(a, b, dims=NN):
    return lax.dot_general(a, b, dims, preferred_element_type=F32)


def iota(shape, dim):
    return lax.broadcasted_iota(jnp.int32, shape, dim)


def group(index):
    return lax.shift_right_logical(index, SHIFT)


def minor(index):
    return lax.bitwise_and(index, PAD - 1)


def one_hot(mask):
    return jnp.where(mask, 1.0, 0.0).astype(BF16)


def spread_matrix(mirror):
    i, j = iota((CHI * CHI, LANES), 0), iota((CHI * CHI, LANES), 1)
    s, t = group(j), minor(j)
    source = jnp.where(mirror, t * CHI + s, s * CHI + t)
    return one_hot((i == source) & (s < CHI) & (t < CHI))


def gather_matrix(mirror):
    i, j = iota((LANES, CHI * CHI), 0), iota((LANES, CHI * CHI), 1)
    s, t = group(i), minor(i)
    source = jnp.where(mirror, t * CHI + s, s * CHI + t)
    return one_hot((j == source) & (s < CHI) & (t < CHI))


def placed_tiles(x, blocks, width):
    lane = iota((PAD, 128), 1)
    lane_group = group(lane)
    tiles = [jnp.zeros((PAD, 128), x.dtype)] * CHI
    for side in range(2):
        moves = {}
        for s in range(side * 8, min(side * 8 + 8, CHI)):
            for k, p in enumerate(blocks):
                moves.setdefault((k * width - (s & 7) * PAD) % 128, []).append((k, p, s))
        for shift, members in moves.items():
            source = None
            for _, p, s in members:
                piece = x[p * PAD : (p + 1) * PAD, side * 128 : side * 128 + 128]
                source = piece if source is None else jnp.where(lane_group == (s & 7), piece, source)
            source = pltpu.roll(source, shift, 1) if shift else source
            for k, _, s in members:
                here = (lane >= k * width) & (lane < (k + 1) * width)
                tiles[s] = jnp.where(here, source, tiles[s])
    return tiles


def block_swap(x):
    halves = [placed_tiles(x, range(8), PAD), placed_tiles(x, range(8, CHI), PAD)]
    return jnp.concatenate([jnp.concatenate(pair, axis=1) for pair in zip(*halves)], axis=0)


def widen(x):
    return jnp.concatenate([x, jnp.zeros((x.shape[0], LANES - x.shape[1]), x.dtype)], axis=1)


def parts3(x):
    a = x.astype(BF16)
    rest = x - a.astype(F32)
    b = rest.astype(BF16)
    c = (rest - b.astype(F32)).astype(BF16)
    return jnp.concatenate([a, b, c], axis=0)


def parts2(x):
    a = x.astype(BF16)
    return jnp.concatenate([a, (x - a.astype(F32)).astype(BF16)], axis=0)


def fold2(y):
    n = y.shape[0] // 2
    return y[n:] + y[:n]


def fold3(y):
    n = y.shape[0] // 3
    return (y[2 * n :] + y[n : 2 * n]) + y[:n]


def compact(x):
    blocks = x.shape[0] // PAD
    legs = x.astype(F32).reshape(blocks, PAD, 128)[:, :CHI]
    return legs.reshape(blocks * CHI, 128).astype(BF16)


def spaced(x):
    blocks = x.shape[0] // CHI
    legs = x.astype(F32).reshape(blocks, CHI, 128)
    rest = jnp.zeros((blocks, PAD - CHI, 128), F32)
    return jnp.concatenate([legs, rest], axis=1).reshape(blocks * PAD, 128).astype(BF16)


def joined(x):
    x = spaced(x)
    lane = iota((PAD, 128), 1)
    sides = []
    for k in range(CHI):
        at = ROWS + (k >> 3) * PAD
        shift = -(k & 7) * PAD % 128
        side = pltpu.roll(x[at : at + PAD], shift, 1) if shift else x[at : at + PAD]
        sides.append(jnp.where(lane < PAD, side, jnp.zeros_like(side)))
    return jnp.concatenate([x[:ROWS], jnp.concatenate(sides, axis=0)], axis=1)


def split(x):
    lane_group = group(iota((PAD, 128), 1))
    tails = [jnp.zeros((PAD, 128), x.dtype)] * 2
    for k in range(CHI):
        block = x[k * PAD : (k + 1) * PAD, 128:]
        tails[k >> 3] = jnp.where(lane_group == (k & 7), block, tails[k >> 3])
    return jnp.concatenate([x[:, :128], *tails], axis=0)


def row_swap(x):
    legs = x.astype(F32).reshape(CHI, PAD, x.shape[1])[:, :CHI]
    turned = jnp.transpose(legs, (1, 0, 2))
    rest = jnp.zeros((CHI, PAD - CHI, x.shape[1]), F32)
    return jnp.concatenate([turned, rest], axis=1).reshape(x.shape).astype(BF16)


def product_part(x, scale=None):
    product = mm(row_swap(x), x, NT)
    product = product if scale is None else product * scale[:, :ROWS]
    return block_swap(widen(product.astype(BF16)))


def outer_part(first, second):
    outer = widen(mm(first, row_swap(second), NT).astype(BF16))
    lane = iota((PAD, 128), 1)
    tiles = placed_tiles(outer, range(128 // CHI + 1), CHI)
    cut = CHI * (CHI - 1) - 128
    for side in range(2):
        pieces = [outer[p * PAD : (p + 1) * PAD, side * 128 : side * 128 + 128] for p in (CHI - 2, CHI - 1)]
        before = pltpu.roll(pieces[0], (cut - CHI) % 128, 1)
        tiles.append(jnp.where(minor(lane) < cut, before, pltpu.roll(pieces[1], cut, 1)))
    return compact(jnp.concatenate(tiles, axis=0))


def turn(first, compact_lanes):
    if not compact_lanes:
        return widen(row_swap(first.T[:ROWS]))
    legs = first.T[: CHI * CHI].astype(F32).reshape(CHI, CHI, ROWS)
    rest = jnp.zeros((CHI, PAD - CHI, ROWS), F32)
    legs = jnp.concatenate([jnp.transpose(legs, (1, 0, 2)), rest], axis=1)
    return widen(legs.reshape(ROWS, ROWS).astype(BF16))


def quotient(index):
    return lax.shift_right_logical(index * 171, 11)


def natural_matrix():
    i, j = iota((LANES, LANES), 0), iota((LANES, LANES), 1)
    return one_hot((j == minor(i) * CHI + group(i)) & (minor(i) < CHI) & (group(i) < CHI))


def start_body(start, first_upper):
    start = jnp.concatenate([start, jnp.zeros((PAD - CHI, CHI * CHI), F32)], axis=0)
    pieces = parts3(start)
    i, j = iota((CHI * CHI, LANES), 0), iota((CHI * CHI, LANES), 1)
    s = quotient(j)
    swapped = fold3(mm(pieces, one_hot((i == (j - s * CHI) * CHI + s) & (s < CHI))))
    turned = fold3(mm(pieces, spread_matrix(first_upper)))
    return jnp.where(first_upper, widen(start), swapped), turned


def row_products(y):
    pieces = parts2(y)
    high, low = pieces[:PAD], pieces[PAD:]
    gram = fold2(mm(pieces, high, NT)) + mm(high, low, NT)
    return [jnp.broadcast_to(gram[:, k : k + 1], (PAD, 128)) for k in range(CHI)]


def line(x, k):
    return jnp.broadcast_to(x[k : k + 1, :], x.shape)


def twice(x, width):
    return jnp.concatenate([x] * (width // 128), axis=1)


def exact_orthonormal(y):
    cols = row_products(y)
    row = iota((PAD, 128), 0)
    scale = jnp.zeros((PAD, 128), F32)
    for k in range(CHI):
        inverse = lax.rsqrt(line(cols[k], k))
        scale = jnp.where(row == k, inverse, scale)
        factor = jnp.where(row > k, cols[k] * (inverse * inverse), 0.0)
        for j in range(k + 1, CHI):
            cols[j] = cols[j] - factor * line(cols[j], k)
        y = y - twice(factor, y.shape[1]) * line(y, k)
    return y * twice(scale, y.shape[1])


def orthonormal(y):
    cols = row_products(y)
    width = y.shape[1]
    row = iota((PAD, 128), 0)
    floors = [line(cols[k], k) * PIVOT for k in range(CHI)]
    scale, inner = jnp.zeros((PAD, 128), F32), jnp.zeros((PAD, 128), F32)
    good = jnp.ones((PAD, 128), F32)
    for k in range(0, CHI, 2):
        here, after = cols[k], cols[k + 1]
        top, side, low = line(here, k), line(here, k + 1), line(after, k + 1)
        det = top * low - side * side
        good = jnp.where((top >= floors[k]) & (det >= floors[k + 1] * top), good, 0.0)
        over, rest = 1.0 / det, row > k + 1
        first = jnp.where(rest, (low * here - side * after) * over, 0.0)
        second = jnp.where(rest, (top * after - side * here) * over, 0.0)
        for j in range(k + 2, CHI):
            cols[j] = cols[j] - first * line(cols[j], k) - second * line(cols[j], k + 1)
        y = y - twice(first, width) * line(y, k) - twice(second, width) * line(y, k + 1)
        scale = jnp.where(row == k, lax.rsqrt(top), scale)
        scale = jnp.where(row == k + 1, lax.rsqrt(det / top), scale)
        inner = jnp.where(row == k + 1, side / top, inner)
    y = y - twice(inner, width) * pltpu.roll(y, 1, 0)
    return y * twice(scale, width), good


def exact_iso(own, other, start, start_turned, shift, natural):
    pieces = parts3(start)
    image = fold3(mm(pieces, own, NT) + mm(pieces, other, NT))
    basis = exact_orthonormal(widen(image) + shift * start_turned)
    pieces = parts3(basis)
    image = fold3(mm(pieces[:, :ROWS], own) + mm(pieces[:, :ROWS], other))
    return exact_orthonormal(image + shift * fold3(mm(pieces, natural)))


def first_image(gram, pieces):
    gram = spaced(gram)
    shared = [gram[ROWS : ROWS + PAD]] * 8 + [gram[ROWS + PAD :]] * (CHI - 8)
    shared = jnp.concatenate([gram[:ROWS], jnp.concatenate(shared, axis=0)], axis=1)
    i, j = iota((ROWS, LANES), 0), iota((ROWS, LANES), 1)
    entry = minor(i) * CHI + group(i)
    place = jnp.where(entry < 128, entry, entry + lax.bitwise_and(group(i), 7) * PAD)
    diagonal = (j == place) & (minor(i) < CHI)
    trace = jnp.sum(jnp.where(diagonal, shared.astype(F32), 0.0), axis=0, keepdims=True)
    images = mm(pieces, shared, NT)
    image = images[: 2 * PAD]
    block = lax.bitwise_and(group(iota((2 * PAD, ROWS), 1)), 7)
    for k in range(1, 8):
        image = jnp.where(block == k, images[2 * PAD * k : 2 * PAD * (k + 1)], image)
    return widen(fold2(image)), jnp.sum(trace, axis=1, keepdims=True)


def iso_kernel(own, own_image, own_trace, other, starts, pieces, iso_o):
    natural = natural_matrix()
    image, trace = first_image(other[...], pieces[...])
    shift = (own_trace[:1, :1] + trace) / (CHI * CHI)
    unit = 1.0 / shift
    image = (own_image[...] + image) * unit + starts[PAD:]
    parts = parts2(image)
    own, other = own[...], joined(other[...])
    image = fold2(mm(parts[:, :ROWS], own) + mm(parts[:, :ROWS], other)) * unit
    basis, good = orthonormal(image + fold2(mm(parts, natural)))
    iso_o[...] = basis.astype(BF16)

    @pl.when(jnp.logical_not(good[0, 0] > 0.5))
    def _():
        basis = exact_iso(own, other, starts[:PAD], starts[PAD:], shift, natural)
        iso_o[...] = basis.astype(BF16)


def packed_pair(index):
    entry = jnp.where(index < 128, index, 128 + minor(index))
    s = quotient(entry)
    return s, entry - s * CHI


def packing(compact_lanes):
    s, t = packed_pair(iota((LANES, LANES), 1))
    j = iota((LANES, LANES), 0)
    return one_hot(j == (s * CHI + t if compact_lanes else s * PAD + t))


def first_second(turned, lower, left, second_ref, first_ref):
    lane = iota((PAD, LANES), 1)
    masked = [jnp.where(quotient(lane) == k, left.astype(F32), 0.0) for k in range(CHI)]
    masked = jnp.concatenate(masked, axis=0).astype(BF16)
    i, j = iota((LANES, LANES), 0), iota((LANES, LANES), 1)
    values = mm(masked, one_hot(i - quotient(i) * CHI == group(j)))
    eye = minor(lane) == iota((PAD, LANES), 0)
    for a in range(CHI):
        blocks = []
        for k in range(CHI):
            line = jnp.broadcast_to(values[k * PAD + a : k * PAD + a + 1, :], (PAD, LANES))
            blocks.append(jnp.where(eye, line, 0.0).astype(BF16))
        kron = jnp.concatenate(blocks, axis=0)
        first = mm(turned[:, :ROWS], kron)
        first_ref[a * ROWS : (a + 1) * ROWS, :] = first.astype(BF16)
    second = mm(first_ref[:, :ROWS], lower).astype(BF16)
    lane_group = group(iota((PAD, 128), 1))
    for a in range(CHI):
        rows = slice(a * PAD, (a + 1) * PAD)
        tails = [jnp.zeros((PAD, 128), BF16)] * 2
        for k in range(CHI):
            block = second[a * ROWS + k * PAD : a * ROWS + (k + 1) * PAD]
            second_ref[rows, k * 128 : (k + 1) * 128] = block[:, :128]
            tails[k >> 3] = jnp.where(lane_group == (k & 7), block[:, 128:], tails[k >> 3])
        for side in range(2):
            at = (CHI + side) * 128
            second_ref[rows, at : at + 128] = tails[side]


def third(second_ref, right, kron_ref, packed):
    lane = iota((CHI * CHI, LANES), 1)
    if packed:
        right = right.astype(F32)
        rest = jnp.concatenate([right[128 % CHI : CHI], right[:CHI]], axis=0)
        rows = [right[:CHI]] * (128 // CHI) + [right[: 128 % CHI]] + [rest] * 8
        values = jnp.concatenate(rows, axis=0).astype(BF16)
        lane_group = packed_pair(lane)[0]
    else:
        values = jnp.concatenate([right] * PAD, axis=0)
        lane_group = jnp.minimum(group(lane), CHI)
    values = values.T.astype(F32)
    entry = iota((CHI * CHI, LANES), 0)
    kept = quotient(entry) == lane_group
    for k in range(CHI):
        block = values[k * CHI : (k + 1) * CHI, :]
        tall = jnp.concatenate([block] * CHI, axis=0)
        tall = jnp.where(kept, tall, 0.0).astype(BF16)
        kron_ref[k * 128 : (k + 1) * 128, :] = tall[:128]
        at = CHI * 128 + k * PAD
        kron_ref[at : at + PAD, :] = tall[128:]
    used = CHI * 128 + CHI * PAD
    kron_ref[used:, :] = jnp.zeros((SECOND - used, LANES), BF16)
    return mm(second_ref[...], kron_ref[...])


def spread(site, mirror, lower):
    legs = site.astype(F32).reshape(CHI, CHI, CHI * CHI)
    legs = jnp.where(lower, jnp.transpose(legs, (1, 0, 2)), legs)
    rest = jnp.zeros((CHI, PAD - CHI, CHI * CHI), F32)
    rows = jnp.concatenate([legs, rest], axis=1).reshape(ROWS, CHI * CHI).astype(BF16)
    return mm(rows, spread_matrix(mirror)).astype(BF16)


def pick(own_first, own, other):
    return jnp.where(own_first, own, other), jnp.where(own_first, other, own)


def roles(level):
    row = lax.axis_index("row")
    own_lower = row >> level & 1
    first_upper = row >> level + 1 & 1 if level < LEVELS - 1 else row * 0 + 1
    flags = own_lower ^ first_upper, first_upper, own_lower, mirrored(row)
    return [flag != 0 for flag in flags]


def spread_kernel(own, spread_o):
    _, _, own_lower, mirror = roles(0)
    spread_o[...] = spread(own[...], mirror, own_lower)


def first_gram_kernel(own, other, mine_o, theirs_o, gram_o):
    own_first, _, own_lower, mirror = roles(0)
    mine = block_swap(own[...])
    theirs = block_swap(spread(other[...], mirror, jnp.logical_not(own_lower)))
    mine_o[...], theirs_o[...] = mine, theirs
    products = pick(own_first, product_part(mine), product_part(theirs))
    gram_o[...] = outer_part(*products)


def mean_square(lines):
    mean = jnp.sum(lines, axis=1, keepdims=True) / (CHI**4) + 1e-06
    return jnp.broadcast_to(mean, (8, 128))


def scaled_product(sent, x):
    mean = mean_square(jnp.sum(jnp.square(sent.astype(F32)), axis=0, keepdims=True))
    return product_part(x, twice(1.0 / mean[:1], LANES)), mean


def own_kernel(own, wide_o, product_o, mean_o):
    wide = joined(own[...])
    wide_o[...] = wide
    product_o[...], mean_o[...] = scaled_product(own[...], wide)


def gram_kernel(level, product, mean, other, gram_o, scale_o):
    other_product, other_mean = scaled_product(other[...], joined(other[...]))
    gram_o[...] = outer_part(*pick(roles(level)[0], product[...], other_product))
    scale_o[...] = lax.rsqrt(mean[...]) * lax.rsqrt(other_mean)


def turn_kernel(
    level, own, other, gram, start, turned_o, lower_o, starts_o, pieces_o, wide_o, image_o, trace_o
):
    later = level > 0
    own_first, first_upper, _, _ = roles(level)
    first, second = pick(own_first, own[...], joined(other[...]) if later else other[...])
    turned_o[...] = turn(first, later)
    lower_o[...] = mm(second, packing(later)).astype(BF16)
    here, turned = start_body(start[level], first_upper)
    starts_o[:PAD], starts_o[PAD:] = here, turned
    parts = parts2(here)
    place = iota((2 * PAD, 128), 1)
    pieces = []
    for k in range(8):
        side = pltpu.roll(parts[:, 128:], k * PAD, 1) if k else parts[:, 128:]
        side = jnp.where(group(place) == k, side, jnp.zeros_like(side))
        pieces.append(jnp.concatenate([parts[:, :128], side], axis=1))
    pieces = jnp.concatenate(pieces, axis=0)
    pieces_o[...] = pieces
    wide_o[...] = joined(gram[...])
    image_o[...], trace = first_image(gram[...], pieces)
    trace_o[...] = jnp.broadcast_to(trace, trace_o.shape)


def second_kernel(turned, lower, left, second_o, first):
    first_second(turned[...], lower[...], left[...], second_o, first)


def third_kernel(second, right, *refs):
    *scales, next_o, kron = refs
    merged = split(third(second, right[...], kron, True))
    for scale in scales:
        merged = merged * scale[:1]
    next_o[...] = compact(merged)


def last_kernel(second, right, scale, *refs):
    *means, coarse_o, log_o, kron = refs
    merged = third(second, right[...], kron, False) * twice(scale[:1], LANES)
    mean = mean_square(jnp.sum(merged * merged, axis=0, keepdims=True))
    log_o[...] = 0.5 * sum(jnp.log(m[:1, :1]) for m in [*means, mean])
    wide = block_swap(merged.astype(BF16))
    narrow = mm(wide, gather_matrix(roles(LEVELS - 1)[3]))
    narrow = narrow * twice(lax.rsqrt(mean[:1]), LANES)[:, : CHI * CHI]
    legs = jnp.transpose(narrow.reshape(CHI, PAD, CHI * CHI)[:, :CHI], (1, 0, 2))
    coarse_o[...] = legs.reshape(CHI * CHI, CHI * CHI)


def call(kernel, outs, scratch=()):
    vmem = pl.BlockSpec(memory_space=pltpu.VMEM)

    def run(*args):
        return pl.pallas_call(
            kernel,
            out_shape=[jax.ShapeDtypeStruct(s, d) for s, d in outs],
            in_specs=[vmem] * len(args),
            out_specs=[vmem] * len(outs),
            scratch_shapes=list(scratch),
            compiler_params=pltpu.CompilerParams(vmem_limit_bytes=VMEM_BYTES),
            cost_estimate=pl.CostEstimate(flops=10**8, bytes_accessed=10**6, transcendentals=0),
        )(*args)

    return run


def from_partner(array, flip):
    count = lax.axis_size("row")
    return lax.ppermute(array, "row", [(i, i ^ flip) for i in range(count)])


def mirrored(row):
    parity = row * 0
    for bit in range(LEVELS):
        parity = parity ^ (row >> bit & 1)
    return parity


def from_bond(array):
    rows, cols = lax.axis_size("row"), lax.axis_size("col")
    pairs = []
    for i in range(rows):
        for c in range(cols):
            target = (c + 1) % cols if mirrored(i) else (c - 1) % cols
            pairs.append((i * cols + c, (i ^ 1) * cols + target))
    return lax.ppermute(array, ("row", "col"), pairs)


def per_device(site_tensors, start_basis):
    square = CHI * CHI
    mat, one = ((ROWS, LANES), BF16), ((8, 128), F32)
    sent = ((CHI * (CHI + 2), 128), BF16)
    kron, firsts = [pltpu.VMEM((SECOND, LANES), BF16)], [pltpu.VMEM((CHI * ROWS, LANES), BF16)]
    scales, means = [], []
    own = site_tensors[0, 0]
    for level in range(LEVELS):
        if level == 0:
            other = from_partner(own, 1)
            (own,) = call(spread_kernel, [mat])(own)
            own, other, gram = call(first_gram_kernel, [mat, mat, sent])(own, other)
        else:
            other = from_partner(own, 1 << level | 1)
            own, product, mean = call(own_kernel, [mat, mat, one])(own)
            gram, scale = call(functools.partial(gram_kernel, level), [sent, one])(
                product, mean, other
            )
            scales, means = [scale], [*means, mean]
        gram_other = from_bond(gram)
        turned, lower, starts, pieces, wide, image, trace = call(
            functools.partial(turn_kernel, level),
            [
                mat,
                mat,
                ((2 * PAD, LANES), F32),
                ((16 * PAD, LANES), BF16),
                mat,
                ((PAD, LANES), F32),
                one,
            ],
        )(own, other, gram, start_basis)
        (left,) = call(iso_kernel, [((PAD, LANES), BF16)])(
            wide, image, trace, gram_other, starts, pieces
        )
        right = from_partner(left, 1)
        (second,) = call(second_kernel, [((ROWS, SECOND), BF16)], firsts)(turned, lower, left)
        if level < LEVELS - 1:
            (own,) = call(third_kernel, [sent], kron)(second, right, *scales)
        else:
            coarse, log_total = call(last_kernel, [((square, square), F32), ((1, 1), F32)], kron)(
                second, right, *scales, *means
            )
    return (coarse[None, None], log_total)


def solution(mesh):
    return jax.shard_map(
        per_device,
        mesh=mesh,
        in_specs=(P("row", "col", None, None), P()),
        out_specs=(P("row", "col", None, None), P("row", "col")),
        check_vma=False,
    )
```

```python
import functools

import functools

import jax
import jax.numpy as jnp
from jax import lax
from jax.experimental import pallas as pl
from jax.experimental.pallas import tpu as pltpu
from jax.sharding import PartitionSpec as P

CHI = 12
LEVELS = 3
SWEEPS = 2
PAD = 16
SHIFT = 4
ROWS = CHI * PAD
LANES = PAD * PAD
VMEM_BYTES = 8 << 20
SECOND = (CHI + 2) * 128
PIVOT = 1.0 / 64
F32 = jnp.float32
BF16 = jnp.bfloat16

NN = (((1,), (0,)), ((), ()))
NT = (((1,), (1,)), ((), ()))
TN = (((0,), (0,)), ((), ()))


def mm(a, b, dims=NN):
    return lax.dot_general(a, b, dims, preferred_element_type=F32)


def iota(shape, dim):
    return lax.broadcasted_iota(jnp.int32, shape, dim)


def group(index):
    return lax.shift_right_logical(index, SHIFT)


def minor(index):
    return lax.bitwise_and(index, PAD - 1)


def one_hot(mask):
    return jnp.where(mask, 1.0, 0.0).astype(BF16)


def spread_matrix(mirror):
    i, j = iota((CHI * CHI, LANES), 0), iota((CHI * CHI, LANES), 1)
    s, t = group(j), minor(j)
    source = jnp.where(mirror, t * CHI + s, s * CHI + t)
    return one_hot((i == source) & (s < CHI) & (t < CHI))


def gather_matrix(mirror):
    i, j = iota((LANES, CHI * CHI), 0), iota((LANES, CHI * CHI), 1)
    s, t = group(i), minor(i)
    source = jnp.where(mirror, t * CHI + s, s * CHI + t)
    return one_hot((j == source) & (s < CHI) & (t < CHI))


def placed_tiles(x, blocks, width):
    lane = iota((PAD, 128), 1)
    lane_group = group(lane)
    tiles = [jnp.zeros((PAD, 128), x.dtype)] * CHI
    for side in range(2):
        moves = {}
        for s in range(side * 8, min(side * 8 + 8, CHI)):
            for k, p in enumerate(blocks):
                moves.setdefault((k * width - (s & 7) * PAD) % 128, []).append((k, p, s))
        for shift, members in moves.items():
            source = None
            for _, p, s in members:
                piece = x[p * PAD : (p + 1) * PAD, side * 128 : side * 128 + 128]
                source = piece if source is None else jnp.where(lane_group == (s & 7), piece, source)
            source = pltpu.roll(source, shift, 1) if shift else source
            for k, _, s in members:
                here = (lane >= k * width) & (lane < (k + 1) * width)
                tiles[s] = jnp.where(here, source, tiles[s])
    return tiles


def block_swap(x):
    halves = [placed_tiles(x, range(8), PAD), placed_tiles(x, range(8, CHI), PAD)]
    return jnp.concatenate([jnp.concatenate(pair, axis=1) for pair in zip(*halves)], axis=0)


def widen(x):
    return jnp.concatenate([x, jnp.zeros((x.shape[0], LANES - x.shape[1]), x.dtype)], axis=1)


def parts3(x):
    a = x.astype(BF16)
    rest = x - a.astype(F32)
    b = rest.astype(BF16)
    c = (rest - b.astype(F32)).astype(BF16)
    return jnp.concatenate([a, b, c], axis=0)


def parts2(x):
    a = x.astype(BF16)
    return jnp.concatenate([a, (x - a.astype(F32)).astype(BF16)], axis=0)


def fold2(y):
    n = y.shape[0] // 2
    return y[n:] + y[:n]


def fold3(y):
    n = y.shape[0] // 3
    return (y[2 * n :] + y[n : 2 * n]) + y[:n]


def compact(x):
    blocks = x.shape[0] // PAD
    legs = x.astype(F32).reshape(blocks, PAD, 128)[:, :CHI]
    return legs.reshape(blocks * CHI, 128).astype(BF16)


def spaced(x):
    blocks = x.shape[0] // CHI
    legs = x.astype(F32).reshape(blocks, CHI, 128)
    rest = jnp.zeros((blocks, PAD - CHI, 128), F32)
    return jnp.concatenate([legs, rest], axis=1).reshape(blocks * PAD, 128).astype(BF16)


def joined(x):
    x = spaced(x)
    lane = iota((PAD, 128), 1)
    sides = []
    for k in range(CHI):
        at = ROWS + (k >> 3) * PAD
        shift = -(k & 7) * PAD % 128
        side = pltpu.roll(x[at : at + PAD], shift, 1) if shift else x[at : at + PAD]
        sides.append(jnp.where(lane < PAD, side, jnp.zeros_like(side)))
    return jnp.concatenate([x[:ROWS], jnp.concatenate(sides, axis=0)], axis=1)


def split(x):
    lane_group = group(iota((PAD, 128), 1))
    tails = [jnp.zeros((PAD, 128), x.dtype)] * 2
    for k in range(CHI):
        block = x[k * PAD : (k + 1) * PAD, 128:]
        tails[k >> 3] = jnp.where(lane_group == (k & 7), block, tails[k >> 3])
    return jnp.concatenate([x[:, :128], *tails], axis=0)


def row_swap(x):
    legs = x.astype(F32).reshape(CHI, PAD, x.shape[1])[:, :CHI]
    turned = jnp.transpose(legs, (1, 0, 2))
    rest = jnp.zeros((CHI, PAD - CHI, x.shape[1]), F32)
    return jnp.concatenate([turned, rest], axis=1).reshape(x.shape).astype(BF16)


def product_part(x, scale=None):
    product = mm(row_swap(x), x, NT)
    product = product if scale is None else product * scale[:, :ROWS]
    return block_swap(widen(product.astype(BF16)))


def outer_part(first, second):
    outer = widen(mm(first, row_swap(second), NT).astype(BF16))
    lane = iota((PAD, 128), 1)
    tiles = placed_tiles(outer, range(128 // CHI + 1), CHI)
    cut = CHI * (CHI - 1) - 128
    for side in range(2):
        pieces = [outer[p * PAD : (p + 1) * PAD, side * 128 : side * 128 + 128] for p in (CHI - 2, CHI - 1)]
        before = pltpu.roll(pieces[0], (cut - CHI) % 128, 1)
        tiles.append(jnp.where(minor(lane) < cut, before, pltpu.roll(pieces[1], cut, 1)))
    return compact(jnp.concatenate(tiles, axis=0))


def turn(first, compact_lanes):
    if not compact_lanes:
        return widen(row_swap(first.T[:ROWS]))
    legs = first.T[: CHI * CHI].astype(F32).reshape(CHI, CHI, ROWS)
    rest = jnp.zeros((CHI, PAD - CHI, ROWS), F32)
    legs = jnp.concatenate([jnp.transpose(legs, (1, 0, 2)), rest], axis=1)
    return widen(legs.reshape(ROWS, ROWS).astype(BF16))


def quotient(index):
    return lax.shift_right_logical(index * 171, 11)


def natural_matrix():
    i, j = iota((LANES, LANES), 0), iota((LANES, LANES), 1)
    return one_hot((j == minor(i) * CHI + group(i)) & (minor(i) < CHI) & (group(i) < CHI))


def start_body(start, first_upper):
    start = jnp.concatenate([start, jnp.zeros((PAD - CHI, CHI * CHI), F32)], axis=0)
    pieces = parts3(start)
    i, j = iota((CHI * CHI, LANES), 0), iota((CHI * CHI, LANES), 1)
    s = quotient(j)
    swapped = fold3(mm(pieces, one_hot((i == (j - s * CHI) * CHI + s) & (s < CHI))))
    turned = fold3(mm(pieces, spread_matrix(first_upper)))
    return jnp.where(first_upper, widen(start), swapped), turned


def row_products(y):
    pieces = parts2(y)
    gram = mm(pieces, pieces, NT)
    near, cross = fold2(gram[:, :PAD]), gram[:PAD, PAD:]
    return [
        jnp.broadcast_to(near[:, k : k + 1], (PAD, 128))
        + jnp.broadcast_to(cross[:, k : k + 1], (PAD, 128))
        for k in range(CHI)
    ]


def line(x, k):
    return jnp.broadcast_to(x[k : k + 1, :], x.shape)


def twice(x, width):
    return jnp.concatenate([x] * (width // 128), axis=1)


def exact_orthonormal(y):
    cols = row_products(y)
    row = iota((PAD, 128), 0)
    scale = jnp.zeros((PAD, 128), F32)
    for k in range(CHI):
        inverse = lax.rsqrt(line(cols[k], k))
        scale = jnp.where(row == k, inverse, scale)
        factor = jnp.where(row > k, cols[k] * (inverse * inverse), 0.0)
        for j in range(k + 1, CHI):
            cols[j] = cols[j] - factor * line(cols[j], k)
        y = y - twice(factor, y.shape[1]) * line(y, k)
    return y * twice(scale, y.shape[1])


def orthonormal(y):
    cols = row_products(y)
    width = y.shape[1]
    row = iota((PAD, 128), 0)
    floors = [line(cols[k], k) * PIVOT for k in range(CHI)]
    scale, inner = jnp.zeros((PAD, 128), F32), jnp.zeros((PAD, 128), F32)
    good = jnp.ones((PAD, 128), F32)
    for k in range(0, CHI, 2):
        here, after = cols[k], cols[k + 1]
        top, side, low = line(here, k), line(here, k + 1), line(after, k + 1)
        det = top * low - side * side
        good = jnp.where((top >= floors[k]) & (det >= floors[k + 1] * top), good, 0.0)
        over, rest = 1.0 / det, row > k + 1
        first = jnp.where(rest, (low * here - side * after) * over, 0.0)
        second = jnp.where(rest, (top * after - side * here) * over, 0.0)
        for j in range(k + 2, CHI):
            cols[j] = cols[j] - first * line(cols[j], k) - second * line(cols[j], k + 1)
        y = y - twice(first, width) * line(y, k) - twice(second, width) * line(y, k + 1)
        scale = jnp.where(row == k, lax.rsqrt(top), scale)
        scale = jnp.where(row == k + 1, lax.rsqrt(det / top), scale)
        inner = jnp.where(row == k + 1, side / top, inner)
    y = y - twice(inner, width) * pltpu.roll(y, 1, 0)
    return y * twice(scale, width), good


def exact_iso(own, other, start, start_turned, shift, natural):
    pieces = parts3(start)
    image = fold3(mm(pieces, own, NT) + mm(pieces, other, NT))
    basis = exact_orthonormal(widen(image) + shift * start_turned)
    pieces = parts3(basis)
    image = fold3(mm(pieces[:, :ROWS], own) + mm(pieces[:, :ROWS], other))
    return exact_orthonormal(image + shift * fold3(mm(pieces, natural)))


def first_image(gram, pieces):
    gram = spaced(gram)
    shared = [gram[ROWS : ROWS + PAD]] * 8 + [gram[ROWS + PAD :]] * (CHI - 8)
    shared = jnp.concatenate([gram[:ROWS], jnp.concatenate(shared, axis=0)], axis=1)
    i, j = iota((ROWS, LANES), 0), iota((ROWS, LANES), 1)
    entry = minor(i) * CHI + group(i)
    place = jnp.where(entry < 128, entry, entry + lax.bitwise_and(group(i), 7) * PAD)
    diagonal = (j == place) & (minor(i) < CHI)
    trace = jnp.sum(jnp.where(diagonal, shared.astype(F32), 0.0), axis=0, keepdims=True)
    images = mm(pieces, shared, NT)
    image = images[: 2 * PAD]
    block = lax.bitwise_and(group(iota((2 * PAD, ROWS), 1)), 7)
    for k in range(1, 8):
        image = jnp.where(block == k, images[2 * PAD * k : 2 * PAD * (k + 1)], image)
    return widen(fold2(image)), jnp.sum(trace, axis=1, keepdims=True)


def iso_kernel(own, own_image, own_trace, other, starts, pieces, iso_o):
    natural = natural_matrix()
    image, trace = first_image(other[...], pieces[...])
    shift = (own_trace[:1, :1] + trace) / (CHI * CHI)
    unit = 1.0 / shift
    image = (own_image[...] + image) * unit + starts[PAD:]
    parts = parts2(image)
    own, other = own[...], joined(other[...])
    image = fold2(mm(parts[:, :ROWS], own) + mm(parts[:, :ROWS], other)) * unit
    basis, good = orthonormal(image + fold2(mm(parts, natural)))
    iso_o[...] = basis.astype(BF16)

    @pl.when(jnp.logical_not(good[0, 0] > 0.5))
    def _():
        basis = exact_iso(own, other, starts[:PAD], starts[PAD:], shift, natural)
        iso_o[...] = basis.astype(BF16)


def packed_pair(index):
    entry = jnp.where(index < 128, index, 128 + minor(index))
    s = quotient(entry)
    return s, entry - s * CHI


def packing(compact_lanes):
    s, t = packed_pair(iota((LANES, LANES), 1))
    j = iota((LANES, LANES), 0)
    return one_hot(j == (s * CHI + t if compact_lanes else s * PAD + t))


def first_second(turned, lower, left, second_ref, first_ref):
    lane = iota((PAD, LANES), 1)
    masked = [jnp.where(quotient(lane) == k, left.astype(F32), 0.0) for k in range(CHI)]
    masked = jnp.concatenate(masked, axis=0).astype(BF16)
    i, j = iota((LANES, LANES), 0), iota((LANES, LANES), 1)
    values = mm(masked, one_hot(i - quotient(i) * CHI == group(j)))
    eye = minor(lane) == iota((PAD, LANES), 0)
    for a in range(CHI):
        blocks = []
        for k in range(CHI):
            line = jnp.broadcast_to(values[k * PAD + a : k * PAD + a + 1, :], (PAD, LANES))
            blocks.append(jnp.where(eye, line, 0.0).astype(BF16))
        kron = jnp.concatenate(blocks, axis=0)
        first = mm(turned[:, :ROWS], kron)
        first_ref[a * ROWS : (a + 1) * ROWS, :] = first.astype(BF16)
    second = mm(first_ref[:, :ROWS], lower).astype(BF16)
    lane_group = group(iota((PAD, 128), 1))
    for a in range(CHI):
        rows = slice(a * PAD, (a + 1) * PAD)
        tails = [jnp.zeros((PAD, 128), BF16)] * 2
        for k in range(CHI):
            block = second[a * ROWS + k * PAD : a * ROWS + (k + 1) * PAD]
            second_ref[rows, k * 128 : (k + 1) * 128] = block[:, :128]
            tails[k >> 3] = jnp.where(lane_group == (k & 7), block[:, 128:], tails[k >> 3])
        for side in range(2):
            at = (CHI + side) * 128
            second_ref[rows, at : at + 128] = tails[side]


def third(second_ref, right, kron_ref, packed):
    lane = iota((CHI * CHI, LANES), 1)
    if packed:
        right = right.astype(F32)
        rest = jnp.concatenate([right[128 % CHI : CHI], right[:CHI]], axis=0)
        rows = [right[:CHI]] * (128 // CHI) + [right[: 128 % CHI]] + [rest] * 8
        values = jnp.concatenate(rows, axis=0).astype(BF16)
        lane_group = packed_pair(lane)[0]
    else:
        values = jnp.concatenate([right] * PAD, axis=0)
        lane_group = jnp.minimum(group(lane), CHI)
    values = values.T.astype(F32)
    entry = iota((CHI * CHI, LANES), 0)
    kept = quotient(entry) == lane_group
    for k in range(CHI):
        block = values[k * CHI : (k + 1) * CHI, :]
        tall = jnp.concatenate([block] * CHI, axis=0)
        tall = jnp.where(kept, tall, 0.0).astype(BF16)
        kron_ref[k * 128 : (k + 1) * 128, :] = tall[:128]
        at = CHI * 128 + k * PAD
        kron_ref[at : at + PAD, :] = tall[128:]
    used = CHI * 128 + CHI * PAD
    kron_ref[used:, :] = jnp.zeros((SECOND - used, LANES), BF16)
    return mm(second_ref[...], kron_ref[...])


def spread(site, mirror, lower):
    legs = site.astype(F32).reshape(CHI, CHI, CHI * CHI)
    legs = jnp.where(lower, jnp.transpose(legs, (1, 0, 2)), legs)
    rest = jnp.zeros((CHI, PAD - CHI, CHI * CHI), F32)
    rows = jnp.concatenate([legs, rest], axis=1).reshape(ROWS, CHI * CHI).astype(BF16)
    return mm(rows, spread_matrix(mirror)).astype(BF16)


def pick(own_first, own, other):
    return jnp.where(own_first, own, other), jnp.where(own_first, other, own)


def roles(level):
    row = lax.axis_index("row")
    own_lower = row >> level & 1
    first_upper = row >> level + 1 & 1 if level < LEVELS - 1 else row * 0 + 1
    flags = own_lower ^ first_upper, first_upper, own_lower, mirrored(row)
    return [flag != 0 for flag in flags]


def spread_kernel(own, spread_o):
    _, _, own_lower, mirror = roles(0)
    spread_o[...] = spread(own[...], mirror, own_lower)


def first_gram_kernel(own, other, mine_o, theirs_o, gram_o):
    own_first, _, own_lower, mirror = roles(0)
    mine = block_swap(own[...])
    theirs = block_swap(spread(other[...], mirror, jnp.logical_not(own_lower)))
    mine_o[...], theirs_o[...] = mine, theirs
    products = pick(own_first, product_part(mine), product_part(theirs))
    gram_o[...] = outer_part(*products)


def mean_square(lines):
    mean = jnp.sum(lines, axis=1, keepdims=True) / (CHI**4) + 1e-06
    return jnp.broadcast_to(mean, (8, 128))


def scaled_product(sent, x):
    mean = mean_square(jnp.sum(jnp.square(sent.astype(F32)), axis=0, keepdims=True))
    return product_part(x, twice(1.0 / mean[:1], LANES)), mean


def own_kernel(own, wide_o, product_o, mean_o):
    wide = joined(own[...])
    wide_o[...] = wide
    product_o[...], mean_o[...] = scaled_product(own[...], wide)


def gram_kernel(level, product, mean, other, gram_o, scale_o):
    other_product, other_mean = scaled_product(other[...], joined(other[...]))
    gram_o[...] = outer_part(*pick(roles(level)[0], product[...], other_product))
    scale_o[...] = lax.rsqrt(mean[...]) * lax.rsqrt(other_mean)


def turn_kernel(
    level, own, other, gram, start, turned_o, lower_o, starts_o, pieces_o, wide_o, image_o, trace_o
):
    later = level > 0
    own_first, first_upper, _, _ = roles(level)
    first, second = pick(own_first, own[...], joined(other[...]) if later else other[...])
    turned_o[...] = turn(first, later)
    lower_o[...] = mm(second, packing(later)).astype(BF16)
    here, turned = start_body(start[level], first_upper)
    starts_o[:PAD], starts_o[PAD:] = here, turned
    parts = parts2(here)
    place = iota((2 * PAD, 128), 1)
    pieces = []
    for k in range(8):
        side = pltpu.roll(parts[:, 128:], k * PAD, 1) if k else parts[:, 128:]
        side = jnp.where(group(place) == k, side, jnp.zeros_like(side))
        pieces.append(jnp.concatenate([parts[:, :128], side], axis=1))
    pieces = jnp.concatenate(pieces, axis=0)
    pieces_o[...] = pieces
    wide_o[...] = joined(gram[...])
    image_o[...], trace = first_image(gram[...], pieces)
    trace_o[...] = jnp.broadcast_to(trace, trace_o.shape)


def second_kernel(turned, lower, left, second_o, first):
    first_second(turned[...], lower[...], left[...], second_o, first)


def third_kernel(second, right, *refs):
    *scales, next_o, kron = refs
    merged = split(third(second, right[...], kron, True))
    for scale in scales:
        merged = merged * scale[:1]
    next_o[...] = compact(merged)


def last_kernel(second, right, scale, *refs):
    *means, coarse_o, log_o, kron = refs
    merged = third(second, right[...], kron, False) * twice(scale[:1], LANES)
    mean = mean_square(jnp.sum(merged * merged, axis=0, keepdims=True))
    log_o[...] = 0.5 * sum(jnp.log(m[:1, :1]) for m in [*means, mean])
    wide = block_swap(merged.astype(BF16))
    narrow = mm(wide, gather_matrix(roles(LEVELS - 1)[3]))
    narrow = narrow * twice(lax.rsqrt(mean[:1]), LANES)[:, : CHI * CHI]
    legs = jnp.transpose(narrow.reshape(CHI, PAD, CHI * CHI)[:, :CHI], (1, 0, 2))
    coarse_o[...] = legs.reshape(CHI * CHI, CHI * CHI)


def call(kernel, outs, scratch=()):
    vmem = pl.BlockSpec(memory_space=pltpu.VMEM)

    def run(*args):
        return pl.pallas_call(
            kernel,
            out_shape=[jax.ShapeDtypeStruct(s, d) for s, d in outs],
            in_specs=[vmem] * len(args),
            out_specs=[vmem] * len(outs),
            scratch_shapes=list(scratch),
            compiler_params=pltpu.CompilerParams(vmem_limit_bytes=VMEM_BYTES),
            cost_estimate=pl.CostEstimate(flops=10**8, bytes_accessed=10**6, transcendentals=0),
        )(*args)

    return run


def from_partner(array, flip):
    count = lax.axis_size("row")
    return lax.ppermute(array, "row", [(i, i ^ flip) for i in range(count)])


def mirrored(row):
    parity = row * 0
    for bit in range(LEVELS):
        parity = parity ^ (row >> bit & 1)
    return parity


def from_bond(array):
    rows, cols = lax.axis_size("row"), lax.axis_size("col")
    pairs = []
    for i in range(rows):
        for c in range(cols):
            target = (c + 1) % cols if mirrored(i) else (c - 1) % cols
            pairs.append((i * cols + c, (i ^ 1) * cols + target))
    return lax.ppermute(array, ("row", "col"), pairs)


def per_device(site_tensors, start_basis):
    square = CHI * CHI
    mat, one = ((ROWS, LANES), BF16), ((8, 128), F32)
    sent = ((CHI * (CHI + 2), 128), BF16)
    kron, firsts = [pltpu.VMEM((SECOND, LANES), BF16)], [pltpu.VMEM((CHI * ROWS, LANES), BF16)]
    scales, means = [], []
    own = site_tensors[0, 0]
    for level in range(LEVELS):
        if level == 0:
            other = from_partner(own, 1)
            (own,) = call(spread_kernel, [mat])(own)
            own, other, gram = call(first_gram_kernel, [mat, mat, sent])(own, other)
        else:
            other = from_partner(own, 1 << level | 1)
            own, product, mean = call(own_kernel, [mat, mat, one])(own)
            gram, scale = call(functools.partial(gram_kernel, level), [sent, one])(
                product, mean, other
            )
            scales, means = [scale], [*means, mean]
        gram_other = from_bond(gram)
        turned, lower, starts, pieces, wide, image, trace = call(
            functools.partial(turn_kernel, level),
            [
                mat,
                mat,
                ((2 * PAD, LANES), F32),
                ((16 * PAD, LANES), BF16),
                mat,
                ((PAD, LANES), F32),
                one,
            ],
        )(own, other, gram, start_basis)
        (left,) = call(iso_kernel, [((PAD, LANES), BF16)])(
            wide, image, trace, gram_other, starts, pieces
        )
        right = from_partner(left, 1)
        (second,) = call(second_kernel, [((ROWS, SECOND), BF16)], firsts)(turned, lower, left)
        if level < LEVELS - 1:
            (own,) = call(third_kernel, [sent], kron)(second, right, *scales)
        else:
            coarse, log_total = call(last_kernel, [((square, square), F32), ((1, 1), F32)], kron)(
                second, right, *scales, *means
            )
    return (coarse[None, None], log_total)


def solution(mesh):
    return jax.shard_map(
        per_device,
        mesh=mesh,
        in_specs=(P("row", "col", None, None), P()),
        out_specs=(P("row", "col", None, None), P("row", "col")),
        check_vma=False,
    )
```
